512 devices in a mesh: dp: 32 (over y_lo, z), tensor: 16 (over y_hi, x, core).
Axes of the slice: x: 4, y: 4 (y_hi: 2, y_lo: 2; y = y_hi * 2 + y_lo), z: 16, core: 2. Of those that a mesh axis runs over, the one named last changes fastest.
Arguments:
- inputs: bfloat16 [4096, 8192], P('dp', 'tensor'), may hold values from -6 to 6
- grad_context: bfloat16 [4096, 8192], P('dp', 'tensor'), may hold values from -24 to 24
- gain: float32 [8192], replicated, may hold values from 0.1 to 1.9
- w_query: bfloat16 [8192, 8192], P('dp', 'tensor'), may hold values from -0.0625 to 0.0625
- w_keyval: bfloat16 [8192, 1024], P('dp', 'tensor'), may hold values from -0.0625 to 0.0625
Outputs:
- grad_input: bfloat16 [4096, 8192], P('dp', 'tensor')
- grad_gain: float32 [8192], P('tensor')
- grad_w_keyval: bfloat16 [8192, 1024], P('dp', 'tensor')
The draws below stay inside these ranges and needn't reach their ends.
All inputs are finite; a program needn't handle non-finite values.
Results may differ from the reference program's by a relative error of at most 0.023.
Values may be sent and summed in bfloat16 or wider, within the bound.
A program may use at most 64 MiB of HBM per device.

```python
import math
import jax
import jax.numpy as jnp
from jax import lax

D = 8192
HD = 128
KV_HEADS = 4
HEADS_DEV = 4
SEQ = 128
HEADS = 64
TOKENS = 4096
N_DP = 32
N_TENSOR = 16


def spiked(drawn, key, source, target, blocks, factor):
    owner, partner = [(jnp.arange(drawn.shape[dim]) // (drawn.shape[dim] // blocks)).reshape([-1 if axis == dim else 1 for axis in range(drawn.ndim)]) for dim in (source, target)]
    chosen = jax.random.permutation(key, blocks)[partner]
    strong = (owner == chosen) | (owner == (partner + blocks // 2) % blocks)
    return jnp.where(strong, factor * drawn, drawn)


def steps_of(own_key, dims, shards, smallest, high):
    factor_of = 1.0
    for dim, shards_of in shards:
        draws = jax.random.uniform(jax.random.fold_in(jax.random.fold_in(own_key, 6), dim), (shards_of,), jnp.float32, smallest / len(shards), high / len(shards))
        factor_of = factor_of * jnp.repeat(jnp.exp(draws), dims[dim] // shards_of).reshape((-1,) + (1,) * (len(dims) - 1 - dim))
    return factor_of


def scatter_about(rng, dims, scale, limit, shards=(), dtype=jnp.bfloat16):
    values = jax.random.normal(rng, dims, jnp.float32) * scale
    if len(shards) > 0:
        values = steps_of(rng, dims, shards, -0.22, 0.18) * values
    return jnp.clip(values, min=-limit, max=limit).astype(dtype)


def gaussian_with(key, dims, spread, bound, cuts, heavy, held_as=jnp.bfloat16):
    array = spread * jax.random.normal(key, dims, jnp.float32)
    if cuts:
        array = array * steps_of(key, dims, cuts, -0.22, 0.18)
    return jnp.clip(spiked(array, jax.random.fold_in(key, 3), *heavy), -bound, bound).astype(held_as)


def setup_inputs(seed: int = 0) -> dict:
    arg_keys = jax.random.split(jax.random.key(seed), 6)
    return {
        "inputs": scatter_about(arg_keys[0], (TOKENS, D), 1.0, 6.0, ((0, 32), (1, 16))),
        "grad_context": gaussian_with(arg_keys[1], (TOKENS, HEADS * HD), 4.0, 24.0, ((0, 32), (1, 16)), (0, 1, 32, 2.75)),
        "gain": jnp.clip(1.0 + 0.18 * jax.random.normal(arg_keys[2], (D,), jnp.float32), 0.1, 1.9),
        "w_query": scatter_about(arg_keys[3], (D, HEADS * HD), D ** -0.5, 0.0625, ((0, 32), (1, 16))),
        "w_keyval": scatter_about(arg_keys[4], (D, 2 * KV_HEADS * HD), D ** -0.5, 0.0625, ((0, 32), (1, 16))),
    }


def rope_tables(length):
    positions = jnp.arange(length).astype(jnp.float32)[:, None]
    index_half = jnp.arange(HD // 2).astype(jnp.float32)[None, :]
    frequency = jnp.exp(-(2.0 * index_half / HD) * math.log(500000.0))
    angles = positions * frequency
    return (jnp.cos(angles), jnp.sin(angles))

def rotate(vectors, cosine_table, sine_table):
    half_size = vectors.shape[-1] // 2
    first_half = vectors[..., :half_size]
    second_half = vectors[..., half_size:]
    return jnp.concatenate([first_half * cosine_table - second_half * sine_table, first_half * sine_table + second_half * cosine_table], axis=-1)

def unrotate(vectors, cosine_table, sine_table):
    half_size = vectors.shape[-1] // 2
    first_half = vectors[..., :half_size]
    second_half = vectors[..., half_size:]
    return jnp.concatenate([first_half * cosine_table + second_half * sine_table, second_half * cosine_table - first_half * sine_table], axis=-1)

def add_group(running, pieces):
    query_part, weight_part, keyval_part, keyweight_part = pieces
    contract_last = (((1,), (1,)), ((), ()))
    term_sum = lax.dot_general(query_part, weight_part, contract_last, preferred_element_type=jnp.float32)
    term_sum = term_sum + lax.dot_general(keyval_part, keyweight_part, contract_last, preferred_element_type=jnp.float32)
    rounded = lax.optimization_barrier(term_sum.astype(jnp.bfloat16))
    return (running + rounded.astype(jnp.float32), None)

def reference(inputs, grad_context, gain, w_query, w_keyval):
    group_size = HEADS // KV_HEADS
    group_cols = 2 * KV_HEADS * HD // N_TENSOR
    device_cols = HEADS_DEV * HD
    score_scale = HD ** (-0.5)
    row_total = N_DP * SEQ
    as_float = inputs.astype(jnp.float32)
    inv_rms = lax.rsqrt(lax.optimization_barrier(jnp.mean(as_float * as_float, axis=1, keepdims=True)) + 1e-05)
    unit_rows = as_float * inv_rms
    normed = (unit_rows * gain).astype(jnp.bfloat16)
    query_proj = jnp.dot(normed, w_query, preferred_element_type=jnp.float32).astype(jnp.bfloat16)
    keyval_proj = jnp.dot(normed, w_keyval, preferred_element_type=jnp.float32).astype(jnp.bfloat16)
    cosine_table, sine_table = rope_tables(SEQ)
    query_grid = query_proj.astype(jnp.float32).reshape(N_DP, SEQ, KV_HEADS, group_size, HD).transpose(0, 2, 3, 1, 4)
    q_rot = rotate(query_grid, cosine_table, sine_table).astype(jnp.bfloat16)
    keyval_grid = keyval_proj.astype(jnp.float32).reshape(N_DP, SEQ, 2, KV_HEADS, HD).transpose(2, 0, 3, 1, 4)
    k_rot = rotate(keyval_grid[0], cosine_table, sine_table).astype(jnp.bfloat16)
    value_grid = keyval_grid[1]
    scores = jnp.einsum('rkgsd,rktd->rkgst', q_rot.astype(jnp.float32), k_rot.astype(jnp.float32)) * score_scale
    causal = jnp.arange(SEQ)[:, None] >= jnp.arange(SEQ)[None, :]
    exponent = jnp.where(causal, jnp.exp(scores), 0.0)
    softmax_probs = exponent / lax.optimization_barrier(jnp.sum(exponent, axis=-1, keepdims=True))
    prob_weights = softmax_probs.astype(jnp.bfloat16)
    context = jnp.einsum('rkgst,rktd->rkgsd', prob_weights.astype(jnp.float32), value_grid).astype(jnp.bfloat16)
    grad_ctx_f = grad_context.astype(jnp.float32).reshape(N_DP, SEQ, KV_HEADS, group_size, HD).transpose(0, 2, 3, 1, 4)
    grad_probs = jnp.einsum('rkgsd,rktd->rkgst', grad_ctx_f, value_grid)
    row_delta = lax.optimization_barrier(jnp.sum(grad_ctx_f * context.astype(jnp.float32), axis=-1, keepdims=True))
    grad_scores = (softmax_probs * (grad_probs - row_delta) * score_scale).astype(jnp.bfloat16)
    grad_scores_f = grad_scores.astype(jnp.float32)
    grad_qrot = jnp.einsum('rkgst,rktd->rkgsd', grad_scores_f, k_rot.astype(jnp.float32))
    grad_krot = jnp.einsum('rkgst,rkgsd->rktd', grad_scores_f, q_rot.astype(jnp.float32))
    grad_value = jnp.einsum('rkgst,rkgsd->rktd', prob_weights.astype(jnp.float32), grad_ctx_f)
    grad_query = unrotate(grad_qrot, cosine_table, sine_table).astype(jnp.bfloat16)
    grad_query = grad_query.transpose(0, 3, 1, 2, 4).reshape(row_total, HEADS * HD)
    grad_keyval = jnp.stack([unrotate(grad_krot, cosine_table, sine_table), grad_value])
    grad_keyval = grad_keyval.transpose(1, 3, 0, 2, 4).reshape(row_total, 2 * KV_HEADS * HD).astype(jnp.bfloat16)
    query_stack = grad_query.reshape(row_total, N_TENSOR, device_cols).transpose(1, 0, 2)
    weight_stack = w_query.reshape(D, N_TENSOR, device_cols).transpose(1, 0, 2)
    keyval_stack = grad_keyval.reshape(row_total, N_TENSOR, group_cols).transpose(1, 0, 2)
    keyweight_stack = w_keyval.reshape(D, N_TENSOR, group_cols).transpose(1, 0, 2)
    grad_normed, _ = lax.scan(add_group, jnp.zeros((row_total, D), jnp.float32), (query_stack, weight_stack, keyval_stack, keyweight_stack))
    scaled_grad = grad_normed * gain
    grad_input = (inv_rms * (scaled_grad - unit_rows * lax.optimization_barrier(jnp.mean(scaled_grad * unit_rows, axis=1, keepdims=True)))).astype(jnp.bfloat16)
    grad_gain = lax.optimization_barrier(jnp.sum(grad_normed * unit_rows, axis=0))
    grad_w_keyval = jnp.dot(normed.T, grad_keyval, preferred_element_type=jnp.float32).astype(jnp.bfloat16)
    return (grad_input, grad_gain, grad_w_keyval)
```

```python
import math

import jax
import jax.numpy as jnp
from jax import lax
from jax.sharding import PartitionSpec as P

HD = 128
KV_HEADS = 4
HEADS_DEV = 4


def rope_tables(length, head_size):
    positions = lax.broadcasted_iota(jnp.int32, (length, head_size // 2), 0).astype(jnp.float32)
    index_half = lax.broadcasted_iota(jnp.int32, (length, head_size // 2), 1).astype(jnp.float32)
    frequency = jnp.exp(-(2.0 * index_half / head_size) * math.log(500000.0))
    angles = positions * frequency
    return (jnp.cos(angles), jnp.sin(angles))


def rotate(vectors, cosine_table, sine_table):
    half_size = vectors.shape[-1] // 2
    first_half = vectors[..., :half_size]
    second_half = vectors[..., half_size:]
    return jnp.concatenate(
        [
            first_half * cosine_table - second_half * sine_table,
            first_half * sine_table + second_half * cosine_table,
        ],
        axis=-1,
    )


def unrotate(vectors, cosine_table, sine_table):
    half_size = vectors.shape[-1] // 2
    first_half = vectors[..., :half_size]
    second_half = vectors[..., half_size:]
    return jnp.concatenate(
        [
            first_half * cosine_table + second_half * sine_table,
            second_half * cosine_table - first_half * sine_table,
        ],
        axis=-1,
    )


def on_device(inputs, grad_context, gain, w_query, w_keyval):
    contract_last = (((1,), (1,)), ((), ()))
    contract_first = (((0,), (0,)), ((), ()))
    seq_length = inputs.shape[0]
    local_cols = inputs.shape[1]
    model_width = gain.shape[0]
    head_size = HD
    heads_here = HEADS_DEV
    group_cols = w_keyval.shape[1]
    tensor_count = lax.axis_size("tensor")
    keyval_total = group_cols * tensor_count
    kv_heads = KV_HEADS
    devices_per_group = tensor_count // kv_heads
    score_scale = head_size ** (-0.5)
    tensor_slot = lax.axis_index("tensor")
    gain_local = lax.dynamic_slice_in_dim(gain, tensor_slot * local_cols, local_cols, 0)
    weight_block = jnp.concatenate([w_query, w_keyval], axis=1)
    weight_full = lax.all_gather(weight_block, "dp", axis=0, tiled=True)
    query_weight = weight_full[:, : w_query.shape[1]]
    keyweight = weight_full[:, w_query.shape[1] :]
    inputs_full = lax.all_gather(inputs, "tensor", axis=1, tiled=True).astype(jnp.float32)
    row_sum = jnp.sum(inputs_full * inputs_full, axis=1, keepdims=True)
    inv_rms = lax.rsqrt(row_sum / model_width + 1e-05)
    unit_full = inputs_full * inv_rms
    normed_full = (unit_full * gain[None, :]).astype(jnp.bfloat16)
    unit_rows = inputs.astype(jnp.float32) * inv_rms
    query_proj = jnp.dot(normed_full, query_weight, preferred_element_type=jnp.float32).astype(
        jnp.bfloat16
    )
    keyval_part = jnp.dot(normed_full, keyweight, preferred_element_type=jnp.float32).astype(
        jnp.bfloat16
    )
    keyval_full = lax.all_gather(keyval_part, "tensor", axis=1, tiled=True)
    group_slot = tensor_slot // devices_per_group
    key_block = lax.dynamic_slice_in_dim(keyval_full, group_slot * head_size, head_size, 1)
    value_block = lax.dynamic_slice_in_dim(
        keyval_full, (kv_heads + group_slot) * head_size, head_size, 1
    )
    cosine_table, sine_table = rope_tables(seq_length, head_size)
    cos_heads = cosine_table[:, None, :]
    sin_heads = sine_table[:, None, :]
    query_heads = query_proj.astype(jnp.float32).reshape(seq_length, heads_here, head_size)
    q_rot = rotate(query_heads, cos_heads, sin_heads).astype(jnp.bfloat16)
    k_rot = rotate(key_block.astype(jnp.float32), cosine_table, sine_table).astype(jnp.bfloat16)
    scores = (
        jnp.einsum("shd,td->hst", q_rot, k_rot, preferred_element_type=jnp.float32) * score_scale
    )
    causal = lax.broadcasted_iota(jnp.int32, (seq_length, seq_length), 0) >= lax.broadcasted_iota(
        jnp.int32, (seq_length, seq_length), 1
    )
    exponent = jnp.where(causal[None, :, :], jnp.exp(scores), 0.0)
    softmax_probs = exponent / jnp.sum(exponent, axis=2, keepdims=True)
    prob_weights = softmax_probs.astype(jnp.bfloat16)
    context = jnp.einsum(
        "hst,td->shd", prob_weights, value_block, preferred_element_type=jnp.float32
    ).astype(jnp.bfloat16)
    grad_ctx = grad_context.reshape(seq_length, heads_here, head_size)
    grad_probs = jnp.einsum(
        "shd,td->hst", grad_ctx, value_block, preferred_element_type=jnp.float32
    )
    row_delta = jnp.sum(grad_ctx.astype(jnp.float32) * context.astype(jnp.float32), axis=2).T[
        :, :, None
    ]
    grad_scores = (softmax_probs * (grad_probs - row_delta) * score_scale).astype(jnp.bfloat16)
    grad_qrot = jnp.einsum("hst,td->shd", grad_scores, k_rot, preferred_element_type=jnp.float32)
    grad_krot = jnp.einsum("hst,shd->td", grad_scores, q_rot, preferred_element_type=jnp.float32)
    grad_value = jnp.einsum(
        "hst,shd->td", prob_weights, grad_ctx, preferred_element_type=jnp.float32
    )
    grad_query = (
        unrotate(grad_qrot, cos_heads, sin_heads)
        .astype(jnp.bfloat16)
        .reshape(seq_length, heads_here * head_size)
    )
    grad_terms = jnp.zeros((seq_length, keyval_total), jnp.float32)
    grad_terms = lax.dynamic_update_slice_in_dim(
        grad_terms, unrotate(grad_krot, cosine_table, sine_table), group_slot * head_size, 1
    )
    grad_terms = lax.dynamic_update_slice_in_dim(
        grad_terms, grad_value, (kv_heads + group_slot) * head_size, 1
    )
    grad_keyval = lax.psum_scatter(
        grad_terms.astype(jnp.bfloat16), "tensor", scatter_dimension=1, tiled=True
    )
    result = lax.dot_general(
        query_weight, grad_query, contract_last, preferred_element_type=jnp.float32
    )
    grad_normed = (
        lax.psum_scatter(
            (
                result
                + lax.dot_general(
                    keyweight, grad_keyval, contract_last, preferred_element_type=jnp.float32
                )
            ).astype(jnp.bfloat16),
            "tensor",
            scatter_dimension=0,
            tiled=True,
        )
        .astype(jnp.float32)
        .T
    )
    scaled_grad = grad_normed * gain_local
    product_sum = lax.psum(jnp.sum(scaled_grad * unit_rows, axis=1, keepdims=True), "tensor")
    grad_input = (inv_rms * (scaled_grad - unit_rows * (product_sum / model_width))).astype(
        jnp.bfloat16
    )
    grad_gain = lax.psum(jnp.sum(grad_normed * unit_rows, axis=0), "dp")
    keyval_all = lax.all_gather(grad_keyval, "dp", axis=0, tiled=True)
    rows_normed = lax.all_to_all(normed_full, "dp", split_axis=1, concat_axis=0, tiled=True)
    keyval_weight_grad = lax.dot_general(
        rows_normed, keyval_all, contract_first, preferred_element_type=jnp.float32
    )
    return (grad_input, grad_gain, keyval_weight_grad.astype(jnp.bfloat16))


def solution(mesh):
    in_specs = (P("dp", "tensor"), P("dp", "tensor"), P(), P("dp", "tensor"), P("dp", "tensor"))
    out_specs = (P("dp", "tensor"), P("tensor"), P("dp", "tensor"))
    return jax.shard_map(
        on_device, mesh=mesh, in_specs=in_specs, out_specs=out_specs, check_vma=False
    )
```

```python
import functools
import math

import jax
import jax.numpy as jnp
from jax import lax
from jax.experimental import pallas as pl
from jax.experimental.pallas import tpu as pltpu
from jax.sharding import PartitionSpec as P

MESH = pl.DeviceIdType.MESH


def exchange_kernel(axis, n, per_peer, *refs):
    count = len(per_peer)
    src_refs = refs[:count]
    out_refs = refs[count : 2 * count]
    send_sems, recv_sems = refs[2 * count :]
    me = lax.axis_index(axis)
    barrier = pltpu.get_barrier_semaphore()
    for step in range(1, n):
        peer = lax.rem(me + step, n)
        pl.semaphore_signal(barrier, inc=1, device_id={axis: peer}, device_id_type=MESH)
    pl.semaphore_wait(barrier, n - 1)
    copies = []
    for index in range(count):
        for step in range(1, n):
            peer = lax.rem(me + step, n)
            source = src_refs[index].at[peer] if per_peer[index] else src_refs[index]
            copy = pltpu.make_async_remote_copy(
                src_ref=source,
                dst_ref=out_refs[index].at[me],
                send_sem=send_sems.at[index, step],
                recv_sem=recv_sems.at[index, step],
                device_id={axis: peer},
                device_id_type=MESH,
            )
            copy.start()
            copies.append(copy)
    for index in range(count):
        own = src_refs[index][me] if per_peer[index] else src_refs[index][...]
        out_refs[index][me] = own
    for copy in copies:
        copy.wait_send()
    for copy in copies:
        copy.wait_recv()


def exchange(axis, blocks, per_peer, collective_id):
    n = lax.axis_size(axis)
    out_shapes = []
    for block, spread in zip(blocks, per_peer):
        shape = block.shape[1:] if spread else block.shape
        out_shapes.append(jax.ShapeDtypeStruct((n,) + tuple(shape), block.dtype))
    count = len(blocks)
    sent = sum(b.size * b.dtype.itemsize * (1 if s else n) for b, s in zip(blocks, per_peer))
    return pl.pallas_call(
        functools.partial(exchange_kernel, axis, n, tuple(per_peer)),
        out_shape=tuple(out_shapes),
        in_specs=[pl.BlockSpec(memory_space=pltpu.VMEM)] * count,
        out_specs=tuple(pl.BlockSpec(memory_space=pltpu.VMEM) for _ in range(count)),
        scratch_shapes=[
            pltpu.SemaphoreType.DMA((count, n)),
            pltpu.SemaphoreType.DMA((count, n)),
        ],
        compiler_params=pltpu.CompilerParams(collective_id=collective_id, has_side_effects=True),
        cost_estimate=pl.CostEstimate(flops=0, bytes_accessed=2 * sent, transcendentals=0),
    )(*blocks)


HD = 128
KV_HEADS = 4
HEADS_DEV = 4


def rope_tables(length, head_size):
    positions = lax.broadcasted_iota(jnp.int32, (length, head_size // 2), 0).astype(jnp.float32)
    index_half = lax.broadcasted_iota(jnp.int32, (length, head_size // 2), 1).astype(jnp.float32)
    frequency = jnp.exp(-(2.0 * index_half / head_size) * math.log(500000.0))
    angles = positions * frequency
    return (jnp.cos(angles), jnp.sin(angles))


def rotate(vectors, cosine_table, sine_table):
    half_size = vectors.shape[-1] // 2
    first_half = vectors[..., :half_size]
    second_half = vectors[..., half_size:]
    return jnp.concatenate(
        [
            first_half * cosine_table - second_half * sine_table,
            first_half * sine_table + second_half * cosine_table,
        ],
        axis=-1,
    )


def unrotate(vectors, cosine_table, sine_table):
    half_size = vectors.shape[-1] // 2
    first_half = vectors[..., :half_size]
    second_half = vectors[..., half_size:]
    return jnp.concatenate(
        [
            first_half * cosine_table + second_half * sine_table,
            second_half * cosine_table - first_half * sine_table,
        ],
        axis=-1,
    )


def on_device(inputs, grad_context, gain, w_query, w_keyval):
    seq_length = inputs.shape[0]
    local_cols = inputs.shape[1]
    model_width = gain.shape[0]
    head_size = HD
    heads_here = HEADS_DEV
    group_cols = w_keyval.shape[1]
    query_cols = w_query.shape[1]
    tensor_count = lax.axis_size("tensor")
    keyval_total = group_cols * tensor_count
    kv_heads = KV_HEADS
    devices_per_group = tensor_count // kv_heads
    score_scale = head_size ** (-0.5)
    tensor_slot = lax.axis_index("tensor")
    gain_local = lax.dynamic_slice_in_dim(gain, tensor_slot * local_cols, local_cols, 0)
    weight_block = jnp.concatenate([w_query, w_keyval], axis=1)
    weight_full = lax.all_gather(weight_block, "dp", axis=0, tiled=True)
    query_weight = weight_full[:, :query_cols]
    keyweight = weight_full[:, query_cols:]
    (input_blocks,) = exchange("tensor", [inputs], [False], 0)
    inputs_full = (
        input_blocks.transpose(1, 0, 2).reshape(seq_length, model_width).astype(jnp.float32)
    )
    row_sum = jnp.sum(inputs_full * inputs_full, axis=1, keepdims=True)
    inv_rms = lax.rsqrt(row_sum / model_width + 1e-05)
    unit_full = inputs_full * inv_rms
    normed_full = (unit_full * gain[None, :]).astype(jnp.bfloat16)
    unit_rows = inputs.astype(jnp.float32) * inv_rms
    query_proj = jnp.dot(normed_full, query_weight, preferred_element_type=jnp.float32).astype(
        jnp.bfloat16
    )
    keyval_part = jnp.dot(normed_full, keyweight, preferred_element_type=jnp.float32).astype(
        jnp.bfloat16
    )
    (keyval_blocks,) = exchange("tensor", [keyval_part], [False], 1)
    keyval_full = keyval_blocks.transpose(1, 0, 2).reshape(seq_length, keyval_total)
    group_slot = tensor_slot // devices_per_group
    key_block = lax.dynamic_slice_in_dim(keyval_full, group_slot * head_size, head_size, 1)
    value_block = lax.dynamic_slice_in_dim(
        keyval_full, (kv_heads + group_slot) * head_size, head_size, 1
    )
    cosine_table, sine_table = rope_tables(seq_length, head_size)
    cos_heads = cosine_table[:, None, :]
    sin_heads = sine_table[:, None, :]
    query_heads = query_proj.astype(jnp.float32).reshape(seq_length, heads_here, head_size)
    q_rot = rotate(query_heads, cos_heads, sin_heads).astype(jnp.bfloat16)
    k_rot = rotate(key_block.astype(jnp.float32), cosine_table, sine_table).astype(jnp.bfloat16)
    scores = (
        jnp.einsum("shd,td->hst", q_rot, k_rot, preferred_element_type=jnp.float32) * score_scale
    )
    causal = lax.broadcasted_iota(jnp.int32, (seq_length, seq_length), 0) >= lax.broadcasted_iota(
        jnp.int32, (seq_length, seq_length), 1
    )
    exponent = jnp.where(causal[None, :, :], jnp.exp(scores), 0.0)
    softmax_probs = exponent / jnp.sum(exponent, axis=2, keepdims=True)
    prob_weights = softmax_probs.astype(jnp.bfloat16)
    context = jnp.einsum(
        "hst,td->shd", prob_weights, value_block, preferred_element_type=jnp.float32
    ).astype(jnp.bfloat16)
    grad_ctx = grad_context.reshape(seq_length, heads_here, head_size)
    grad_probs = jnp.einsum(
        "shd,td->hst", grad_ctx, value_block, preferred_element_type=jnp.float32
    )
    row_delta = jnp.sum(grad_ctx.astype(jnp.float32) * context.astype(jnp.float32), axis=2).T[
        :, :, None
    ]
    grad_scores = (softmax_probs * (grad_probs - row_delta) * score_scale).astype(jnp.bfloat16)
    grad_qrot = jnp.einsum("hst,td->shd", grad_scores, k_rot, preferred_element_type=jnp.float32)
    grad_krot = jnp.einsum("hst,shd->td", grad_scores, q_rot, preferred_element_type=jnp.float32)
    grad_value = jnp.einsum(
        "hst,shd->td", prob_weights, grad_ctx, preferred_element_type=jnp.float32
    )
    grad_query = (
        unrotate(grad_qrot, cos_heads, sin_heads)
        .astype(jnp.bfloat16)
        .reshape(seq_length, heads_here * head_size)
    )
    grad_terms = jnp.zeros((seq_length, keyval_total), jnp.float32)
    grad_terms = lax.dynamic_update_slice_in_dim(
        grad_terms, unrotate(grad_krot, cosine_table, sine_table), group_slot * head_size, 1
    )
    grad_terms = lax.dynamic_update_slice_in_dim(
        grad_terms, grad_value, (kv_heads + group_slot) * head_size, 1
    )
    term_blocks = grad_terms.reshape(seq_length, tensor_count, group_cols).transpose(1, 0, 2)
    (keyval_terms,) = exchange("tensor", [term_blocks], [True], 2)
    grad_keyval = jnp.sum(keyval_terms, axis=0).astype(jnp.bfloat16)
    query_weight_blocks = query_weight.reshape(tensor_count, local_cols, query_cols)
    keyweight_blocks = keyweight.reshape(tensor_count, local_cols, group_cols)
    normed_terms = (
        jnp.einsum("rc,pkc->prk", grad_query, query_weight_blocks, preferred_element_type=jnp.float32)
        + jnp.einsum(
            "rc,pkc->prk", grad_keyval, keyweight_blocks, preferred_element_type=jnp.float32
        )
    ).astype(jnp.bfloat16)
    unit_blocks = unit_full.reshape(seq_length, tensor_count, local_cols).transpose(1, 0, 2)
    gain_blocks = gain.reshape(tensor_count, 1, local_cols)
    product_part = jnp.sum(
        normed_terms.astype(jnp.float32) * gain_blocks * unit_blocks, axis=(0, 2)
    ).reshape(1, seq_length)
    normed_sums, product_parts = exchange(
        "tensor", [normed_terms, product_part], [True, False], 3
    )
    grad_normed = jnp.sum(normed_sums.astype(jnp.float32), axis=0)
    product_sum = jnp.sum(product_parts, axis=0).reshape(seq_length, 1)
    scaled_grad = grad_normed * gain_local
    grad_input = (inv_rms * (scaled_grad - unit_rows * (product_sum / model_width))).astype(
        jnp.bfloat16
    )
    gain_part = jnp.sum(grad_normed * unit_rows, axis=0).reshape(1, local_cols)
    (gain_parts,) = exchange("dp", [gain_part], [False], 4)
    grad_gain = jnp.sum(gain_parts, axis=(0, 1))
    (keyval_rows,) = exchange("dp", [grad_keyval], [False], 5)
    keyval_all = keyval_rows.reshape(-1, group_cols)
    rows_normed = lax.all_to_all(normed_full, "dp", split_axis=1, concat_axis=0, tiled=True)
    keyval_weight_grad = lax.dot_general(
        rows_normed, keyval_all, (((0,), (0,)), ((), ())), preferred_element_type=jnp.float32
    )
    return (grad_input, grad_gain, keyval_weight_grad.astype(jnp.bfloat16))


def solution(mesh):
    in_specs = (P("dp", "tensor"), P("dp", "tensor"), P(), P("dp", "tensor"), P("dp", "tensor"))
    out_specs = (P("dp", "tensor"), P("tensor"), P("dp", "tensor"))
    return jax.shard_map(
        on_device, mesh=mesh, in_specs=in_specs, out_specs=out_specs, check_vma=False
    )
```

```python
import functools
import math

import jax
import jax.numpy as jnp
from jax import lax
from jax.experimental import pallas as pl
from jax.experimental.pallas import tpu as pltpu
from jax.sharding import PartitionSpec as P

MESH = pl.DeviceIdType.MESH


def exchange_kernel(axis, n, per_peer, *refs):
    count = len(per_peer)
    src_refs = refs[:count]
    out_refs = refs[count : 2 * count]
    send_sems, recv_sems = refs[2 * count :]
    me = lax.axis_index(axis)
    barrier = pltpu.get_barrier_semaphore()
    for step in range(1, n):
        peer = lax.rem(me + step, n)
        pl.semaphore_signal(barrier, inc=1, device_id={axis: peer}, device_id_type=MESH)
    pl.semaphore_wait(barrier, n - 1)
    copies = []
    for index in range(count):
        for step in range(1, n):
            peer = lax.rem(me + step, n)
            source = src_refs[index].at[peer] if per_peer[index] else src_refs[index]
            copy = pltpu.make_async_remote_copy(
                src_ref=source,
                dst_ref=out_refs[index].at[me],
                send_sem=send_sems.at[index, step],
                recv_sem=recv_sems.at[index, step],
                device_id={axis: peer},
                device_id_type=MESH,
            )
            copy.start()
            copies.append(copy)
    for index in range(count):
        own = src_refs[index][me] if per_peer[index] else src_refs[index][...]
        out_refs[index][me] = own
    for copy in copies:
        copy.wait_send()
    for copy in copies:
        copy.wait_recv()


def exchange(axis, blocks, per_peer, collective_id):
    n = lax.axis_size(axis)
    out_shapes = []
    for block, spread in zip(blocks, per_peer):
        shape = block.shape[1:] if spread else block.shape
        out_shapes.append(jax.ShapeDtypeStruct((n,) + tuple(shape), block.dtype))
    count = len(blocks)
    sent = sum(b.size * b.dtype.itemsize * (1 if s else n) for b, s in zip(blocks, per_peer))
    return pl.pallas_call(
        functools.partial(exchange_kernel, axis, n, tuple(per_peer)),
        out_shape=tuple(out_shapes),
        in_specs=[pl.BlockSpec(memory_space=pltpu.VMEM)] * count,
        out_specs=tuple(pl.BlockSpec(memory_space=pltpu.VMEM) for _ in range(count)),
        scratch_shapes=[
            pltpu.SemaphoreType.DMA((count, n)),
            pltpu.SemaphoreType.DMA((count, n)),
        ],
        compiler_params=pltpu.CompilerParams(collective_id=collective_id, has_side_effects=True),
        cost_estimate=pl.CostEstimate(flops=0, bytes_accessed=2 * sent, transcendentals=0),
    )(*blocks)


def ring_gather_kernel(pair_count, ring_count, block_ref, out_ref, send_sems, recv_sems):
    pair_slot = lax.axis_index("dp") // ring_count
    ring_slot = lax.axis_index("dp") % ring_count
    partner = (1 - pair_slot) * ring_count + ring_slot
    right = pair_slot * ring_count + lax.rem(ring_slot + 1, ring_count)
    left = pair_slot * ring_count + lax.rem(ring_slot + ring_count - 1, ring_count)
    me = pair_slot * ring_count + ring_slot
    barrier = pltpu.get_barrier_semaphore()
    for peer in (partner, right, left):
        pl.semaphore_signal(barrier, inc=1, device_id={"dp": peer}, device_id_type=MESH)
    pl.semaphore_wait(barrier, 3)
    swap = pltpu.make_async_remote_copy(
        src_ref=block_ref,
        dst_ref=out_ref.at[me],
        send_sem=send_sems.at[2, 0, 0],
        recv_sem=recv_sems.at[2, 0, 0],
        device_id={"dp": partner},
        device_id_type=MESH,
    )
    swap.start()
    own = pltpu.make_async_copy(block_ref, out_ref.at[me], send_sems.at[2, 1, 0])
    own.start()
    own.wait()
    swap.wait_send()
    swap.wait_recv()
    right_steps = ring_count // 2
    left_steps = ring_count - 1 - right_steps
    sent = []

    def send(direction, step, target, origin):
        copies = []
        for member in range(pair_count):
            slot = member * ring_count + origin
            copy = pltpu.make_async_remote_copy(
                src_ref=out_ref.at[slot],
                dst_ref=out_ref.at[slot],
                send_sem=send_sems.at[direction, step, member],
                recv_sem=recv_sems.at[direction, step, member],
                device_id={"dp": target},
                device_id_type=MESH,
            )
            copy.start()
            copies.append(copy)
        sent.extend(copies)
        return copies

    right_copies = send(0, 0, right, ring_slot)
    left_copies = send(1, 0, left, ring_slot) if left_steps > 0 else []
    for step in range(1, right_steps):
        for copy in right_copies:
            copy.wait_recv()
        origin = lax.rem(ring_slot + ring_count - step, ring_count)
        right_copies = send(0, step, right, origin)
        if step < left_steps:
            for copy in left_copies:
                copy.wait_recv()
            origin = lax.rem(ring_slot + step, ring_count)
            left_copies = send(1, step, left, origin)
    for copy in right_copies + left_copies:
        copy.wait_recv()
    for copy in sent:
        copy.wait_send()


def ring_gather(block, collective_id):
    count = lax.axis_size("dp")
    pair_count = 2
    ring_count = count // pair_count
    return pl.pallas_call(
        functools.partial(ring_gather_kernel, pair_count, ring_count),
        out_shape=jax.ShapeDtypeStruct((count,) + block.shape, block.dtype),
        in_specs=[pl.BlockSpec(memory_space=pltpu.VMEM)],
        out_specs=pl.BlockSpec(memory_space=pltpu.VMEM),
        scratch_shapes=[
            pltpu.SemaphoreType.DMA((3, ring_count, pair_count)),
            pltpu.SemaphoreType.DMA((3, ring_count, pair_count)),
        ],
        compiler_params=pltpu.CompilerParams(
            collective_id=collective_id, has_side_effects=True, vmem_limit_bytes=48 * 1024 * 1024
        ),
        cost_estimate=pl.CostEstimate(
            flops=0, bytes_accessed=2 * count * block.size * block.dtype.itemsize, transcendentals=0
        ),
    )(block)


HD = 128
KV_HEADS = 4
HEADS_DEV = 4


def rope_tables(length, head_size):
    positions = lax.broadcasted_iota(jnp.int32, (length, head_size // 2), 0).astype(jnp.float32)
    index_half = lax.broadcasted_iota(jnp.int32, (length, head_size // 2), 1).astype(jnp.float32)
    frequency = jnp.exp(-(2.0 * index_half / head_size) * math.log(500000.0))
    angles = positions * frequency
    return (jnp.cos(angles), jnp.sin(angles))


def rotate(vectors, cosine_table, sine_table):
    half_size = vectors.shape[-1] // 2
    first_half = vectors[..., :half_size]
    second_half = vectors[..., half_size:]
    return jnp.concatenate(
        [
            first_half * cosine_table - second_half * sine_table,
            first_half * sine_table + second_half * cosine_table,
        ],
        axis=-1,
    )


def unrotate(vectors, cosine_table, sine_table):
    half_size = vectors.shape[-1] // 2
    first_half = vectors[..., :half_size]
    second_half = vectors[..., half_size:]
    return jnp.concatenate(
        [
            first_half * cosine_table + second_half * sine_table,
            second_half * cosine_table - first_half * sine_table,
        ],
        axis=-1,
    )


def on_device(inputs, grad_context, gain, w_query, w_keyval):
    seq_length = inputs.shape[0]
    local_cols = inputs.shape[1]
    model_width = gain.shape[0]
    head_size = HD
    heads_here = HEADS_DEV
    group_cols = w_keyval.shape[1]
    query_cols = w_query.shape[1]
    tensor_count = lax.axis_size("tensor")
    keyval_total = group_cols * tensor_count
    kv_heads = KV_HEADS
    devices_per_group = tensor_count // kv_heads
    score_scale = head_size ** (-0.5)
    tensor_slot = lax.axis_index("tensor")
    gain_local = lax.dynamic_slice_in_dim(gain, tensor_slot * local_cols, local_cols, 0)
    weight_block = jnp.concatenate([w_query, w_keyval], axis=1)
    weight_full = ring_gather(weight_block, 6).reshape(-1, weight_block.shape[1])
    query_weight = weight_full[:, :query_cols]
    keyweight = weight_full[:, query_cols:]
    (input_blocks,) = exchange("tensor", [inputs], [False], 0)
    inputs_full = (
        input_blocks.transpose(1, 0, 2).reshape(seq_length, model_width).astype(jnp.float32)
    )
    row_sum = jnp.sum(inputs_full * inputs_full, axis=1, keepdims=True)
    inv_rms = lax.rsqrt(row_sum / model_width + 1e-05)
    unit_full = inputs_full * inv_rms
    normed_full = (unit_full * gain[None, :]).astype(jnp.bfloat16)
    unit_rows = inputs.astype(jnp.float32) * inv_rms
    query_proj = jnp.dot(normed_full, query_weight, preferred_element_type=jnp.float32).astype(
        jnp.bfloat16
    )
    keyval_part = jnp.dot(normed_full, keyweight, preferred_element_type=jnp.float32).astype(
        jnp.bfloat16
    )
    (keyval_blocks,) = exchange("tensor", [keyval_part], [False], 1)
    keyval_full = keyval_blocks.transpose(1, 0, 2).reshape(seq_length, keyval_total)
    group_slot = tensor_slot // devices_per_group
    key_block = lax.dynamic_slice_in_dim(keyval_full, group_slot * head_size, head_size, 1)
    value_block = lax.dynamic_slice_in_dim(
        keyval_full, (kv_heads + group_slot) * head_size, head_size, 1
    )
    cosine_table, sine_table = rope_tables(seq_length, head_size)
    cos_heads = cosine_table[:, None, :]
    sin_heads = sine_table[:, None, :]
    query_heads = query_proj.astype(jnp.float32).reshape(seq_length, heads_here, head_size)
    q_rot = rotate(query_heads, cos_heads, sin_heads).astype(jnp.bfloat16)
    k_rot = rotate(key_block.astype(jnp.float32), cosine_table, sine_table).astype(jnp.bfloat16)
    scores = (
        jnp.einsum("shd,td->hst", q_rot, k_rot, preferred_element_type=jnp.float32) * score_scale
    )
    causal = lax.broadcasted_iota(jnp.int32, (seq_length, seq_length), 0) >= lax.broadcasted_iota(
        jnp.int32, (seq_length, seq_length), 1
    )
    exponent = jnp.where(causal[None, :, :], jnp.exp(scores), 0.0)
    softmax_probs = exponent / jnp.sum(exponent, axis=2, keepdims=True)
    prob_weights = softmax_probs.astype(jnp.bfloat16)
    context = jnp.einsum(
        "hst,td->shd", prob_weights, value_block, preferred_element_type=jnp.float32
    ).astype(jnp.bfloat16)
    grad_ctx = grad_context.reshape(seq_length, heads_here, head_size)
    grad_probs = jnp.einsum(
        "shd,td->hst", grad_ctx, value_block, preferred_element_type=jnp.float32
    )
    row_delta = jnp.sum(grad_ctx.astype(jnp.float32) * context.astype(jnp.float32), axis=2).T[
        :, :, None
    ]
    grad_scores = (softmax_probs * (grad_probs - row_delta) * score_scale).astype(jnp.bfloat16)
    grad_qrot = jnp.einsum("hst,td->shd", grad_scores, k_rot, preferred_element_type=jnp.float32)
    grad_krot = jnp.einsum("hst,shd->td", grad_scores, q_rot, preferred_element_type=jnp.float32)
    grad_value = jnp.einsum(
        "hst,shd->td", prob_weights, grad_ctx, preferred_element_type=jnp.float32
    )
    grad_query = (
        unrotate(grad_qrot, cos_heads, sin_heads)
        .astype(jnp.bfloat16)
        .reshape(seq_length, heads_here * head_size)
    )
    grad_terms = jnp.zeros((seq_length, keyval_total), jnp.float32)
    grad_terms = lax.dynamic_update_slice_in_dim(
        grad_terms, unrotate(grad_krot, cosine_table, sine_table), group_slot * head_size, 1
    )
    grad_terms = lax.dynamic_update_slice_in_dim(
        grad_terms, grad_value, (kv_heads + group_slot) * head_size, 1
    )
    term_blocks = grad_terms.reshape(seq_length, tensor_count, group_cols).transpose(1, 0, 2)
    (keyval_terms,) = exchange("tensor", [term_blocks], [True], 2)
    grad_keyval = jnp.sum(keyval_terms, axis=0).astype(jnp.bfloat16)
    query_weight_blocks = query_weight.reshape(tensor_count, local_cols, query_cols)
    keyweight_blocks = keyweight.reshape(tensor_count, local_cols, group_cols)
    normed_terms = (
        jnp.einsum("rc,pkc->prk", grad_query, query_weight_blocks, preferred_element_type=jnp.float32)
        + jnp.einsum(
            "rc,pkc->prk", grad_keyval, keyweight_blocks, preferred_element_type=jnp.float32
        )
    ).astype(jnp.bfloat16)
    unit_blocks = unit_full.reshape(seq_length, tensor_count, local_cols).transpose(1, 0, 2)
    gain_blocks = gain.reshape(tensor_count, 1, local_cols)
    product_part = jnp.sum(
        normed_terms.astype(jnp.float32) * gain_blocks * unit_blocks, axis=(0, 2)
    ).reshape(1, seq_length)
    normed_sums, product_parts = exchange(
        "tensor", [normed_terms, product_part], [True, False], 3
    )
    grad_normed = jnp.sum(normed_sums.astype(jnp.float32), axis=0)
    product_sum = jnp.sum(product_parts, axis=0).reshape(seq_length, 1)
    scaled_grad = grad_normed * gain_local
    grad_input = (inv_rms * (scaled_grad - unit_rows * (product_sum / model_width))).astype(
        jnp.bfloat16
    )
    gain_part = jnp.sum(grad_normed * unit_rows, axis=0).reshape(1, local_cols)
    (gain_parts,) = exchange("dp", [gain_part], [False], 4)
    grad_gain = jnp.sum(gain_parts, axis=(0, 1))
    (keyval_rows,) = exchange("dp", [grad_keyval], [False], 5)
    keyval_all = keyval_rows.reshape(-1, group_cols)
    rows_normed = lax.all_to_all(normed_full, "dp", split_axis=1, concat_axis=0, tiled=True)
    keyval_weight_grad = lax.dot_general(
        rows_normed, keyval_all, (((0,), (0,)), ((), ())), preferred_element_type=jnp.float32
    )
    return (grad_input, grad_gain, keyval_weight_grad.astype(jnp.bfloat16))


def solution(mesh):
    in_specs = (P("dp", "tensor"), P("dp", "tensor"), P(), P("dp", "tensor"), P("dp", "tensor"))
    out_specs = (P("dp", "tensor"), P("tensor"), P("dp", "tensor"))
    return jax.shard_map(
        on_device, mesh=mesh, in_specs=in_specs, out_specs=out_specs, check_vma=False
    )
```

```python
import functools
import math

import jax
import jax.numpy as jnp
from jax import lax
from jax.experimental import pallas as pl
from jax.experimental.pallas import tpu as pltpu
from jax.sharding import PartitionSpec as P

MESH = pl.DeviceIdType.MESH


def exchange_kernel(axis, n, per_peer, *refs):
    count = len(per_peer)
    src_refs = refs[:count]
    out_refs = refs[count : 2 * count]
    send_sems, recv_sems = refs[2 * count :]
    me = lax.axis_index(axis)
    barrier = pltpu.get_barrier_semaphore()
    for step in range(1, n):
        peer = lax.rem(me + step, n)
        pl.semaphore_signal(barrier, inc=1, device_id={axis: peer}, device_id_type=MESH)
    pl.semaphore_wait(barrier, n - 1)
    copies = []
    for index in range(count):
        for step in range(1, n):
            peer = lax.rem(me + step, n)
            source = src_refs[index].at[peer] if per_peer[index] else src_refs[index]
            copy = pltpu.make_async_remote_copy(
                src_ref=source,
                dst_ref=out_refs[index].at[me],
                send_sem=send_sems.at[index, step],
                recv_sem=recv_sems.at[index, step],
                device_id={axis: peer},
                device_id_type=MESH,
            )
            copy.start()
            copies.append(copy)
    for index in range(count):
        own = src_refs[index][me] if per_peer[index] else src_refs[index][...]
        out_refs[index][me] = own
    for copy in copies:
        copy.wait_send()
    for copy in copies:
        copy.wait_recv()


def exchange(axis, blocks, per_peer, collective_id):
    n = lax.axis_size(axis)
    out_shapes = []
    for block, spread in zip(blocks, per_peer):
        shape = block.shape[1:] if spread else block.shape
        out_shapes.append(jax.ShapeDtypeStruct((n,) + tuple(shape), block.dtype))
    count = len(blocks)
    sent = sum(b.size * b.dtype.itemsize * (1 if s else n) for b, s in zip(blocks, per_peer))
    return pl.pallas_call(
        functools.partial(exchange_kernel, axis, n, tuple(per_peer)),
        out_shape=tuple(out_shapes),
        in_specs=[pl.BlockSpec(memory_space=pltpu.VMEM)] * count,
        out_specs=tuple(pl.BlockSpec(memory_space=pltpu.VMEM) for _ in range(count)),
        scratch_shapes=[
            pltpu.SemaphoreType.DMA((count, n)),
            pltpu.SemaphoreType.DMA((count, n)),
        ],
        compiler_params=pltpu.CompilerParams(collective_id=collective_id, has_side_effects=True),
        cost_estimate=pl.CostEstimate(flops=0, bytes_accessed=2 * sent, transcendentals=0),
    )(*blocks)


def ring_gather_kernel(pair_count, ring_count, block_ref, out_ref, send_sems, recv_sems):
    pair_slot = lax.axis_index("dp") // ring_count
    ring_slot = lax.axis_index("dp") % ring_count
    partner = (1 - pair_slot) * ring_count + ring_slot
    right = pair_slot * ring_count + lax.rem(ring_slot + 1, ring_count)
    left = pair_slot * ring_count + lax.rem(ring_slot + ring_count - 1, ring_count)
    me = pair_slot * ring_count + ring_slot
    barrier = pltpu.get_barrier_semaphore()
    for peer in (partner, right, left):
        pl.semaphore_signal(barrier, inc=1, device_id={"dp": peer}, device_id_type=MESH)
    pl.semaphore_wait(barrier, 3)
    swap = pltpu.make_async_remote_copy(
        src_ref=block_ref,
        dst_ref=out_ref.at[me],
        send_sem=send_sems.at[2, 0, 0],
        recv_sem=recv_sems.at[2, 0, 0],
        device_id={"dp": partner},
        device_id_type=MESH,
    )
    swap.start()
    own = pltpu.make_async_copy(block_ref, out_ref.at[me], send_sems.at[2, 1, 0])
    own.start()
    own.wait()
    swap.wait_send()
    swap.wait_recv()
    right_steps = ring_count // 2
    left_steps = ring_count - 1 - right_steps
    sent = []

    def send(direction, step, target, origin):
        copies = []
        for member in range(pair_count):
            slot = member * ring_count + origin
            copy = pltpu.make_async_remote_copy(
                src_ref=out_ref.at[slot],
                dst_ref=out_ref.at[slot],
                send_sem=send_sems.at[direction, step, member],
                recv_sem=recv_sems.at[direction, step, member],
                device_id={"dp": target},
                device_id_type=MESH,
            )
            copy.start()
            copies.append(copy)
        sent.extend(copies)
        return copies

    right_copies = send(0, 0, right, ring_slot)
    left_copies = send(1, 0, left, ring_slot) if left_steps > 0 else []
    for step in range(1, right_steps):
        for copy in right_copies:
            copy.wait_recv()
        origin = lax.rem(ring_slot + ring_count - step, ring_count)
        right_copies = send(0, step, right, origin)
        if step < left_steps:
            for copy in left_copies:
                copy.wait_recv()
            origin = lax.rem(ring_slot + step, ring_count)
            left_copies = send(1, step, left, origin)
    for copy in right_copies + left_copies:
        copy.wait_recv()
    for copy in sent:
        copy.wait_send()


def ring_gather(block, collective_id):
    count = lax.axis_size("dp")
    pair_count = 2
    ring_count = count // pair_count
    return pl.pallas_call(
        functools.partial(ring_gather_kernel, pair_count, ring_count),
        out_shape=jax.ShapeDtypeStruct((count,) + block.shape, block.dtype),
        in_specs=[pl.BlockSpec(memory_space=pltpu.VMEM)],
        out_specs=pl.BlockSpec(memory_space=pltpu.VMEM),
        scratch_shapes=[
            pltpu.SemaphoreType.DMA((3, ring_count, pair_count)),
            pltpu.SemaphoreType.DMA((3, ring_count, pair_count)),
        ],
        compiler_params=pltpu.CompilerParams(
            collective_id=collective_id, has_side_effects=True, vmem_limit_bytes=48 * 1024 * 1024
        ),
        cost_estimate=pl.CostEstimate(
            flops=0, bytes_accessed=2 * count * block.size * block.dtype.itemsize, transcendentals=0
        ),
    )(block)


HD = 128
KV_HEADS = 4
HEADS_DEV = 4


def rope_tables(length, head_size):
    positions = lax.broadcasted_iota(jnp.int32, (length, head_size // 2), 0).astype(jnp.float32)
    index_half = lax.broadcasted_iota(jnp.int32, (length, head_size // 2), 1).astype(jnp.float32)
    frequency = jnp.exp(-(2.0 * index_half / head_size) * math.log(500000.0))
    angles = positions * frequency
    return (jnp.cos(angles), jnp.sin(angles))


def rotate(vectors, cosine_table, sine_table):
    half_size = vectors.shape[-1] // 2
    first_half = vectors[..., :half_size]
    second_half = vectors[..., half_size:]
    return jnp.concatenate(
        [
            first_half * cosine_table - second_half * sine_table,
            first_half * sine_table + second_half * cosine_table,
        ],
        axis=-1,
    )


def unrotate(vectors, cosine_table, sine_table):
    half_size = vectors.shape[-1] // 2
    first_half = vectors[..., :half_size]
    second_half = vectors[..., half_size:]
    return jnp.concatenate(
        [
            first_half * cosine_table + second_half * sine_table,
            second_half * cosine_table - first_half * sine_table,
        ],
        axis=-1,
    )


def on_device(inputs, grad_context, gain, w_query, w_keyval):
    seq_length = inputs.shape[0]
    local_cols = inputs.shape[1]
    model_width = gain.shape[0]
    head_size = HD
    heads_here = HEADS_DEV
    group_cols = w_keyval.shape[1]
    query_cols = w_query.shape[1]
    tensor_count = lax.axis_size("tensor")
    keyval_total = group_cols * tensor_count
    kv_heads = KV_HEADS
    devices_per_group = tensor_count // kv_heads
    score_scale = head_size ** (-0.5)
    tensor_slot = lax.axis_index("tensor")
    gain_local = lax.dynamic_slice_in_dim(gain, tensor_slot * local_cols, local_cols, 0)
    split_cols = query_cols // 2
    engine_block = jnp.concatenate([w_query[:, :split_cols], w_keyval], axis=1)
    engine_full = lax.all_gather(engine_block, "dp", axis=0, tiled=True)
    ring_full = ring_gather(w_query[:, split_cols:], 6).reshape(-1, query_cols - split_cols)
    (input_blocks,) = exchange("tensor", [inputs], [False], 0)
    inputs_full = (
        input_blocks.transpose(1, 0, 2).reshape(seq_length, model_width).astype(jnp.float32)
    )
    row_sum = jnp.sum(inputs_full * inputs_full, axis=1, keepdims=True)
    inv_rms = lax.rsqrt(row_sum / model_width + 1e-05)
    unit_full = inputs_full * inv_rms
    normed_full = (unit_full * gain[None, :]).astype(jnp.bfloat16)
    unit_rows = inputs.astype(jnp.float32) * inv_rms
    engine_proj = jnp.dot(normed_full, engine_full, preferred_element_type=jnp.float32).astype(
        jnp.bfloat16
    )
    ring_proj = jnp.dot(normed_full, ring_full, preferred_element_type=jnp.float32).astype(
        jnp.bfloat16
    )
    query_proj = jnp.concatenate([engine_proj[:, :split_cols], ring_proj], axis=1)
    keyval_part = engine_proj[:, split_cols:]
    (keyval_blocks,) = exchange("tensor", [keyval_part], [False], 1)
    keyval_full = keyval_blocks.transpose(1, 0, 2).reshape(seq_length, keyval_total)
    group_slot = tensor_slot // devices_per_group
    key_block = lax.dynamic_slice_in_dim(keyval_full, group_slot * head_size, head_size, 1)
    value_block = lax.dynamic_slice_in_dim(
        keyval_full, (kv_heads + group_slot) * head_size, head_size, 1
    )
    cosine_table, sine_table = rope_tables(seq_length, head_size)
    cos_heads = cosine_table[:, None, :]
    sin_heads = sine_table[:, None, :]
    query_heads = query_proj.astype(jnp.float32).reshape(seq_length, heads_here, head_size)
    q_rot = rotate(query_heads, cos_heads, sin_heads).astype(jnp.bfloat16)
    k_rot = rotate(key_block.astype(jnp.float32), cosine_table, sine_table).astype(jnp.bfloat16)
    scores = (
        jnp.einsum("shd,td->hst", q_rot, k_rot, preferred_element_type=jnp.float32) * score_scale
    )
    causal = lax.broadcasted_iota(jnp.int32, (seq_length, seq_length), 0) >= lax.broadcasted_iota(
        jnp.int32, (seq_length, seq_length), 1
    )
    exponent = jnp.where(causal[None, :, :], jnp.exp(scores), 0.0)
    softmax_probs = exponent / jnp.sum(exponent, axis=2, keepdims=True)
    prob_weights = softmax_probs.astype(jnp.bfloat16)
    context = jnp.einsum(
        "hst,td->shd", prob_weights, value_block, preferred_element_type=jnp.float32
    ).astype(jnp.bfloat16)
    grad_ctx = grad_context.reshape(seq_length, heads_here, head_size)
    grad_probs = jnp.einsum(
        "shd,td->hst", grad_ctx, value_block, preferred_element_type=jnp.float32
    )
    row_delta = jnp.sum(grad_ctx.astype(jnp.float32) * context.astype(jnp.float32), axis=2).T[
        :, :, None
    ]
    grad_scores = (softmax_probs * (grad_probs - row_delta) * score_scale).astype(jnp.bfloat16)
    grad_qrot = jnp.einsum("hst,td->shd", grad_scores, k_rot, preferred_element_type=jnp.float32)
    grad_krot = jnp.einsum("hst,shd->td", grad_scores, q_rot, preferred_element_type=jnp.float32)
    grad_value = jnp.einsum(
        "hst,shd->td", prob_weights, grad_ctx, preferred_element_type=jnp.float32
    )
    grad_query = (
        unrotate(grad_qrot, cos_heads, sin_heads)
        .astype(jnp.bfloat16)
        .reshape(seq_length, heads_here * head_size)
    )
    grad_terms = jnp.zeros((seq_length, keyval_total), jnp.float32)
    grad_terms = lax.dynamic_update_slice_in_dim(
        grad_terms, unrotate(grad_krot, cosine_table, sine_table), group_slot * head_size, 1
    )
    grad_terms = lax.dynamic_update_slice_in_dim(
        grad_terms, grad_value, (kv_heads + group_slot) * head_size, 1
    )
    term_blocks = grad_terms.reshape(seq_length, tensor_count, group_cols).transpose(1, 0, 2)
    (keyval_terms,) = exchange("tensor", [term_blocks], [True], 2)
    grad_keyval = jnp.sum(keyval_terms, axis=0).astype(jnp.bfloat16)
    engine_blocks = engine_full.reshape(tensor_count, local_cols, split_cols + group_cols)
    ring_blocks = ring_full.reshape(tensor_count, local_cols, query_cols - split_cols)
    engine_grads = jnp.concatenate([grad_query[:, :split_cols], grad_keyval], axis=1)
    normed_terms = (
        jnp.einsum("rc,pkc->prk", engine_grads, engine_blocks, preferred_element_type=jnp.float32)
        + jnp.einsum(
            "rc,pkc->prk",
            grad_query[:, split_cols:],
            ring_blocks,
            preferred_element_type=jnp.float32,
        )
    ).astype(jnp.bfloat16)
    unit_blocks = unit_full.reshape(seq_length, tensor_count, local_cols).transpose(1, 0, 2)
    gain_blocks = gain.reshape(tensor_count, 1, local_cols)
    product_part = jnp.sum(
        normed_terms.astype(jnp.float32) * gain_blocks * unit_blocks, axis=(0, 2)
    ).reshape(1, seq_length)
    normed_sums, product_parts = exchange(
        "tensor", [normed_terms, product_part], [True, False], 3
    )
    grad_normed = jnp.sum(normed_sums.astype(jnp.float32), axis=0)
    product_sum = jnp.sum(product_parts, axis=0).reshape(seq_length, 1)
    scaled_grad = grad_normed * gain_local
    grad_input = (inv_rms * (scaled_grad - unit_rows * (product_sum / model_width))).astype(
        jnp.bfloat16
    )
    gain_part = jnp.sum(grad_normed * unit_rows, axis=0).reshape(1, local_cols)
    (gain_parts,) = exchange("dp", [gain_part], [False], 4)
    grad_gain = jnp.sum(gain_parts, axis=(0, 1))
    (keyval_rows,) = exchange("dp", [grad_keyval], [False], 5)
    keyval_all = keyval_rows.reshape(-1, group_cols)
    normed_late, _ = lax.optimization_barrier((normed_full, grad_keyval))
    rows_normed = lax.all_to_all(normed_late, "dp", split_axis=1, concat_axis=0, tiled=True)
    keyval_weight_grad = lax.dot_general(
        rows_normed, keyval_all, (((0,), (0,)), ((), ())), preferred_element_type=jnp.float32
    )
    return (grad_input, grad_gain, keyval_weight_grad.astype(jnp.bfloat16))


def solution(mesh):
    in_specs = (P("dp", "tensor"), P("dp", "tensor"), P(), P("dp", "tensor"), P("dp", "tensor"))
    out_specs = (P("dp", "tensor"), P("tensor"), P("dp", "tensor"))
    return jax.shard_map(
        on_device, mesh=mesh, in_specs=in_specs, out_specs=out_specs, check_vma=False
    )
```

```python
import functools
import math

import jax
import jax.numpy as jnp
from jax import lax
from jax.experimental import pallas as pl
from jax.experimental.pallas import tpu as pltpu
from jax.sharding import PartitionSpec as P

MESH = pl.DeviceIdType.MESH


def exchange_kernel(axes, sizes, per_peer, *refs):
    count = len(per_peer)
    src_refs = refs[:count]
    out_refs = refs[count : 2 * count]
    send_sems, recv_sems = refs[2 * count :]
    barrier = pltpu.get_barrier_semaphore()
    waits = 0
    for axis in dict.fromkeys(axes):
        n = sizes[axes.index(axis)]
        me = lax.axis_index(axis)
        for step in range(1, n):
            peer = lax.rem(me + step, n)
            pl.semaphore_signal(barrier, inc=1, device_id={axis: peer}, device_id_type=MESH)
        waits += n - 1
    pl.semaphore_wait(barrier, waits)
    copies = []
    for index in range(count):
        axis, n = axes[index], sizes[index]
        me = lax.axis_index(axis)
        for step in range(1, n):
            peer = lax.rem(me + step, n)
            source = src_refs[index].at[peer] if per_peer[index] else src_refs[index]
            copy = pltpu.make_async_remote_copy(
                src_ref=source,
                dst_ref=out_refs[index].at[me],
                send_sem=send_sems.at[index, step],
                recv_sem=recv_sems.at[index, step],
                device_id={axis: peer},
                device_id_type=MESH,
            )
            copy.start()
            copies.append(copy)
    for index in range(count):
        me = lax.axis_index(axes[index])
        own = src_refs[index][me] if per_peer[index] else src_refs[index][...]
        out_refs[index][me] = own
    for copy in copies:
        copy.wait_send()
    for copy in copies:
        copy.wait_recv()


def exchange_multi(items, collective_id):
    axes = tuple(axis for axis, _, _ in items)
    sizes = tuple(lax.axis_size(axis) for axis in axes)
    blocks = [block for _, block, _ in items]
    per_peer = tuple(spread for _, _, spread in items)
    out_shapes = []
    sent = 0
    for n, block, spread in zip(sizes, blocks, per_peer):
        shape = block.shape[1:] if spread else block.shape
        out_shapes.append(jax.ShapeDtypeStruct((n,) + tuple(shape), block.dtype))
        sent += block.size * block.dtype.itemsize * (1 if spread else n)
    count = len(blocks)
    return pl.pallas_call(
        functools.partial(exchange_kernel, axes, sizes, per_peer),
        out_shape=tuple(out_shapes),
        in_specs=[pl.BlockSpec(memory_space=pltpu.VMEM)] * count,
        out_specs=tuple(pl.BlockSpec(memory_space=pltpu.VMEM) for _ in range(count)),
        scratch_shapes=[
            pltpu.SemaphoreType.DMA((count, max(sizes))),
            pltpu.SemaphoreType.DMA((count, max(sizes))),
        ],
        compiler_params=pltpu.CompilerParams(collective_id=collective_id, has_side_effects=True),
        cost_estimate=pl.CostEstimate(flops=0, bytes_accessed=2 * sent, transcendentals=0),
    )(*blocks)


def exchange(axis, blocks, per_peer, collective_id):
    return exchange_multi([(axis, b, s) for b, s in zip(blocks, per_peer)], collective_id)


def ring_gather_kernel(pair_count, ring_count, block_ref, out_ref, send_sems, recv_sems):
    pair_slot = lax.axis_index("dp") // ring_count
    ring_slot = lax.axis_index("dp") % ring_count
    partner = (1 - pair_slot) * ring_count + ring_slot
    right = pair_slot * ring_count + lax.rem(ring_slot + 1, ring_count)
    left = pair_slot * ring_count + lax.rem(ring_slot + ring_count - 1, ring_count)
    me = pair_slot * ring_count + ring_slot
    barrier = pltpu.get_barrier_semaphore()
    for peer in (partner, right, left):
        pl.semaphore_signal(barrier, inc=1, device_id={"dp": peer}, device_id_type=MESH)
    pl.semaphore_wait(barrier, 3)
    swap = pltpu.make_async_remote_copy(
        src_ref=block_ref,
        dst_ref=out_ref.at[me],
        send_sem=send_sems.at[2, 0, 0],
        recv_sem=recv_sems.at[2, 0, 0],
        device_id={"dp": partner},
        device_id_type=MESH,
    )
    swap.start()
    own = pltpu.make_async_copy(block_ref, out_ref.at[me], send_sems.at[2, 1, 0])
    own.start()
    own.wait()
    swap.wait_send()
    swap.wait_recv()
    right_steps = ring_count // 2
    left_steps = ring_count - 1 - right_steps
    sent = []

    def send(direction, step, target, origin):
        copies = []
        for member in range(pair_count):
            slot = member * ring_count + origin
            copy = pltpu.make_async_remote_copy(
                src_ref=out_ref.at[slot],
                dst_ref=out_ref.at[slot],
                send_sem=send_sems.at[direction, step, member],
                recv_sem=recv_sems.at[direction, step, member],
                device_id={"dp": target},
                device_id_type=MESH,
            )
            copy.start()
            copies.append(copy)
        sent.extend(copies)
        return copies

    right_copies = send(0, 0, right, ring_slot)
    left_copies = send(1, 0, left, ring_slot) if left_steps > 0 else []
    for step in range(1, right_steps):
        for copy in right_copies:
            copy.wait_recv()
        origin = lax.rem(ring_slot + ring_count - step, ring_count)
        right_copies = send(0, step, right, origin)
        if step < left_steps:
            for copy in left_copies:
                copy.wait_recv()
            origin = lax.rem(ring_slot + step, ring_count)
            left_copies = send(1, step, left, origin)
    for copy in right_copies + left_copies:
        copy.wait_recv()
    for copy in sent:
        copy.wait_send()


def ring_gather(block, collective_id):
    count = lax.axis_size("dp")
    pair_count = 2
    ring_count = count // pair_count
    return pl.pallas_call(
        functools.partial(ring_gather_kernel, pair_count, ring_count),
        out_shape=jax.ShapeDtypeStruct((count,) + block.shape, block.dtype),
        in_specs=[pl.BlockSpec(memory_space=pltpu.VMEM)],
        out_specs=pl.BlockSpec(memory_space=pltpu.VMEM),
        scratch_shapes=[
            pltpu.SemaphoreType.DMA((3, ring_count, pair_count)),
            pltpu.SemaphoreType.DMA((3, ring_count, pair_count)),
        ],
        compiler_params=pltpu.CompilerParams(
            collective_id=collective_id, has_side_effects=True, vmem_limit_bytes=48 * 1024 * 1024
        ),
        cost_estimate=pl.CostEstimate(
            flops=0, bytes_accessed=2 * count * block.size * block.dtype.itemsize, transcendentals=0
        ),
    )(block)


HD = 128
KV_HEADS = 4
HEADS_DEV = 4


def rope_tables(length, head_size):
    positions = lax.broadcasted_iota(jnp.int32, (length, head_size // 2), 0).astype(jnp.float32)
    index_half = lax.broadcasted_iota(jnp.int32, (length, head_size // 2), 1).astype(jnp.float32)
    frequency = jnp.exp(-(2.0 * index_half / head_size) * math.log(500000.0))
    angles = positions * frequency
    return (jnp.cos(angles), jnp.sin(angles))


def rotate(vectors, cosine_table, sine_table):
    half_size = vectors.shape[-1] // 2
    first_half = vectors[..., :half_size]
    second_half = vectors[..., half_size:]
    return jnp.concatenate(
        [
            first_half * cosine_table - second_half * sine_table,
            first_half * sine_table + second_half * cosine_table,
        ],
        axis=-1,
    )


def unrotate(vectors, cosine_table, sine_table):
    half_size = vectors.shape[-1] // 2
    first_half = vectors[..., :half_size]
    second_half = vectors[..., half_size:]
    return jnp.concatenate(
        [
            first_half * cosine_table + second_half * sine_table,
            second_half * cosine_table - first_half * sine_table,
        ],
        axis=-1,
    )


def on_device(inputs, grad_context, gain, w_query, w_keyval):
    seq_length = inputs.shape[0]
    local_cols = inputs.shape[1]
    model_width = gain.shape[0]
    head_size = HD
    heads_here = HEADS_DEV
    group_cols = w_keyval.shape[1]
    query_cols = w_query.shape[1]
    tensor_count = lax.axis_size("tensor")
    keyval_total = group_cols * tensor_count
    kv_heads = KV_HEADS
    devices_per_group = tensor_count // kv_heads
    score_scale = head_size ** (-0.5)
    tensor_slot = lax.axis_index("tensor")
    gain_local = lax.dynamic_slice_in_dim(gain, tensor_slot * local_cols, local_cols, 0)
    split_cols = query_cols // 2
    engine_block = jnp.concatenate([w_query[:, :split_cols], w_keyval], axis=1)
    engine_full = lax.all_gather(engine_block, "dp", axis=0, tiled=True)
    ring_full = ring_gather(w_query[:, split_cols:], 6).reshape(-1, query_cols - split_cols)
    (input_blocks,) = exchange("tensor", [inputs], [False], 0)
    inputs_full = (
        input_blocks.transpose(1, 0, 2).reshape(seq_length, model_width).astype(jnp.float32)
    )
    row_sum = jnp.sum(inputs_full * inputs_full, axis=1, keepdims=True)
    inv_rms = lax.rsqrt(row_sum / model_width + 1e-05)
    unit_full = inputs_full * inv_rms
    normed_full = (unit_full * gain[None, :]).astype(jnp.bfloat16)
    unit_rows = inputs.astype(jnp.float32) * inv_rms
    engine_proj = jnp.dot(normed_full, engine_full, preferred_element_type=jnp.float32).astype(
        jnp.bfloat16
    )
    ring_proj = jnp.dot(normed_full, ring_full, preferred_element_type=jnp.float32).astype(
        jnp.bfloat16
    )
    query_proj = jnp.concatenate([engine_proj[:, :split_cols], ring_proj], axis=1)
    keyval_part = engine_proj[:, split_cols:]
    (keyval_blocks,) = exchange("tensor", [keyval_part], [False], 1)
    keyval_full = keyval_blocks.transpose(1, 0, 2).reshape(seq_length, keyval_total)
    group_slot = tensor_slot // devices_per_group
    key_block = lax.dynamic_slice_in_dim(keyval_full, group_slot * head_size, head_size, 1)
    value_block = lax.dynamic_slice_in_dim(
        keyval_full, (kv_heads + group_slot) * head_size, head_size, 1
    )
    cosine_table, sine_table = rope_tables(seq_length, head_size)
    cos_heads = cosine_table[:, None, :]
    sin_heads = sine_table[:, None, :]
    query_heads = query_proj.astype(jnp.float32).reshape(seq_length, heads_here, head_size)
    q_rot = rotate(query_heads, cos_heads, sin_heads).astype(jnp.bfloat16)
    k_rot = rotate(key_block.astype(jnp.float32), cosine_table, sine_table).astype(jnp.bfloat16)
    scores = (
        jnp.einsum("shd,td->hst", q_rot, k_rot, preferred_element_type=jnp.float32) * score_scale
    )
    causal = lax.broadcasted_iota(jnp.int32, (seq_length, seq_length), 0) >= lax.broadcasted_iota(
        jnp.int32, (seq_length, seq_length), 1
    )
    exponent = jnp.where(causal[None, :, :], jnp.exp(scores), 0.0)
    softmax_probs = exponent / jnp.sum(exponent, axis=2, keepdims=True)
    prob_weights = softmax_probs.astype(jnp.bfloat16)
    context = jnp.einsum(
        "hst,td->shd", prob_weights, value_block, preferred_element_type=jnp.float32
    ).astype(jnp.bfloat16)
    grad_ctx = grad_context.reshape(seq_length, heads_here, head_size)
    grad_probs = jnp.einsum(
        "shd,td->hst", grad_ctx, value_block, preferred_element_type=jnp.float32
    )
    row_delta = jnp.sum(grad_ctx.astype(jnp.float32) * context.astype(jnp.float32), axis=2).T[
        :, :, None
    ]
    grad_scores = (softmax_probs * (grad_probs - row_delta) * score_scale).astype(jnp.bfloat16)
    grad_qrot = jnp.einsum("hst,td->shd", grad_scores, k_rot, preferred_element_type=jnp.float32)
    grad_krot = jnp.einsum("hst,shd->td", grad_scores, q_rot, preferred_element_type=jnp.float32)
    grad_value = jnp.einsum(
        "hst,shd->td", prob_weights, grad_ctx, preferred_element_type=jnp.float32
    )
    grad_query = (
        unrotate(grad_qrot, cos_heads, sin_heads)
        .astype(jnp.bfloat16)
        .reshape(seq_length, heads_here * head_size)
    )
    grad_terms = jnp.zeros((seq_length, keyval_total), jnp.float32)
    grad_terms = lax.dynamic_update_slice_in_dim(
        grad_terms, unrotate(grad_krot, cosine_table, sine_table), group_slot * head_size, 1
    )
    grad_terms = lax.dynamic_update_slice_in_dim(
        grad_terms, grad_value, (kv_heads + group_slot) * head_size, 1
    )
    term_blocks = grad_terms.reshape(seq_length, tensor_count, group_cols).transpose(1, 0, 2)
    (keyval_terms,) = exchange("tensor", [term_blocks], [True], 2)
    grad_keyval = jnp.sum(keyval_terms, axis=0).astype(jnp.bfloat16)
    engine_blocks = engine_full.reshape(tensor_count, local_cols, split_cols + group_cols)
    ring_blocks = ring_full.reshape(tensor_count, local_cols, query_cols - split_cols)
    engine_grads = jnp.concatenate([grad_query[:, :split_cols], grad_keyval], axis=1)
    normed_terms = (
        jnp.einsum("rc,pkc->prk", engine_grads, engine_blocks, preferred_element_type=jnp.float32)
        + jnp.einsum(
            "rc,pkc->prk",
            grad_query[:, split_cols:],
            ring_blocks,
            preferred_element_type=jnp.float32,
        )
    ).astype(jnp.bfloat16)
    unit_blocks = unit_full.reshape(seq_length, tensor_count, local_cols).transpose(1, 0, 2)
    gain_blocks = gain.reshape(tensor_count, 1, local_cols)
    product_part = jnp.sum(
        normed_terms.astype(jnp.float32) * gain_blocks * unit_blocks, axis=(0, 2)
    ).reshape(1, seq_length)
    keyval_partials = (
        jnp.einsum("rk,rc->kc", normed_full, grad_keyval, preferred_element_type=jnp.float32)
        .astype(jnp.bfloat16)
        .reshape(lax.axis_size("dp"), -1, group_cols)
    )
    normed_sums, product_parts, keyval_sums = exchange_multi(
        [
            ("tensor", normed_terms, True),
            ("tensor", product_part, False),
            ("dp", keyval_partials, True),
        ],
        3,
    )
    grad_normed = jnp.sum(normed_sums.astype(jnp.float32), axis=0)
    product_sum = jnp.sum(product_parts, axis=0).reshape(seq_length, 1)
    scaled_grad = grad_normed * gain_local
    grad_input = (inv_rms * (scaled_grad - unit_rows * (product_sum / model_width))).astype(
        jnp.bfloat16
    )
    gain_part = jnp.sum(grad_normed * unit_rows, axis=0).reshape(1, local_cols)
    (gain_parts,) = exchange("dp", [gain_part], [False], 4)
    grad_gain = jnp.sum(gain_parts, axis=(0, 1))
    keyval_weight_grad = jnp.sum(keyval_sums.astype(jnp.float32), axis=0)
    return (grad_input, grad_gain, keyval_weight_grad.astype(jnp.bfloat16))


def solution(mesh):
    in_specs = (P("dp", "tensor"), P("dp", "tensor"), P(), P("dp", "tensor"), P("dp", "tensor"))
    out_specs = (P("dp", "tensor"), P("tensor"), P("dp", "tensor"))
    return jax.shard_map(
        on_device, mesh=mesh, in_specs=in_specs, out_specs=out_specs, check_vma=False
    )
```

```python
import functools
import math

import jax
import jax.numpy as jnp
from jax import lax
from jax.experimental import pallas as pl
from jax.experimental.pallas import tpu as pltpu
from jax.sharding import PartitionSpec as P

MESH = pl.DeviceIdType.MESH


def exchange_kernel(axes, sizes, per_peer, *refs):
    count = len(per_peer)
    src_refs = refs[:count]
    out_refs = refs[count : 2 * count]
    send_sems, recv_sems = refs[2 * count :]
    barrier = pltpu.get_barrier_semaphore()
    waits = 0
    for axis in dict.fromkeys(axes):
        n = sizes[axes.index(axis)]
        me = lax.axis_index(axis)
        for step in range(1, n):
            peer = lax.rem(me + step, n)
            pl.semaphore_signal(barrier, inc=1, device_id={axis: peer}, device_id_type=MESH)
        waits += n - 1
    pl.semaphore_wait(barrier, waits)
    copies = []
    for index in range(count):
        axis, n = axes[index], sizes[index]
        me = lax.axis_index(axis)
        for step in range(1, n):
            peer = lax.rem(me + step, n)
            source = src_refs[index].at[peer] if per_peer[index] else src_refs[index]
            copy = pltpu.make_async_remote_copy(
                src_ref=source,
                dst_ref=out_refs[index].at[me],
                send_sem=send_sems.at[index, step],
                recv_sem=recv_sems.at[index, step],
                device_id={axis: peer},
                device_id_type=MESH,
            )
            copy.start()
            copies.append(copy)
    for index in range(count):
        me = lax.axis_index(axes[index])
        own = src_refs[index][me] if per_peer[index] else src_refs[index][...]
        out_refs[index][me] = own
    for copy in copies:
        copy.wait_send()
    for copy in copies:
        copy.wait_recv()


def exchange_multi(items, collective_id):
    axes = tuple(axis for axis, _, _ in items)
    sizes = tuple(lax.axis_size(axis) for axis in axes)
    blocks = [block for _, block, _ in items]
    per_peer = tuple(spread for _, _, spread in items)
    out_shapes = []
    sent = 0
    for n, block, spread in zip(sizes, blocks, per_peer):
        shape = block.shape[1:] if spread else block.shape
        out_shapes.append(jax.ShapeDtypeStruct((n,) + tuple(shape), block.dtype))
        sent += block.size * block.dtype.itemsize * (1 if spread else n)
    count = len(blocks)
    return pl.pallas_call(
        functools.partial(exchange_kernel, axes, sizes, per_peer),
        out_shape=tuple(out_shapes),
        in_specs=[pl.BlockSpec(memory_space=pltpu.VMEM)] * count,
        out_specs=tuple(pl.BlockSpec(memory_space=pltpu.VMEM) for _ in range(count)),
        scratch_shapes=[
            pltpu.SemaphoreType.DMA((count, max(sizes))),
            pltpu.SemaphoreType.DMA((count, max(sizes))),
        ],
        compiler_params=pltpu.CompilerParams(collective_id=collective_id, has_side_effects=True),
        cost_estimate=pl.CostEstimate(flops=0, bytes_accessed=2 * sent, transcendentals=0),
    )(*blocks)


def exchange(axis, blocks, per_peer, collective_id):
    return exchange_multi([(axis, b, s) for b, s in zip(blocks, per_peer)], collective_id)


def ring_gather_kernel(pair_count, ring_count, block_ref, out_ref, send_sems, recv_sems):
    pair_slot = lax.axis_index("dp") // ring_count
    ring_slot = lax.axis_index("dp") % ring_count
    partner = (1 - pair_slot) * ring_count + ring_slot
    right = pair_slot * ring_count + lax.rem(ring_slot + 1, ring_count)
    left = pair_slot * ring_count + lax.rem(ring_slot + ring_count - 1, ring_count)
    me = pair_slot * ring_count + ring_slot
    barrier = pltpu.get_barrier_semaphore()
    for peer in (partner, right, left):
        pl.semaphore_signal(barrier, inc=1, device_id={"dp": peer}, device_id_type=MESH)
    pl.semaphore_wait(barrier, 3)
    swap = pltpu.make_async_remote_copy(
        src_ref=block_ref,
        dst_ref=out_ref.at[me],
        send_sem=send_sems.at[2, 0, 0],
        recv_sem=recv_sems.at[2, 0, 0],
        device_id={"dp": partner},
        device_id_type=MESH,
    )
    swap.start()
    own = pltpu.make_async_copy(block_ref, out_ref.at[me], send_sems.at[2, 1, 0])
    own.start()
    own.wait()
    swap.wait_send()
    swap.wait_recv()
    right_steps = ring_count // 2
    left_steps = ring_count - 1 - right_steps
    sent = []

    def send(direction, step, target, origin):
        copies = []
        for member in range(pair_count):
            slot = member * ring_count + origin
            copy = pltpu.make_async_remote_copy(
                src_ref=out_ref.at[slot],
                dst_ref=out_ref.at[slot],
                send_sem=send_sems.at[direction, step, member],
                recv_sem=recv_sems.at[direction, step, member],
                device_id={"dp": target},
                device_id_type=MESH,
            )
            copy.start()
            copies.append(copy)
        sent.extend(copies)
        return copies

    right_copies = send(0, 0, right, ring_slot)
    left_copies = send(1, 0, left, ring_slot) if left_steps > 0 else []
    for step in range(1, right_steps):
        for copy in right_copies:
            copy.wait_recv()
        origin = lax.rem(ring_slot + ring_count - step, ring_count)
        right_copies = send(0, step, right, origin)
        if step < left_steps:
            for copy in left_copies:
                copy.wait_recv()
            origin = lax.rem(ring_slot + step, ring_count)
            left_copies = send(1, step, left, origin)
    for copy in right_copies + left_copies:
        copy.wait_recv()
    for copy in sent:
        copy.wait_send()


def ring_gather(block, collective_id):
    count = lax.axis_size("dp")
    pair_count = 2
    ring_count = count // pair_count
    return pl.pallas_call(
        functools.partial(ring_gather_kernel, pair_count, ring_count),
        out_shape=jax.ShapeDtypeStruct((count,) + block.shape, block.dtype),
        in_specs=[pl.BlockSpec(memory_space=pltpu.VMEM)],
        out_specs=pl.BlockSpec(memory_space=pltpu.VMEM),
        scratch_shapes=[
            pltpu.SemaphoreType.DMA((3, ring_count, pair_count)),
            pltpu.SemaphoreType.DMA((3, ring_count, pair_count)),
        ],
        compiler_params=pltpu.CompilerParams(
            collective_id=collective_id, has_side_effects=True, vmem_limit_bytes=48 * 1024 * 1024
        ),
        cost_estimate=pl.CostEstimate(
            flops=0, bytes_accessed=2 * count * block.size * block.dtype.itemsize, transcendentals=0
        ),
    )(block)


HD = 128
KV_HEADS = 4
HEADS_DEV = 4


def rope_tables(length, head_size):
    positions = lax.broadcasted_iota(jnp.int32, (length, head_size // 2), 0).astype(jnp.float32)
    index_half = lax.broadcasted_iota(jnp.int32, (length, head_size // 2), 1).astype(jnp.float32)
    frequency = jnp.exp(-(2.0 * index_half / head_size) * math.log(500000.0))
    angles = positions * frequency
    return (jnp.cos(angles), jnp.sin(angles))


def rotate(vectors, cosine_table, sine_table):
    half_size = vectors.shape[-1] // 2
    first_half = vectors[..., :half_size]
    second_half = vectors[..., half_size:]
    return jnp.concatenate(
        [
            first_half * cosine_table - second_half * sine_table,
            first_half * sine_table + second_half * cosine_table,
        ],
        axis=-1,
    )


def unrotate(vectors, cosine_table, sine_table):
    half_size = vectors.shape[-1] // 2
    first_half = vectors[..., :half_size]
    second_half = vectors[..., half_size:]
    return jnp.concatenate(
        [
            first_half * cosine_table + second_half * sine_table,
            second_half * cosine_table - first_half * sine_table,
        ],
        axis=-1,
    )


def on_device(inputs, grad_context, gain, w_query, w_keyval):
    seq_length = inputs.shape[0]
    local_cols = inputs.shape[1]
    model_width = gain.shape[0]
    head_size = HD
    heads_here = HEADS_DEV
    group_cols = w_keyval.shape[1]
    query_cols = w_query.shape[1]
    tensor_count = lax.axis_size("tensor")
    keyval_total = group_cols * tensor_count
    kv_heads = KV_HEADS
    devices_per_group = tensor_count // kv_heads
    score_scale = head_size ** (-0.5)
    tensor_slot = lax.axis_index("tensor")
    gain_local = lax.dynamic_slice_in_dim(gain, tensor_slot * local_cols, local_cols, 0)
    split_cols = query_cols // 2
    engine_block = jnp.concatenate([w_query[:, :split_cols], w_keyval], axis=1)
    engine_full = lax.all_gather(engine_block, "dp", axis=0, tiled=True)
    ring_full = ring_gather(w_query[:, split_cols:], 6).reshape(-1, query_cols - split_cols)
    (input_blocks,) = exchange("tensor", [inputs], [False], 0)
    inputs_full = (
        input_blocks.transpose(1, 0, 2).reshape(seq_length, model_width).astype(jnp.float32)
    )
    row_sum = jnp.sum(inputs_full * inputs_full, axis=1, keepdims=True)
    inv_rms = lax.rsqrt(row_sum / model_width + 1e-05)
    unit_full = inputs_full * inv_rms
    normed_full = (unit_full * gain[None, :]).astype(jnp.bfloat16)
    unit_rows = inputs.astype(jnp.float32) * inv_rms
    engine_proj = jnp.dot(normed_full, engine_full, preferred_element_type=jnp.float32).astype(
        jnp.bfloat16
    )
    ring_proj = jnp.dot(normed_full, ring_full, preferred_element_type=jnp.float32).astype(
        jnp.bfloat16
    )
    query_proj = jnp.concatenate([engine_proj[:, :split_cols], ring_proj], axis=1)
    keyval_part = engine_proj[:, split_cols:]
    (keyval_blocks,) = exchange("tensor", [keyval_part], [False], 1)
    keyval_full = keyval_blocks.transpose(1, 0, 2).reshape(seq_length, keyval_total)
    group_slot = tensor_slot // devices_per_group
    key_block = lax.dynamic_slice_in_dim(keyval_full, group_slot * head_size, head_size, 1)
    value_block = lax.dynamic_slice_in_dim(
        keyval_full, (kv_heads + group_slot) * head_size, head_size, 1
    )
    cosine_table, sine_table = rope_tables(seq_length, head_size)
    cos_heads = cosine_table[:, None, :]
    sin_heads = sine_table[:, None, :]
    query_heads = query_proj.astype(jnp.float32).reshape(seq_length, heads_here, head_size)
    q_rot = rotate(query_heads, cos_heads, sin_heads).astype(jnp.bfloat16)
    k_rot = rotate(key_block.astype(jnp.float32), cosine_table, sine_table).astype(jnp.bfloat16)
    scores = (
        jnp.einsum("shd,td->hst", q_rot, k_rot, preferred_element_type=jnp.float32) * score_scale
    )
    causal = lax.broadcasted_iota(jnp.int32, (seq_length, seq_length), 0) >= lax.broadcasted_iota(
        jnp.int32, (seq_length, seq_length), 1
    )
    exponent = jnp.where(causal[None, :, :], jnp.exp(scores), 0.0)
    softmax_probs = exponent / jnp.sum(exponent, axis=2, keepdims=True)
    prob_weights = softmax_probs.astype(jnp.bfloat16)
    context = jnp.einsum(
        "hst,td->shd", prob_weights, value_block, preferred_element_type=jnp.float32
    ).astype(jnp.bfloat16)
    grad_ctx = grad_context.reshape(seq_length, heads_here, head_size)
    grad_probs = jnp.einsum(
        "shd,td->hst", grad_ctx, value_block, preferred_element_type=jnp.float32
    )
    row_delta = jnp.sum(grad_ctx.astype(jnp.float32) * context.astype(jnp.float32), axis=2).T[
        :, :, None
    ]
    grad_scores = (softmax_probs * (grad_probs - row_delta) * score_scale).astype(jnp.bfloat16)
    grad_qrot = jnp.einsum("hst,td->shd", grad_scores, k_rot, preferred_element_type=jnp.float32)
    grad_krot = jnp.einsum("hst,shd->td", grad_scores, q_rot, preferred_element_type=jnp.float32)
    grad_value = jnp.einsum(
        "hst,shd->td", prob_weights, grad_ctx, preferred_element_type=jnp.float32
    )
    grad_query = (
        unrotate(grad_qrot, cos_heads, sin_heads)
        .astype(jnp.bfloat16)
        .reshape(seq_length, heads_here * head_size)
    )
    grad_terms = jnp.zeros((seq_length, keyval_total), jnp.float32)
    grad_terms = lax.dynamic_update_slice_in_dim(
        grad_terms, unrotate(grad_krot, cosine_table, sine_table), group_slot * head_size, 1
    )
    grad_terms = lax.dynamic_update_slice_in_dim(
        grad_terms, grad_value, (kv_heads + group_slot) * head_size, 1
    )
    term_blocks = grad_terms.reshape(seq_length, tensor_count, group_cols).transpose(1, 0, 2)
    (keyval_terms,) = exchange("tensor", [term_blocks], [True], 2)
    grad_keyval = jnp.sum(keyval_terms, axis=0).astype(jnp.bfloat16)
    engine_blocks = engine_full.reshape(tensor_count, local_cols, split_cols + group_cols)
    ring_blocks = ring_full.reshape(tensor_count, local_cols, query_cols - split_cols)
    engine_grads = jnp.concatenate([grad_query[:, :split_cols], grad_keyval], axis=1)
    normed_terms = (
        jnp.einsum("rc,pkc->prk", engine_grads, engine_blocks, preferred_element_type=jnp.float32)
        + jnp.einsum(
            "rc,pkc->prk",
            grad_query[:, split_cols:],
            ring_blocks,
            preferred_element_type=jnp.float32,
        )
    ).astype(jnp.bfloat16)
    unit_blocks = unit_full.reshape(seq_length, tensor_count, local_cols).transpose(1, 0, 2)
    gain_blocks = gain.reshape(tensor_count, 1, local_cols)
    product_part = jnp.sum(
        normed_terms.astype(jnp.float32) * gain_blocks * unit_blocks, axis=(0, 2)
    ).reshape(1, seq_length)
    dp_count = lax.axis_size("dp")
    keyval_partials = jnp.einsum(
        "rk,rc->kc", normed_full, grad_keyval, preferred_element_type=jnp.float32
    )
    keyval_sums = lax.psum_scatter(keyval_partials, "dp", scatter_dimension=0, tiled=True)
    normed_sums, product_parts = exchange(
        "tensor", [normed_terms, product_part], [True, False], 3
    )
    grad_normed = jnp.sum(normed_sums.astype(jnp.float32), axis=0)
    product_sum = jnp.sum(product_parts, axis=0).reshape(seq_length, 1)
    scaled_grad = grad_normed * gain_local
    grad_input = (inv_rms * (scaled_grad - unit_rows * (product_sum / model_width))).astype(
        jnp.bfloat16
    )
    gain_part = jnp.sum(grad_normed * unit_rows, axis=0).reshape(1, local_cols)
    (gain_parts,) = exchange("dp", [gain_part], [False], 4)
    grad_gain = jnp.sum(gain_parts, axis=(0, 1))
    keyval_weight_grad = keyval_sums
    return (grad_input, grad_gain, keyval_weight_grad.astype(jnp.bfloat16))


def solution(mesh):
    in_specs = (P("dp", "tensor"), P("dp", "tensor"), P(), P("dp", "tensor"), P("dp", "tensor"))
    out_specs = (P("dp", "tensor"), P("tensor"), P("dp", "tensor"))
    return jax.shard_map(
        on_device, mesh=mesh, in_specs=in_specs, out_specs=out_specs, check_vma=False
    )
```

```python
import functools
import math

import jax
import jax.numpy as jnp
from jax import lax
from jax.experimental import pallas as pl
from jax.experimental.pallas import tpu as pltpu
from jax.sharding import PartitionSpec as P

MESH = pl.DeviceIdType.MESH


def exchange_kernel(axes, sizes, per_peer, *refs):
    count = len(per_peer)
    src_refs = refs[:count]
    out_refs = refs[count : 2 * count]
    send_sems, recv_sems = refs[2 * count :]
    barrier = pltpu.get_barrier_semaphore()
    waits = 0
    for axis in dict.fromkeys(axes):
        n = sizes[axes.index(axis)]
        me = lax.axis_index(axis)
        for step in range(1, n):
            peer = lax.rem(me + step, n)
            pl.semaphore_signal(barrier, inc=1, device_id={axis: peer}, device_id_type=MESH)
        waits += n - 1
    pl.semaphore_wait(barrier, waits)
    copies = []
    for index in range(count):
        axis, n = axes[index], sizes[index]
        me = lax.axis_index(axis)
        for step in range(1, n):
            peer = lax.rem(me + step, n)
            source = src_refs[index].at[peer] if per_peer[index] else src_refs[index]
            copy = pltpu.make_async_remote_copy(
                src_ref=source,
                dst_ref=out_refs[index].at[me],
                send_sem=send_sems.at[index, step],
                recv_sem=recv_sems.at[index, step],
                device_id={axis: peer},
                device_id_type=MESH,
            )
            copy.start()
            copies.append(copy)
    for index in range(count):
        me = lax.axis_index(axes[index])
        own = src_refs[index][me] if per_peer[index] else src_refs[index][...]
        out_refs[index][me] = own
    for copy in copies:
        copy.wait_send()
    for copy in copies:
        copy.wait_recv()


def exchange_multi(items, collective_id):
    axes = tuple(axis for axis, _, _ in items)
    sizes = tuple(lax.axis_size(axis) for axis in axes)
    blocks = [block for _, block, _ in items]
    per_peer = tuple(spread for _, _, spread in items)
    out_shapes = []
    sent = 0
    for n, block, spread in zip(sizes, blocks, per_peer):
        shape = block.shape[1:] if spread else block.shape
        out_shapes.append(jax.ShapeDtypeStruct((n,) + tuple(shape), block.dtype))
        sent += block.size * block.dtype.itemsize * (1 if spread else n)
    count = len(blocks)
    return pl.pallas_call(
        functools.partial(exchange_kernel, axes, sizes, per_peer),
        out_shape=tuple(out_shapes),
        in_specs=[pl.BlockSpec(memory_space=pltpu.VMEM)] * count,
        out_specs=tuple(pl.BlockSpec(memory_space=pltpu.VMEM) for _ in range(count)),
        scratch_shapes=[
            pltpu.SemaphoreType.DMA((count, max(sizes))),
            pltpu.SemaphoreType.DMA((count, max(sizes))),
        ],
        compiler_params=pltpu.CompilerParams(collective_id=collective_id, has_side_effects=True),
        cost_estimate=pl.CostEstimate(flops=0, bytes_accessed=2 * sent, transcendentals=0),
    )(*blocks)


def exchange(axis, blocks, per_peer, collective_id):
    return exchange_multi([(axis, b, s) for b, s in zip(blocks, per_peer)], collective_id)


def ring_gather_kernel(
    pair_count, ring_count, side_count, block_ref, side_ref, out_ref, side_out, send_sems, recv_sems, side_send, side_recv
):
    pair_slot = lax.axis_index("dp") // ring_count
    ring_slot = lax.axis_index("dp") % ring_count
    partner = (1 - pair_slot) * ring_count + ring_slot
    right = pair_slot * ring_count + lax.rem(ring_slot + 1, ring_count)
    left = pair_slot * ring_count + lax.rem(ring_slot + ring_count - 1, ring_count)
    me = pair_slot * ring_count + ring_slot
    side_me = lax.axis_index("tensor")
    barrier = pltpu.get_barrier_semaphore()
    for peer in (partner, right, left):
        pl.semaphore_signal(barrier, inc=1, device_id={"dp": peer}, device_id_type=MESH)
    for step in range(1, side_count):
        peer = lax.rem(side_me + step, side_count)
        pl.semaphore_signal(barrier, inc=1, device_id={"tensor": peer}, device_id_type=MESH)
    pl.semaphore_wait(barrier, 3 + side_count - 1)
    side_copies = []
    for step in range(1, side_count):
        peer = lax.rem(side_me + step, side_count)
        copy = pltpu.make_async_remote_copy(
            src_ref=side_ref,
            dst_ref=side_out.at[side_me],
            send_sem=side_send.at[step],
            recv_sem=side_recv.at[step],
            device_id={"tensor": peer},
            device_id_type=MESH,
        )
        copy.start()
        side_copies.append(copy)
    swap = pltpu.make_async_remote_copy(
        src_ref=block_ref,
        dst_ref=out_ref.at[me],
        send_sem=send_sems.at[2, 0, 0],
        recv_sem=recv_sems.at[2, 0, 0],
        device_id={"dp": partner},
        device_id_type=MESH,
    )
    swap.start()
    own = pltpu.make_async_copy(block_ref, out_ref.at[me], send_sems.at[2, 1, 0])
    own.start()
    side_out[side_me] = side_ref[...]
    own.wait()
    swap.wait_send()
    swap.wait_recv()
    right_steps = ring_count // 2
    left_steps = ring_count - 1 - right_steps
    sent = []

    def send(direction, step, target, origin):
        copies = []
        for member in range(pair_count):
            slot = member * ring_count + origin
            copy = pltpu.make_async_remote_copy(
                src_ref=out_ref.at[slot],
                dst_ref=out_ref.at[slot],
                send_sem=send_sems.at[direction, step, member],
                recv_sem=recv_sems.at[direction, step, member],
                device_id={"dp": target},
                device_id_type=MESH,
            )
            copy.start()
            copies.append(copy)
        sent.extend(copies)
        return copies

    right_copies = send(0, 0, right, ring_slot)
    left_copies = send(1, 0, left, ring_slot) if left_steps > 0 else []
    for step in range(1, right_steps):
        for copy in right_copies:
            copy.wait_recv()
        origin = lax.rem(ring_slot + ring_count - step, ring_count)
        right_copies = send(0, step, right, origin)
        if step < left_steps:
            for copy in left_copies:
                copy.wait_recv()
            origin = lax.rem(ring_slot + step, ring_count)
            left_copies = send(1, step, left, origin)
    for copy in right_copies + left_copies:
        copy.wait_recv()
    for copy in sent + side_copies:
        copy.wait_send()
    for copy in side_copies:
        copy.wait_recv()


def ring_gather(block, side, collective_id):
    count = lax.axis_size("dp")
    side_count = lax.axis_size("tensor")
    pair_count = 2
    ring_count = count // pair_count
    sent = count * block.size * block.dtype.itemsize + side_count * side.size * side.dtype.itemsize
    return pl.pallas_call(
        functools.partial(ring_gather_kernel, pair_count, ring_count, side_count),
        out_shape=(
            jax.ShapeDtypeStruct((count,) + block.shape, block.dtype),
            jax.ShapeDtypeStruct((side_count,) + side.shape, side.dtype),
        ),
        in_specs=[pl.BlockSpec(memory_space=pltpu.VMEM)] * 2,
        out_specs=(pl.BlockSpec(memory_space=pltpu.VMEM), pl.BlockSpec(memory_space=pltpu.VMEM)),
        scratch_shapes=[
            pltpu.SemaphoreType.DMA((3, ring_count, pair_count)),
            pltpu.SemaphoreType.DMA((3, ring_count, pair_count)),
            pltpu.SemaphoreType.DMA((side_count,)),
            pltpu.SemaphoreType.DMA((side_count,)),
        ],
        compiler_params=pltpu.CompilerParams(
            collective_id=collective_id, has_side_effects=True, vmem_limit_bytes=48 * 1024 * 1024
        ),
        cost_estimate=pl.CostEstimate(flops=0, bytes_accessed=2 * sent, transcendentals=0),
    )(block, side)

HD = 128
KV_HEADS = 4
HEADS_DEV = 4


def rope_tables(length, head_size):
    positions = lax.broadcasted_iota(jnp.int32, (length, head_size // 2), 0).astype(jnp.float32)
    index_half = lax.broadcasted_iota(jnp.int32, (length, head_size // 2), 1).astype(jnp.float32)
    frequency = jnp.exp(-(2.0 * index_half / head_size) * math.log(500000.0))
    angles = positions * frequency
    return (jnp.cos(angles), jnp.sin(angles))


def rotate(vectors, cosine_table, sine_table):
    half_size = vectors.shape[-1] // 2
    first_half = vectors[..., :half_size]
    second_half = vectors[..., half_size:]
    return jnp.concatenate(
        [
            first_half * cosine_table - second_half * sine_table,
            first_half * sine_table + second_half * cosine_table,
        ],
        axis=-1,
    )


def unrotate(vectors, cosine_table, sine_table):
    half_size = vectors.shape[-1] // 2
    first_half = vectors[..., :half_size]
    second_half = vectors[..., half_size:]
    return jnp.concatenate(
        [
            first_half * cosine_table + second_half * sine_table,
            second_half * cosine_table - first_half * sine_table,
        ],
        axis=-1,
    )


def on_device(inputs, grad_context, gain, w_query, w_keyval):
    seq_length = inputs.shape[0]
    local_cols = inputs.shape[1]
    model_width = gain.shape[0]
    head_size = HD
    heads_here = HEADS_DEV
    group_cols = w_keyval.shape[1]
    query_cols = w_query.shape[1]
    tensor_count = lax.axis_size("tensor")
    keyval_total = group_cols * tensor_count
    kv_heads = KV_HEADS
    devices_per_group = tensor_count // kv_heads
    score_scale = head_size ** (-0.5)
    tensor_slot = lax.axis_index("tensor")
    gain_local = lax.dynamic_slice_in_dim(gain, tensor_slot * local_cols, local_cols, 0)
    split_cols = query_cols // 2
    engine_block = jnp.concatenate([w_query[:, :split_cols], w_keyval], axis=1)
    engine_full = lax.all_gather(engine_block, "dp", axis=0, tiled=True)
    ring_blocks_out, input_blocks = ring_gather(w_query[:, split_cols:], inputs, 6)
    ring_full = ring_blocks_out.reshape(-1, query_cols - split_cols)
    inputs_full = (
        input_blocks.transpose(1, 0, 2).reshape(seq_length, model_width).astype(jnp.float32)
    )
    row_sum = jnp.sum(inputs_full * inputs_full, axis=1, keepdims=True)
    inv_rms = lax.rsqrt(row_sum / model_width + 1e-05)
    unit_full = inputs_full * inv_rms
    normed_full = (unit_full * gain[None, :]).astype(jnp.bfloat16)
    unit_rows = inputs.astype(jnp.float32) * inv_rms
    engine_proj = jnp.dot(normed_full, engine_full, preferred_element_type=jnp.float32).astype(
        jnp.bfloat16
    )
    ring_proj = jnp.dot(normed_full, ring_full, preferred_element_type=jnp.float32).astype(
        jnp.bfloat16
    )
    query_proj = jnp.concatenate([engine_proj[:, :split_cols], ring_proj], axis=1)
    keyval_part = engine_proj[:, split_cols:]
    (keyval_blocks,) = exchange("tensor", [keyval_part], [False], 1)
    keyval_full = keyval_blocks.transpose(1, 0, 2).reshape(seq_length, keyval_total)
    group_slot = tensor_slot // devices_per_group
    key_block = lax.dynamic_slice_in_dim(keyval_full, group_slot * head_size, head_size, 1)
    value_block = lax.dynamic_slice_in_dim(
        keyval_full, (kv_heads + group_slot) * head_size, head_size, 1
    )
    cosine_table, sine_table = rope_tables(seq_length, head_size)
    cos_heads = cosine_table[:, None, :]
    sin_heads = sine_table[:, None, :]
    query_heads = query_proj.astype(jnp.float32).reshape(seq_length, heads_here, head_size)
    q_rot = rotate(query_heads, cos_heads, sin_heads).astype(jnp.bfloat16)
    k_rot = rotate(key_block.astype(jnp.float32), cosine_table, sine_table).astype(jnp.bfloat16)
    scores = (
        jnp.einsum("shd,td->hst", q_rot, k_rot, preferred_element_type=jnp.float32) * score_scale
    )
    causal = lax.broadcasted_iota(jnp.int32, (seq_length, seq_length), 0) >= lax.broadcasted_iota(
        jnp.int32, (seq_length, seq_length), 1
    )
    exponent = jnp.where(causal[None, :, :], jnp.exp(scores), 0.0)
    softmax_probs = exponent / jnp.sum(exponent, axis=2, keepdims=True)
    prob_weights = softmax_probs.astype(jnp.bfloat16)
    context = jnp.einsum(
        "hst,td->shd", prob_weights, value_block, preferred_element_type=jnp.float32
    ).astype(jnp.bfloat16)
    grad_ctx = grad_context.reshape(seq_length, heads_here, head_size)
    grad_probs = jnp.einsum(
        "shd,td->hst", grad_ctx, value_block, preferred_element_type=jnp.float32
    )
    row_delta = jnp.sum(grad_ctx.astype(jnp.float32) * context.astype(jnp.float32), axis=2).T[
        :, :, None
    ]
    grad_scores = (softmax_probs * (grad_probs - row_delta) * score_scale).astype(jnp.bfloat16)
    grad_qrot = jnp.einsum("hst,td->shd", grad_scores, k_rot, preferred_element_type=jnp.float32)
    grad_krot = jnp.einsum("hst,shd->td", grad_scores, q_rot, preferred_element_type=jnp.float32)
    grad_value = jnp.einsum(
        "hst,shd->td", prob_weights, grad_ctx, preferred_element_type=jnp.float32
    )
    grad_query = (
        unrotate(grad_qrot, cos_heads, sin_heads)
        .astype(jnp.bfloat16)
        .reshape(seq_length, heads_here * head_size)
    )
    grad_terms = jnp.zeros((seq_length, keyval_total), jnp.float32)
    grad_terms = lax.dynamic_update_slice_in_dim(
        grad_terms, unrotate(grad_krot, cosine_table, sine_table), group_slot * head_size, 1
    )
    grad_terms = lax.dynamic_update_slice_in_dim(
        grad_terms, grad_value, (kv_heads + group_slot) * head_size, 1
    )
    term_blocks = grad_terms.reshape(seq_length, tensor_count, group_cols).transpose(1, 0, 2)
    (keyval_terms,) = exchange("tensor", [term_blocks], [True], 2)
    grad_keyval = jnp.sum(keyval_terms, axis=0).astype(jnp.bfloat16)
    engine_blocks = engine_full.reshape(tensor_count, local_cols, split_cols + group_cols)
    ring_blocks = ring_full.reshape(tensor_count, local_cols, query_cols - split_cols)
    engine_grads = jnp.concatenate([grad_query[:, :split_cols], grad_keyval], axis=1)
    normed_terms = (
        jnp.einsum("rc,pkc->prk", engine_grads, engine_blocks, preferred_element_type=jnp.float32)
        + jnp.einsum(
            "rc,pkc->prk",
            grad_query[:, split_cols:],
            ring_blocks,
            preferred_element_type=jnp.float32,
        )
    ).astype(jnp.bfloat16)
    unit_blocks = unit_full.reshape(seq_length, tensor_count, local_cols).transpose(1, 0, 2)
    gain_blocks = gain.reshape(tensor_count, 1, local_cols)
    product_part = jnp.sum(
        normed_terms.astype(jnp.float32) * gain_blocks * unit_blocks, axis=(0, 2)
    ).reshape(1, seq_length)
    dp_count = lax.axis_size("dp")
    keyval_partials = jnp.einsum(
        "rk,rc->kc", normed_full, grad_keyval, preferred_element_type=jnp.float32
    ).reshape(model_width // 2, 2 * group_cols)
    keyval_sums = lax.psum_scatter(keyval_partials, "dp", scatter_dimension=0, tiled=True)
    normed_sums, product_parts = exchange(
        "tensor", [normed_terms, product_part], [True, False], 3
    )
    grad_normed = jnp.sum(normed_sums.astype(jnp.float32), axis=0)
    product_sum = jnp.sum(product_parts, axis=0).reshape(seq_length, 1)
    scaled_grad = grad_normed * gain_local
    grad_input = (inv_rms * (scaled_grad - unit_rows * (product_sum / model_width))).astype(
        jnp.bfloat16
    )
    gain_part = jnp.sum(grad_normed * unit_rows, axis=0).reshape(1, local_cols)
    (gain_parts,) = exchange("dp", [gain_part], [False], 4)
    grad_gain = jnp.sum(gain_parts, axis=(0, 1))
    keyval_weight_grad = keyval_sums.reshape(-1, group_cols)
    return (grad_input, grad_gain, keyval_weight_grad.astype(jnp.bfloat16))


def solution(mesh):
    in_specs = (P("dp", "tensor"), P("dp", "tensor"), P(), P("dp", "tensor"), P("dp", "tensor"))
    out_specs = (P("dp", "tensor"), P("tensor"), P("dp", "tensor"))
    return jax.shard_map(
        on_device, mesh=mesh, in_specs=in_specs, out_specs=out_specs, check_vma=False
    )
```

```python
import functools
import math

import jax
import jax.numpy as jnp
from jax import lax
from jax.experimental import pallas as pl
from jax.experimental.pallas import tpu as pltpu
from jax.sharding import PartitionSpec as P

MESH = pl.DeviceIdType.MESH


def exchange_kernel(axes, sizes, per_peer, *refs):
    count = len(per_peer)
    src_refs = refs[:count]
    out_refs = refs[count : 2 * count]
    send_sems, recv_sems = refs[2 * count :]
    barrier = pltpu.get_barrier_semaphore()
    waits = 0
    for axis in dict.fromkeys(axes):
        n = sizes[axes.index(axis)]
        me = lax.axis_index(axis)
        for step in range(1, n):
            peer = lax.rem(me + step, n)
            pl.semaphore_signal(barrier, inc=1, device_id={axis: peer}, device_id_type=MESH)
        waits += n - 1
    pl.semaphore_wait(barrier, waits)
    copies = []
    for index in range(count):
        axis, n = axes[index], sizes[index]
        me = lax.axis_index(axis)
        for step in range(1, n):
            peer = lax.rem(me + step, n)
            source = src_refs[index].at[peer] if per_peer[index] else src_refs[index]
            copy = pltpu.make_async_remote_copy(
                src_ref=source,
                dst_ref=out_refs[index].at[me],
                send_sem=send_sems.at[index, step],
                recv_sem=recv_sems.at[index, step],
                device_id={axis: peer},
                device_id_type=MESH,
            )
            copy.start()
            copies.append(copy)
    for index in range(count):
        me = lax.axis_index(axes[index])
        own = src_refs[index][me] if per_peer[index] else src_refs[index][...]
        out_refs[index][me] = own
    for copy in copies:
        copy.wait_send()
    for copy in copies:
        copy.wait_recv()


def exchange_multi(items, collective_id):
    axes = tuple(axis for axis, _, _ in items)
    sizes = tuple(lax.axis_size(axis) for axis in axes)
    blocks = [block for _, block, _ in items]
    per_peer = tuple(spread for _, _, spread in items)
    out_shapes = []
    sent = 0
    for n, block, spread in zip(sizes, blocks, per_peer):
        shape = block.shape[1:] if spread else block.shape
        out_shapes.append(jax.ShapeDtypeStruct((n,) + tuple(shape), block.dtype))
        sent += block.size * block.dtype.itemsize * (1 if spread else n)
    count = len(blocks)
    return pl.pallas_call(
        functools.partial(exchange_kernel, axes, sizes, per_peer),
        out_shape=tuple(out_shapes),
        in_specs=[pl.BlockSpec(memory_space=pltpu.VMEM)] * count,
        out_specs=tuple(pl.BlockSpec(memory_space=pltpu.VMEM) for _ in range(count)),
        scratch_shapes=[
            pltpu.SemaphoreType.DMA((count, max(sizes))),
            pltpu.SemaphoreType.DMA((count, max(sizes))),
        ],
        compiler_params=pltpu.CompilerParams(collective_id=collective_id, has_side_effects=True),
        cost_estimate=pl.CostEstimate(flops=0, bytes_accessed=2 * sent, transcendentals=0),
    )(*blocks)


def exchange(axis, blocks, per_peer, collective_id):
    return exchange_multi([(axis, b, s) for b, s in zip(blocks, per_peer)], collective_id)


def ring_gather_kernel(
    pair_count, ring_count, side_count, block_ref, side_ref, out_ref, side_out, send_sems, recv_sems, side_send, side_recv
):
    pair_slot = lax.axis_index("dp") // ring_count
    ring_slot = lax.axis_index("dp") % ring_count
    partner = (1 - pair_slot) * ring_count + ring_slot
    right = pair_slot * ring_count + lax.rem(ring_slot + 1, ring_count)
    left = pair_slot * ring_count + lax.rem(ring_slot + ring_count - 1, ring_count)
    me = pair_slot * ring_count + ring_slot
    side_me = lax.axis_index("tensor")
    barrier = pltpu.get_barrier_semaphore()
    for peer in (partner, right, left):
        pl.semaphore_signal(barrier, inc=1, device_id={"dp": peer}, device_id_type=MESH)
    for step in range(1, side_count):
        peer = lax.rem(side_me + step, side_count)
        pl.semaphore_signal(barrier, inc=1, device_id={"tensor": peer}, device_id_type=MESH)
    pl.semaphore_wait(barrier, 3 + side_count - 1)
    side_copies = []
    for step in range(1, side_count):
        peer = lax.rem(side_me + step, side_count)
        copy = pltpu.make_async_remote_copy(
            src_ref=side_ref,
            dst_ref=side_out.at[side_me],
            send_sem=side_send.at[step],
            recv_sem=side_recv.at[step],
            device_id={"tensor": peer},
            device_id_type=MESH,
        )
        copy.start()
        side_copies.append(copy)
    swap = pltpu.make_async_remote_copy(
        src_ref=block_ref,
        dst_ref=out_ref.at[me],
        send_sem=send_sems.at[2, 0, 0],
        recv_sem=recv_sems.at[2, 0, 0],
        device_id={"dp": partner},
        device_id_type=MESH,
    )
    swap.start()
    own = pltpu.make_async_copy(block_ref, out_ref.at[me], send_sems.at[2, 1, 0])
    own.start()
    side_out[side_me] = side_ref[...]
    own.wait()
    swap.wait_send()
    swap.wait_recv()
    right_steps = ring_count // 2
    left_steps = ring_count - 1 - right_steps
    sent = []

    def send(direction, step, target, origin):
        copies = []
        for member in range(pair_count):
            slot = member * ring_count + origin
            copy = pltpu.make_async_remote_copy(
                src_ref=out_ref.at[slot],
                dst_ref=out_ref.at[slot],
                send_sem=send_sems.at[direction, step, member],
                recv_sem=recv_sems.at[direction, step, member],
                device_id={"dp": target},
                device_id_type=MESH,
            )
            copy.start()
            copies.append(copy)
        sent.extend(copies)
        return copies

    right_copies = send(0, 0, right, ring_slot)
    left_copies = send(1, 0, left, ring_slot) if left_steps > 0 else []
    for step in range(1, right_steps):
        for copy in right_copies:
            copy.wait_recv()
        origin = lax.rem(ring_slot + ring_count - step, ring_count)
        right_copies = send(0, step, right, origin)
        if step < left_steps:
            for copy in left_copies:
                copy.wait_recv()
            origin = lax.rem(ring_slot + step, ring_count)
            left_copies = send(1, step, left, origin)
    for copy in right_copies + left_copies:
        copy.wait_recv()
    for copy in sent + side_copies:
        copy.wait_send()
    for copy in side_copies:
        copy.wait_recv()


def ring_gather(block, side, collective_id):
    count = lax.axis_size("dp")
    side_count = lax.axis_size("tensor")
    pair_count = 2
    ring_count = count // pair_count
    sent = count * block.size * block.dtype.itemsize + side_count * side.size * side.dtype.itemsize
    return pl.pallas_call(
        functools.partial(ring_gather_kernel, pair_count, ring_count, side_count),
        out_shape=(
            jax.ShapeDtypeStruct((count,) + block.shape, block.dtype),
            jax.ShapeDtypeStruct((side_count,) + side.shape, side.dtype),
        ),
        in_specs=[pl.BlockSpec(memory_space=pltpu.VMEM)] * 2,
        out_specs=(pl.BlockSpec(memory_space=pltpu.VMEM), pl.BlockSpec(memory_space=pltpu.VMEM)),
        scratch_shapes=[
            pltpu.SemaphoreType.DMA((3, ring_count, pair_count)),
            pltpu.SemaphoreType.DMA((3, ring_count, pair_count)),
            pltpu.SemaphoreType.DMA((side_count,)),
            pltpu.SemaphoreType.DMA((side_count,)),
        ],
        compiler_params=pltpu.CompilerParams(
            collective_id=collective_id, has_side_effects=True, vmem_limit_bytes=48 * 1024 * 1024
        ),
        cost_estimate=pl.CostEstimate(flops=0, bytes_accessed=2 * sent, transcendentals=0),
    )(block, side)

HD = 128
KV_HEADS = 4
HEADS_DEV = 4


def rope_tables(length, head_size):
    positions = lax.broadcasted_iota(jnp.int32, (length, head_size // 2), 0).astype(jnp.float32)
    index_half = lax.broadcasted_iota(jnp.int32, (length, head_size // 2), 1).astype(jnp.float32)
    frequency = jnp.exp(-(2.0 * index_half / head_size) * math.log(500000.0))
    angles = positions * frequency
    return (jnp.cos(angles), jnp.sin(angles))


def rotate(vectors, cosine_table, sine_table):
    half_size = vectors.shape[-1] // 2
    first_half = vectors[..., :half_size]
    second_half = vectors[..., half_size:]
    return jnp.concatenate(
        [
            first_half * cosine_table - second_half * sine_table,
            first_half * sine_table + second_half * cosine_table,
        ],
        axis=-1,
    )


def unrotate(vectors, cosine_table, sine_table):
    half_size = vectors.shape[-1] // 2
    first_half = vectors[..., :half_size]
    second_half = vectors[..., half_size:]
    return jnp.concatenate(
        [
            first_half * cosine_table + second_half * sine_table,
            second_half * cosine_table - first_half * sine_table,
        ],
        axis=-1,
    )


def on_device(inputs, grad_context, gain, w_query, w_keyval):
    seq_length = inputs.shape[0]
    local_cols = inputs.shape[1]
    model_width = gain.shape[0]
    head_size = HD
    heads_here = HEADS_DEV
    group_cols = w_keyval.shape[1]
    query_cols = w_query.shape[1]
    tensor_count = lax.axis_size("tensor")
    keyval_total = group_cols * tensor_count
    kv_heads = KV_HEADS
    devices_per_group = tensor_count // kv_heads
    score_scale = head_size ** (-0.5)
    tensor_slot = lax.axis_index("tensor")
    gain_local = lax.dynamic_slice_in_dim(gain, tensor_slot * local_cols, local_cols, 0)
    split_cols = query_cols // 2
    engine_block = jnp.concatenate([w_query[:, :split_cols], w_keyval], axis=1)
    engine_full = lax.all_gather(engine_block, "dp", axis=0, tiled=True)
    ring_blocks_out, input_blocks = ring_gather(w_query[:, split_cols:], inputs, 6)
    ring_full = ring_blocks_out.reshape(-1, query_cols - split_cols)
    inputs_full = (
        input_blocks.transpose(1, 0, 2).reshape(seq_length, model_width).astype(jnp.float32)
    )
    row_sum = jnp.sum(inputs_full * inputs_full, axis=1, keepdims=True)
    inv_rms = lax.rsqrt(row_sum / model_width + 1e-05)
    unit_full = inputs_full * inv_rms
    normed_full = (unit_full * gain[None, :]).astype(jnp.bfloat16)
    unit_rows = inputs.astype(jnp.float32) * inv_rms
    engine_proj = jnp.dot(normed_full, engine_full, preferred_element_type=jnp.float32).astype(
        jnp.bfloat16
    )
    ring_proj = jnp.dot(normed_full, ring_full, preferred_element_type=jnp.float32).astype(
        jnp.bfloat16
    )
    query_proj = jnp.concatenate([engine_proj[:, :split_cols], ring_proj], axis=1)
    keyval_part = engine_proj[:, split_cols:]
    (keyval_blocks,) = exchange("tensor", [keyval_part], [False], 1)
    keyval_full = keyval_blocks.transpose(1, 0, 2).reshape(seq_length, keyval_total)
    group_slot = tensor_slot // devices_per_group
    key_block = lax.dynamic_slice_in_dim(keyval_full, group_slot * head_size, head_size, 1)
    value_block = lax.dynamic_slice_in_dim(
        keyval_full, (kv_heads + group_slot) * head_size, head_size, 1
    )
    cosine_table, sine_table = rope_tables(seq_length, head_size)
    cos_heads = cosine_table[:, None, :]
    sin_heads = sine_table[:, None, :]
    query_heads = query_proj.astype(jnp.float32).reshape(seq_length, heads_here, head_size)
    q_rot = rotate(query_heads, cos_heads, sin_heads).astype(jnp.bfloat16)
    k_rot = rotate(key_block.astype(jnp.float32), cosine_table, sine_table).astype(jnp.bfloat16)
    scores = (
        jnp.einsum("shd,td->hst", q_rot, k_rot, preferred_element_type=jnp.float32) * score_scale
    )
    causal = lax.broadcasted_iota(jnp.int32, (seq_length, seq_length), 0) >= lax.broadcasted_iota(
        jnp.int32, (seq_length, seq_length), 1
    )
    exponent = jnp.where(causal[None, :, :], jnp.exp(scores), 0.0)
    softmax_probs = exponent / jnp.sum(exponent, axis=2, keepdims=True)
    prob_weights = softmax_probs.astype(jnp.bfloat16)
    context = jnp.einsum(
        "hst,td->shd", prob_weights, value_block, preferred_element_type=jnp.float32
    ).astype(jnp.bfloat16)
    grad_ctx = grad_context.reshape(seq_length, heads_here, head_size)
    grad_probs = jnp.einsum(
        "shd,td->hst", grad_ctx, value_block, preferred_element_type=jnp.float32
    )
    row_delta = jnp.sum(grad_ctx.astype(jnp.float32) * context.astype(jnp.float32), axis=2).T[
        :, :, None
    ]
    grad_scores = (softmax_probs * (grad_probs - row_delta) * score_scale).astype(jnp.bfloat16)
    grad_qrot = jnp.einsum("hst,td->shd", grad_scores, k_rot, preferred_element_type=jnp.float32)
    grad_krot = jnp.einsum("hst,shd->td", grad_scores, q_rot, preferred_element_type=jnp.float32)
    grad_value = jnp.einsum(
        "hst,shd->td", prob_weights, grad_ctx, preferred_element_type=jnp.float32
    )
    grad_query = (
        unrotate(grad_qrot, cos_heads, sin_heads)
        .astype(jnp.bfloat16)
        .reshape(seq_length, heads_here * head_size)
    )
    grad_terms = jnp.zeros((seq_length, keyval_total), jnp.float32)
    grad_terms = lax.dynamic_update_slice_in_dim(
        grad_terms, unrotate(grad_krot, cosine_table, sine_table), group_slot * head_size, 1
    )
    grad_terms = lax.dynamic_update_slice_in_dim(
        grad_terms, grad_value, (kv_heads + group_slot) * head_size, 1
    )
    term_blocks = grad_terms.reshape(seq_length, tensor_count, group_cols).transpose(1, 0, 2)
    (keyval_terms,) = exchange("tensor", [term_blocks], [True], 2)
    grad_keyval = jnp.sum(keyval_terms, axis=0).astype(jnp.bfloat16)
    engine_blocks = engine_full.reshape(tensor_count, local_cols, split_cols + group_cols)
    ring_blocks = ring_full.reshape(tensor_count, local_cols, query_cols - split_cols)
    engine_grads = jnp.concatenate([grad_query[:, :split_cols], grad_keyval], axis=1)
    normed_terms = (
        jnp.einsum("rc,pkc->prk", engine_grads, engine_blocks, preferred_element_type=jnp.float32)
        + jnp.einsum(
            "rc,pkc->prk",
            grad_query[:, split_cols:],
            ring_blocks,
            preferred_element_type=jnp.float32,
        )
    ).astype(jnp.bfloat16)
    unit_blocks = unit_full.reshape(seq_length, tensor_count, local_cols).transpose(1, 0, 2)
    gain_blocks = gain.reshape(tensor_count, 1, local_cols)
    product_part = jnp.sum(
        normed_terms.astype(jnp.float32) * gain_blocks * unit_blocks, axis=(0, 2)
    ).reshape(1, seq_length)
    dp_count = lax.axis_size("dp")
    keyval_partials = jnp.einsum(
        "rk,rc->kc", normed_full, grad_keyval, preferred_element_type=jnp.float32
    ).reshape(model_width // 2, 2 * group_cols).astype(jnp.bfloat16)
    keyval_sums = lax.psum_scatter(keyval_partials, "dp", scatter_dimension=0, tiled=True)
    normed_sums, product_parts = exchange(
        "tensor", [normed_terms, product_part], [True, False], 3
    )
    grad_normed = jnp.sum(normed_sums.astype(jnp.float32), axis=0)
    product_sum = jnp.sum(product_parts, axis=0).reshape(seq_length, 1)
    scaled_grad = grad_normed * gain_local
    grad_input = (inv_rms * (scaled_grad - unit_rows * (product_sum / model_width))).astype(
        jnp.bfloat16
    )
    gain_part = jnp.sum(grad_normed * unit_rows, axis=0).reshape(1, local_cols)
    (gain_parts,) = exchange("dp", [gain_part], [False], 4)
    grad_gain = jnp.sum(gain_parts, axis=(0, 1))
    keyval_weight_grad = keyval_sums.reshape(-1, group_cols)
    return (grad_input, grad_gain, keyval_weight_grad.astype(jnp.bfloat16))


def solution(mesh):
    in_specs = (P("dp", "tensor"), P("dp", "tensor"), P(), P("dp", "tensor"), P("dp", "tensor"))
    out_specs = (P("dp", "tensor"), P("tensor"), P("dp", "tensor"))
    return jax.shard_map(
        on_device, mesh=mesh, in_specs=in_specs, out_specs=out_specs, check_vma=False
    )
```

```python
import functools
import math

import jax
import jax.numpy as jnp
from jax import lax
from jax.experimental import pallas as pl
from jax.experimental.pallas import tpu as pltpu
from jax.sharding import PartitionSpec as P

MESH = pl.DeviceIdType.MESH


def exchange_kernel(axes, sizes, per_peer, *refs):
    count = len(per_peer)
    src_refs = refs[:count]
    out_refs = refs[count : 2 * count]
    send_sems, recv_sems = refs[2 * count :]
    barrier = pltpu.get_barrier_semaphore()
    waits = 0
    for axis in dict.fromkeys(axes):
        n = sizes[axes.index(axis)]
        me = lax.axis_index(axis)
        for step in range(1, n):
            peer = lax.rem(me + step, n)
            pl.semaphore_signal(barrier, inc=1, device_id={axis: peer}, device_id_type=MESH)
        waits += n - 1
    pl.semaphore_wait(barrier, waits)
    copies = []
    for index in range(count):
        axis, n = axes[index], sizes[index]
        me = lax.axis_index(axis)
        for step in range(1, n):
            peer = lax.rem(me + step, n)
            source = src_refs[index].at[peer] if per_peer[index] else src_refs[index]
            copy = pltpu.make_async_remote_copy(
                src_ref=source,
                dst_ref=out_refs[index].at[me],
                send_sem=send_sems.at[index, step],
                recv_sem=recv_sems.at[index, step],
                device_id={axis: peer},
                device_id_type=MESH,
            )
            copy.start()
            copies.append(copy)
    for index in range(count):
        me = lax.axis_index(axes[index])
        own = src_refs[index][me] if per_peer[index] else src_refs[index][...]
        out_refs[index][me] = own
    for copy in copies:
        copy.wait_send()
    for copy in copies:
        copy.wait_recv()


def exchange_multi(items, collective_id):
    axes = tuple(axis for axis, _, _ in items)
    sizes = tuple(lax.axis_size(axis) for axis in axes)
    blocks = [block for _, block, _ in items]
    per_peer = tuple(spread for _, _, spread in items)
    out_shapes = []
    sent = 0
    for n, block, spread in zip(sizes, blocks, per_peer):
        shape = block.shape[1:] if spread else block.shape
        out_shapes.append(jax.ShapeDtypeStruct((n,) + tuple(shape), block.dtype))
        sent += block.size * block.dtype.itemsize * (1 if spread else n)
    count = len(blocks)
    return pl.pallas_call(
        functools.partial(exchange_kernel, axes, sizes, per_peer),
        out_shape=tuple(out_shapes),
        in_specs=[pl.BlockSpec(memory_space=pltpu.VMEM)] * count,
        out_specs=tuple(pl.BlockSpec(memory_space=pltpu.VMEM) for _ in range(count)),
        scratch_shapes=[
            pltpu.SemaphoreType.DMA((count, max(sizes))),
            pltpu.SemaphoreType.DMA((count, max(sizes))),
        ],
        compiler_params=pltpu.CompilerParams(collective_id=collective_id, has_side_effects=True),
        cost_estimate=pl.CostEstimate(flops=0, bytes_accessed=2 * sent, transcendentals=0),
    )(*blocks)


def exchange(axis, blocks, per_peer, collective_id):
    return exchange_multi([(axis, b, s) for b, s in zip(blocks, per_peer)], collective_id)


def ring_gather_kernel(
    pair_count, ring_count, side_count, block_ref, side_ref, out_ref, side_out, send_sems, recv_sems, side_send, side_recv
):
    pair_slot = lax.axis_index("dp") // ring_count
    ring_slot = lax.axis_index("dp") % ring_count
    partner = (1 - pair_slot) * ring_count + ring_slot
    right = pair_slot * ring_count + lax.rem(ring_slot + 1, ring_count)
    left = pair_slot * ring_count + lax.rem(ring_slot + ring_count - 1, ring_count)
    me = pair_slot * ring_count + ring_slot
    side_me = lax.axis_index("tensor")
    barrier = pltpu.get_barrier_semaphore()
    for peer in (partner, right, left):
        pl.semaphore_signal(barrier, inc=1, device_id={"dp": peer}, device_id_type=MESH)
    for step in range(1, side_count):
        peer = lax.rem(side_me + step, side_count)
        pl.semaphore_signal(barrier, inc=1, device_id={"tensor": peer}, device_id_type=MESH)
    pl.semaphore_wait(barrier, 3 + side_count - 1)
    side_copies = []
    for step in range(1, side_count):
        peer = lax.rem(side_me + step, side_count)
        copy = pltpu.make_async_remote_copy(
            src_ref=side_ref,
            dst_ref=side_out.at[side_me],
            send_sem=side_send.at[step],
            recv_sem=side_recv.at[step],
            device_id={"tensor": peer},
            device_id_type=MESH,
        )
        copy.start()
        side_copies.append(copy)
    swap = pltpu.make_async_remote_copy(
        src_ref=block_ref,
        dst_ref=out_ref.at[me],
        send_sem=send_sems.at[2, 0, 0],
        recv_sem=recv_sems.at[2, 0, 0],
        device_id={"dp": partner},
        device_id_type=MESH,
    )
    swap.start()
    own = pltpu.make_async_copy(block_ref, out_ref.at[me], send_sems.at[2, 1, 0])
    own.start()
    side_out[side_me] = side_ref[...]
    own.wait()
    swap.wait_send()
    swap.wait_recv()
    right_steps = ring_count // 2
    left_steps = ring_count - 1 - right_steps
    sent = []

    def send(direction, step, target, origin):
        copies = []
        for member in range(pair_count):
            slot = member * ring_count + origin
            copy = pltpu.make_async_remote_copy(
                src_ref=out_ref.at[slot],
                dst_ref=out_ref.at[slot],
                send_sem=send_sems.at[direction, step, member],
                recv_sem=recv_sems.at[direction, step, member],
                device_id={"dp": target},
                device_id_type=MESH,
            )
            copy.start()
            copies.append(copy)
        sent.extend(copies)
        return copies

    right_copies = send(0, 0, right, ring_slot)
    left_copies = send(1, 0, left, ring_slot) if left_steps > 0 else []
    for step in range(1, right_steps):
        for copy in right_copies:
            copy.wait_recv()
        origin = lax.rem(ring_slot + ring_count - step, ring_count)
        right_copies = send(0, step, right, origin)
        if step < left_steps:
            for copy in left_copies:
                copy.wait_recv()
            origin = lax.rem(ring_slot + step, ring_count)
            left_copies = send(1, step, left, origin)
    for copy in right_copies + left_copies:
        copy.wait_recv()
    for copy in sent + side_copies:
        copy.wait_send()
    for copy in side_copies:
        copy.wait_recv()


def ring_gather(block, side, collective_id):
    count = lax.axis_size("dp")
    side_count = lax.axis_size("tensor")
    pair_count = 2
    ring_count = count // pair_count
    sent = count * block.size * block.dtype.itemsize + side_count * side.size * side.dtype.itemsize
    return pl.pallas_call(
        functools.partial(ring_gather_kernel, pair_count, ring_count, side_count),
        out_shape=(
            jax.ShapeDtypeStruct((count,) + block.shape, block.dtype),
            jax.ShapeDtypeStruct((side_count,) + side.shape, side.dtype),
        ),
        in_specs=[pl.BlockSpec(memory_space=pltpu.VMEM)] * 2,
        out_specs=(pl.BlockSpec(memory_space=pltpu.VMEM), pl.BlockSpec(memory_space=pltpu.VMEM)),
        scratch_shapes=[
            pltpu.SemaphoreType.DMA((3, ring_count, pair_count)),
            pltpu.SemaphoreType.DMA((3, ring_count, pair_count)),
            pltpu.SemaphoreType.DMA((side_count,)),
            pltpu.SemaphoreType.DMA((side_count,)),
        ],
        compiler_params=pltpu.CompilerParams(
            collective_id=collective_id, has_side_effects=True, vmem_limit_bytes=48 * 1024 * 1024
        ),
        cost_estimate=pl.CostEstimate(flops=0, bytes_accessed=2 * sent, transcendentals=0),
    )(block, side)

def pair_sum_kernel(ring_count, block_ref, out_ref, landing, sems):
    pair_slot = lax.axis_index("dp") // ring_count
    ring_slot = lax.axis_index("dp") % ring_count
    partner = (1 - pair_slot) * ring_count + ring_slot
    barrier = pltpu.get_barrier_semaphore()
    pl.semaphore_signal(barrier, inc=1, device_id={"dp": partner}, device_id_type=MESH)
    pl.semaphore_wait(barrier, 1)
    copy = pltpu.make_async_remote_copy(
        src_ref=block_ref.at[1 - pair_slot],
        dst_ref=landing,
        send_sem=sems.at[0],
        recv_sem=sems.at[1],
        device_id={"dp": partner},
        device_id_type=MESH,
    )
    copy.start()
    copy.wait_send()
    copy.wait_recv()
    out_ref[...] = block_ref[pair_slot] + landing[...]


def pair_sum(blocks, ring_count, collective_id):
    return pl.pallas_call(
        functools.partial(pair_sum_kernel, ring_count),
        out_shape=jax.ShapeDtypeStruct(blocks.shape[1:], blocks.dtype),
        in_specs=[pl.BlockSpec(memory_space=pltpu.VMEM)],
        out_specs=pl.BlockSpec(memory_space=pltpu.VMEM),
        scratch_shapes=[pltpu.VMEM(blocks.shape[1:], blocks.dtype), pltpu.SemaphoreType.DMA((2,))],
        compiler_params=pltpu.CompilerParams(collective_id=collective_id, has_side_effects=True),
        cost_estimate=pl.CostEstimate(
            flops=0, bytes_accessed=3 * blocks.size * blocks.dtype.itemsize, transcendentals=0
        ),
    )(blocks)


HD = 128
KV_HEADS = 4
HEADS_DEV = 4


def rope_tables(length, head_size):
    positions = lax.broadcasted_iota(jnp.int32, (length, head_size // 2), 0).astype(jnp.float32)
    index_half = lax.broadcasted_iota(jnp.int32, (length, head_size // 2), 1).astype(jnp.float32)
    frequency = jnp.exp(-(2.0 * index_half / head_size) * math.log(500000.0))
    angles = positions * frequency
    return (jnp.cos(angles), jnp.sin(angles))


def rotate(vectors, cosine_table, sine_table):
    half_size = vectors.shape[-1] // 2
    first_half = vectors[..., :half_size]
    second_half = vectors[..., half_size:]
    return jnp.concatenate(
        [
            first_half * cosine_table - second_half * sine_table,
            first_half * sine_table + second_half * cosine_table,
        ],
        axis=-1,
    )


def unrotate(vectors, cosine_table, sine_table):
    half_size = vectors.shape[-1] // 2
    first_half = vectors[..., :half_size]
    second_half = vectors[..., half_size:]
    return jnp.concatenate(
        [
            first_half * cosine_table + second_half * sine_table,
            second_half * cosine_table - first_half * sine_table,
        ],
        axis=-1,
    )


def on_device(inputs, grad_context, gain, w_query, w_keyval):
    seq_length = inputs.shape[0]
    local_cols = inputs.shape[1]
    model_width = gain.shape[0]
    head_size = HD
    heads_here = HEADS_DEV
    group_cols = w_keyval.shape[1]
    query_cols = w_query.shape[1]
    tensor_count = lax.axis_size("tensor")
    keyval_total = group_cols * tensor_count
    kv_heads = KV_HEADS
    devices_per_group = tensor_count // kv_heads
    score_scale = head_size ** (-0.5)
    tensor_slot = lax.axis_index("tensor")
    gain_local = lax.dynamic_slice_in_dim(gain, tensor_slot * local_cols, local_cols, 0)
    split_cols = query_cols // 2
    engine_block = jnp.concatenate([w_query[:, :split_cols], w_keyval], axis=1)
    engine_full = lax.all_gather(engine_block, "dp", axis=0, tiled=True)
    ring_blocks_out, input_blocks = ring_gather(w_query[:, split_cols:], inputs, 6)
    ring_full = ring_blocks_out.reshape(-1, query_cols - split_cols)
    inputs_full = (
        input_blocks.transpose(1, 0, 2).reshape(seq_length, model_width).astype(jnp.float32)
    )
    row_sum = jnp.sum(inputs_full * inputs_full, axis=1, keepdims=True)
    inv_rms = lax.rsqrt(row_sum / model_width + 1e-05)
    unit_full = inputs_full * inv_rms
    normed_full = (unit_full * gain[None, :]).astype(jnp.bfloat16)
    unit_rows = inputs.astype(jnp.float32) * inv_rms
    engine_proj = jnp.dot(normed_full, engine_full, preferred_element_type=jnp.float32).astype(
        jnp.bfloat16
    )
    ring_proj = jnp.dot(normed_full, ring_full, preferred_element_type=jnp.float32).astype(
        jnp.bfloat16
    )
    query_proj = jnp.concatenate([engine_proj[:, :split_cols], ring_proj], axis=1)
    keyval_part = engine_proj[:, split_cols:]
    (keyval_blocks,) = exchange("tensor", [keyval_part], [False], 1)
    keyval_full = keyval_blocks.transpose(1, 0, 2).reshape(seq_length, keyval_total)
    group_slot = tensor_slot // devices_per_group
    key_block = lax.dynamic_slice_in_dim(keyval_full, group_slot * head_size, head_size, 1)
    value_block = lax.dynamic_slice_in_dim(
        keyval_full, (kv_heads + group_slot) * head_size, head_size, 1
    )
    cosine_table, sine_table = rope_tables(seq_length, head_size)
    cos_heads = cosine_table[:, None, :]
    sin_heads = sine_table[:, None, :]
    query_heads = query_proj.astype(jnp.float32).reshape(seq_length, heads_here, head_size)
    q_rot = rotate(query_heads, cos_heads, sin_heads).astype(jnp.bfloat16)
    k_rot = rotate(key_block.astype(jnp.float32), cosine_table, sine_table).astype(jnp.bfloat16)
    scores = (
        jnp.einsum("shd,td->hst", q_rot, k_rot, preferred_element_type=jnp.float32) * score_scale
    )
    causal = lax.broadcasted_iota(jnp.int32, (seq_length, seq_length), 0) >= lax.broadcasted_iota(
        jnp.int32, (seq_length, seq_length), 1
    )
    exponent = jnp.where(causal[None, :, :], jnp.exp(scores), 0.0)
    softmax_probs = exponent / jnp.sum(exponent, axis=2, keepdims=True)
    prob_weights = softmax_probs.astype(jnp.bfloat16)
    context = jnp.einsum(
        "hst,td->shd", prob_weights, value_block, preferred_element_type=jnp.float32
    ).astype(jnp.bfloat16)
    grad_ctx = grad_context.reshape(seq_length, heads_here, head_size)
    grad_probs = jnp.einsum(
        "shd,td->hst", grad_ctx, value_block, preferred_element_type=jnp.float32
    )
    row_delta = jnp.sum(grad_ctx.astype(jnp.float32) * context.astype(jnp.float32), axis=2).T[
        :, :, None
    ]
    grad_scores = (softmax_probs * (grad_probs - row_delta) * score_scale).astype(jnp.bfloat16)
    grad_qrot = jnp.einsum("hst,td->shd", grad_scores, k_rot, preferred_element_type=jnp.float32)
    grad_krot = jnp.einsum("hst,shd->td", grad_scores, q_rot, preferred_element_type=jnp.float32)
    grad_value = jnp.einsum(
        "hst,shd->td", prob_weights, grad_ctx, preferred_element_type=jnp.float32
    )
    grad_query = (
        unrotate(grad_qrot, cos_heads, sin_heads)
        .astype(jnp.bfloat16)
        .reshape(seq_length, heads_here * head_size)
    )
    grad_terms = jnp.zeros((seq_length, keyval_total), jnp.float32)
    grad_terms = lax.dynamic_update_slice_in_dim(
        grad_terms, unrotate(grad_krot, cosine_table, sine_table), group_slot * head_size, 1
    )
    grad_terms = lax.dynamic_update_slice_in_dim(
        grad_terms, grad_value, (kv_heads + group_slot) * head_size, 1
    )
    term_blocks = grad_terms.reshape(seq_length, tensor_count, group_cols).transpose(1, 0, 2)
    (keyval_terms,) = exchange("tensor", [term_blocks], [True], 2)
    grad_keyval = jnp.sum(keyval_terms, axis=0).astype(jnp.bfloat16)
    engine_blocks = engine_full.reshape(tensor_count, local_cols, split_cols + group_cols)
    ring_blocks = ring_full.reshape(tensor_count, local_cols, query_cols - split_cols)
    engine_grads = jnp.concatenate([grad_query[:, :split_cols], grad_keyval], axis=1)
    normed_terms = (
        jnp.einsum("rc,pkc->prk", engine_grads, engine_blocks, preferred_element_type=jnp.float32)
        + jnp.einsum(
            "rc,pkc->prk",
            grad_query[:, split_cols:],
            ring_blocks,
            preferred_element_type=jnp.float32,
        )
    ).astype(jnp.bfloat16)
    unit_blocks = unit_full.reshape(seq_length, tensor_count, local_cols).transpose(1, 0, 2)
    gain_blocks = gain.reshape(tensor_count, 1, local_cols)
    product_part = jnp.sum(
        normed_terms.astype(jnp.float32) * gain_blocks * unit_blocks, axis=(0, 2)
    ).reshape(1, seq_length)
    dp_count = lax.axis_size("dp")
    pair_count = 2
    ring_count = dp_count // pair_count
    keyval_partials = (
        jnp.einsum("rk,rc->kc", normed_full, grad_keyval, preferred_element_type=jnp.float32)
        .reshape(pair_count, ring_count, -1, group_cols)
        .transpose(1, 0, 2, 3)
        .reshape(model_width // 2, 2 * group_cols)
    )
    ring_groups = [
        [pair * ring_count + slot for slot in range(ring_count)] for pair in range(pair_count)
    ]
    ring_sums = lax.psum_scatter(
        keyval_partials, "dp", scatter_dimension=0, tiled=True, axis_index_groups=ring_groups
    )
    normed_sums, product_parts = exchange(
        "tensor", [normed_terms, product_part], [True, False], 3
    )
    grad_normed = jnp.sum(normed_sums.astype(jnp.float32), axis=0)
    product_sum = jnp.sum(product_parts, axis=0).reshape(seq_length, 1)
    scaled_grad = grad_normed * gain_local
    grad_input = (inv_rms * (scaled_grad - unit_rows * (product_sum / model_width))).astype(
        jnp.bfloat16
    )
    gain_part = jnp.sum(grad_normed * unit_rows, axis=0).reshape(1, local_cols)
    (gain_parts,) = exchange("dp", [gain_part], [False], 4)
    grad_gain = jnp.sum(gain_parts, axis=(0, 1))
    lane_rows = ring_sums.size // (pair_count * 128)
    keyval_sums = pair_sum(ring_sums.reshape(pair_count, lane_rows, 128), ring_count, 7)
    keyval_weight_grad = keyval_sums.reshape(-1, group_cols)
    return (grad_input, grad_gain, keyval_weight_grad.astype(jnp.bfloat16))


def solution(mesh):
    in_specs = (P("dp", "tensor"), P("dp", "tensor"), P(), P("dp", "tensor"), P("dp", "tensor"))
    out_specs = (P("dp", "tensor"), P("tensor"), P("dp", "tensor"))
    return jax.shard_map(
        on_device, mesh=mesh, in_specs=in_specs, out_specs=out_specs, check_vma=False
    )
```

```python
import functools
import math

import jax
import jax.numpy as jnp
from jax import lax
from jax.experimental import pallas as pl
from jax.experimental.pallas import tpu as pltpu
from jax.sharding import PartitionSpec as P

MESH = pl.DeviceIdType.MESH


def exchange_kernel(axes, sizes, per_peer, *refs):
    count = len(per_peer)
    src_refs = refs[:count]
    out_refs = refs[count : 2 * count]
    send_sems, recv_sems = refs[2 * count :]
    barrier = pltpu.get_barrier_semaphore()
    waits = 0
    for axis in dict.fromkeys(axes):
        n = sizes[axes.index(axis)]
        me = lax.axis_index(axis)
        for step in range(1, n):
            peer = lax.rem(me + step, n)
            pl.semaphore_signal(barrier, inc=1, device_id={axis: peer}, device_id_type=MESH)
        waits += n - 1
    pl.semaphore_wait(barrier, waits)
    copies = []
    for index in range(count):
        axis, n = axes[index], sizes[index]
        me = lax.axis_index(axis)
        for step in range(1, n):
            peer = lax.rem(me + step, n)
            source = src_refs[index].at[peer] if per_peer[index] else src_refs[index]
            copy = pltpu.make_async_remote_copy(
                src_ref=source,
                dst_ref=out_refs[index].at[me],
                send_sem=send_sems.at[index, step],
                recv_sem=recv_sems.at[index, step],
                device_id={axis: peer},
                device_id_type=MESH,
            )
            copy.start()
            copies.append(copy)
    for index in range(count):
        me = lax.axis_index(axes[index])
        own = src_refs[index][me] if per_peer[index] else src_refs[index][...]
        out_refs[index][me] = own
    for copy in copies:
        copy.wait_send()
    for copy in copies:
        copy.wait_recv()


def exchange_multi(items, collective_id):
    axes = tuple(axis for axis, _, _ in items)
    sizes = tuple(lax.axis_size(axis) for axis in axes)
    blocks = [block for _, block, _ in items]
    per_peer = tuple(spread for _, _, spread in items)
    out_shapes = []
    sent = 0
    for n, block, spread in zip(sizes, blocks, per_peer):
        shape = block.shape[1:] if spread else block.shape
        out_shapes.append(jax.ShapeDtypeStruct((n,) + tuple(shape), block.dtype))
        sent += block.size * block.dtype.itemsize * (1 if spread else n)
    count = len(blocks)
    return pl.pallas_call(
        functools.partial(exchange_kernel, axes, sizes, per_peer),
        out_shape=tuple(out_shapes),
        in_specs=[pl.BlockSpec(memory_space=pltpu.VMEM)] * count,
        out_specs=tuple(pl.BlockSpec(memory_space=pltpu.VMEM) for _ in range(count)),
        scratch_shapes=[
            pltpu.SemaphoreType.DMA((count, max(sizes))),
            pltpu.SemaphoreType.DMA((count, max(sizes))),
        ],
        compiler_params=pltpu.CompilerParams(collective_id=collective_id, has_side_effects=True),
        cost_estimate=pl.CostEstimate(flops=0, bytes_accessed=2 * sent, transcendentals=0),
    )(*blocks)


def exchange(axis, blocks, per_peer, collective_id):
    return exchange_multi([(axis, b, s) for b, s in zip(blocks, per_peer)], collective_id)


def ring_gather_kernel(
    pair_count, ring_count, side_count, block_ref, side_ref, out_ref, side_out, send_sems, recv_sems, side_send, side_recv
):
    pair_slot = lax.axis_index("dp") // ring_count
    ring_slot = lax.axis_index("dp") % ring_count
    partner = (1 - pair_slot) * ring_count + ring_slot
    right = pair_slot * ring_count + lax.rem(ring_slot + 1, ring_count)
    left = pair_slot * ring_count + lax.rem(ring_slot + ring_count - 1, ring_count)
    me = pair_slot * ring_count + ring_slot
    side_me = lax.axis_index("tensor")
    barrier = pltpu.get_barrier_semaphore()
    for peer in (partner, right, left):
        pl.semaphore_signal(barrier, inc=1, device_id={"dp": peer}, device_id_type=MESH)
    for step in range(1, side_count):
        peer = lax.rem(side_me + step, side_count)
        pl.semaphore_signal(barrier, inc=1, device_id={"tensor": peer}, device_id_type=MESH)
    pl.semaphore_wait(barrier, 3 + side_count - 1)
    side_copies = []
    for step in range(1, side_count):
        peer = lax.rem(side_me + step, side_count)
        copy = pltpu.make_async_remote_copy(
            src_ref=side_ref,
            dst_ref=side_out.at[side_me],
            send_sem=side_send.at[step],
            recv_sem=side_recv.at[step],
            device_id={"tensor": peer},
            device_id_type=MESH,
        )
        copy.start()
        side_copies.append(copy)
    swap = pltpu.make_async_remote_copy(
        src_ref=block_ref,
        dst_ref=out_ref.at[me],
        send_sem=send_sems.at[2, 0, 0],
        recv_sem=recv_sems.at[2, 0, 0],
        device_id={"dp": partner},
        device_id_type=MESH,
    )
    swap.start()
    own = pltpu.make_async_copy(block_ref, out_ref.at[me], send_sems.at[2, 1, 0])
    own.start()
    side_out[side_me] = side_ref[...]
    own.wait()
    swap.wait_send()
    swap.wait_recv()
    right_steps = ring_count // 2
    left_steps = ring_count - 1 - right_steps
    sent = []

    def send(direction, step, target, origin):
        copies = []
        for member in range(pair_count):
            slot = member * ring_count + origin
            copy = pltpu.make_async_remote_copy(
                src_ref=out_ref.at[slot],
                dst_ref=out_ref.at[slot],
                send_sem=send_sems.at[direction, step, member],
                recv_sem=recv_sems.at[direction, step, member],
                device_id={"dp": target},
                device_id_type=MESH,
            )
            copy.start()
            copies.append(copy)
        sent.extend(copies)
        return copies

    right_copies = send(0, 0, right, ring_slot)
    left_copies = send(1, 0, left, ring_slot) if left_steps > 0 else []
    for step in range(1, right_steps):
        for copy in right_copies:
            copy.wait_recv()
        origin = lax.rem(ring_slot + ring_count - step, ring_count)
        right_copies = send(0, step, right, origin)
        if step < left_steps:
            for copy in left_copies:
                copy.wait_recv()
            origin = lax.rem(ring_slot + step, ring_count)
            left_copies = send(1, step, left, origin)
    for copy in right_copies + left_copies:
        copy.wait_recv()
    for copy in sent + side_copies:
        copy.wait_send()
    for copy in side_copies:
        copy.wait_recv()


def ring_gather(block, side, collective_id):
    count = lax.axis_size("dp")
    side_count = lax.axis_size("tensor")
    pair_count = 2
    ring_count = count // pair_count
    sent = count * block.size * block.dtype.itemsize + side_count * side.size * side.dtype.itemsize
    return pl.pallas_call(
        functools.partial(ring_gather_kernel, pair_count, ring_count, side_count),
        out_shape=(
            jax.ShapeDtypeStruct((count,) + block.shape, block.dtype),
            jax.ShapeDtypeStruct((side_count,) + side.shape, side.dtype),
        ),
        in_specs=[pl.BlockSpec(memory_space=pltpu.VMEM)] * 2,
        out_specs=(pl.BlockSpec(memory_space=pltpu.VMEM), pl.BlockSpec(memory_space=pltpu.VMEM)),
        scratch_shapes=[
            pltpu.SemaphoreType.DMA((3, ring_count, pair_count)),
            pltpu.SemaphoreType.DMA((3, ring_count, pair_count)),
            pltpu.SemaphoreType.DMA((side_count,)),
            pltpu.SemaphoreType.DMA((side_count,)),
        ],
        compiler_params=pltpu.CompilerParams(
            collective_id=collective_id, has_side_effects=True, vmem_limit_bytes=48 * 1024 * 1024
        ),
        cost_estimate=pl.CostEstimate(flops=0, bytes_accessed=2 * sent, transcendentals=0),
    )(block, side)

def pair_sum_kernel(ring_count, block_ref, out_ref, landing, sems):
    pair_slot = lax.axis_index("dp") // ring_count
    ring_slot = lax.axis_index("dp") % ring_count
    partner = (1 - pair_slot) * ring_count + ring_slot
    barrier = pltpu.get_barrier_semaphore()
    pl.semaphore_signal(barrier, inc=1, device_id={"dp": partner}, device_id_type=MESH)
    pl.semaphore_wait(barrier, 1)
    copy = pltpu.make_async_remote_copy(
        src_ref=block_ref.at[1 - pair_slot],
        dst_ref=landing,
        send_sem=sems.at[0],
        recv_sem=sems.at[1],
        device_id={"dp": partner},
        device_id_type=MESH,
    )
    copy.start()
    copy.wait_send()
    copy.wait_recv()
    out_ref[...] = block_ref[pair_slot] + landing[...]


def pair_sum(blocks, ring_count, collective_id):
    return pl.pallas_call(
        functools.partial(pair_sum_kernel, ring_count),
        out_shape=jax.ShapeDtypeStruct(blocks.shape[1:], blocks.dtype),
        in_specs=[pl.BlockSpec(memory_space=pltpu.VMEM)],
        out_specs=pl.BlockSpec(memory_space=pltpu.VMEM),
        scratch_shapes=[pltpu.VMEM(blocks.shape[1:], blocks.dtype), pltpu.SemaphoreType.DMA((2,))],
        compiler_params=pltpu.CompilerParams(collective_id=collective_id, has_side_effects=True),
        cost_estimate=pl.CostEstimate(
            flops=0, bytes_accessed=3 * blocks.size * blocks.dtype.itemsize, transcendentals=0
        ),
    )(blocks)


HD = 128
KV_HEADS = 4
HEADS_DEV = 4


def rope_tables(length, head_size):
    positions = lax.broadcasted_iota(jnp.int32, (length, head_size // 2), 0).astype(jnp.float32)
    index_half = lax.broadcasted_iota(jnp.int32, (length, head_size // 2), 1).astype(jnp.float32)
    frequency = jnp.exp(-(2.0 * index_half / head_size) * math.log(500000.0))
    angles = positions * frequency
    return (jnp.cos(angles), jnp.sin(angles))


def rotate(vectors, cosine_table, sine_table):
    half_size = vectors.shape[-1] // 2
    first_half = vectors[..., :half_size]
    second_half = vectors[..., half_size:]
    return jnp.concatenate(
        [
            first_half * cosine_table - second_half * sine_table,
            first_half * sine_table + second_half * cosine_table,
        ],
        axis=-1,
    )


def unrotate(vectors, cosine_table, sine_table):
    half_size = vectors.shape[-1] // 2
    first_half = vectors[..., :half_size]
    second_half = vectors[..., half_size:]
    return jnp.concatenate(
        [
            first_half * cosine_table + second_half * sine_table,
            second_half * cosine_table - first_half * sine_table,
        ],
        axis=-1,
    )


def on_device(inputs, grad_context, gain, w_query, w_keyval):
    seq_length = inputs.shape[0]
    local_cols = inputs.shape[1]
    model_width = gain.shape[0]
    head_size = HD
    heads_here = HEADS_DEV
    group_cols = w_keyval.shape[1]
    query_cols = w_query.shape[1]
    tensor_count = lax.axis_size("tensor")
    keyval_total = group_cols * tensor_count
    kv_heads = KV_HEADS
    devices_per_group = tensor_count // kv_heads
    score_scale = head_size ** (-0.5)
    tensor_slot = lax.axis_index("tensor")
    gain_local = lax.dynamic_slice_in_dim(gain, tensor_slot * local_cols, local_cols, 0)
    split_cols = query_cols // 2
    engine_block = jnp.concatenate([w_query[:, :split_cols], w_keyval], axis=1)
    engine_full = lax.all_gather(engine_block, "dp", axis=0, tiled=True)
    ring_blocks_out, input_blocks = ring_gather(w_query[:, split_cols:], inputs, 6)
    ring_full = ring_blocks_out.reshape(-1, query_cols - split_cols)
    input_values = input_blocks.astype(jnp.float32)
    row_sum = jnp.sum(input_values * input_values, axis=(0, 2)).reshape(seq_length, 1)
    inv_rms = lax.rsqrt(row_sum / model_width + 1e-05)
    gain_blocks = gain.reshape(tensor_count, 1, local_cols)
    unit_blocks = input_values * inv_rms[None, :, :]
    normed_blocks = (unit_blocks * gain_blocks).astype(jnp.bfloat16)
    normed_full = normed_blocks.transpose(1, 0, 2).reshape(seq_length, model_width)
    unit_rows = inputs.astype(jnp.float32) * inv_rms
    engine_proj = jnp.dot(normed_full, engine_full, preferred_element_type=jnp.float32).astype(
        jnp.bfloat16
    )
    ring_proj = jnp.dot(normed_full, ring_full, preferred_element_type=jnp.float32).astype(
        jnp.bfloat16
    )
    query_proj = jnp.concatenate([engine_proj[:, :split_cols], ring_proj], axis=1)
    keyval_part = engine_proj[:, split_cols:]
    (keyval_blocks,) = exchange("tensor", [keyval_part], [False], 1)
    keyval_full = keyval_blocks.transpose(1, 0, 2).reshape(seq_length, keyval_total)
    group_slot = tensor_slot // devices_per_group
    key_block = lax.dynamic_slice_in_dim(keyval_full, group_slot * head_size, head_size, 1)
    value_block = lax.dynamic_slice_in_dim(
        keyval_full, (kv_heads + group_slot) * head_size, head_size, 1
    )
    cosine_table, sine_table = rope_tables(seq_length, head_size)
    cos_heads = cosine_table[:, None, :]
    sin_heads = sine_table[:, None, :]
    query_heads = query_proj.astype(jnp.float32).reshape(seq_length, heads_here, head_size)
    q_rot = rotate(query_heads, cos_heads, sin_heads).astype(jnp.bfloat16)
    k_rot = rotate(key_block.astype(jnp.float32), cosine_table, sine_table).astype(jnp.bfloat16)
    scores = (
        jnp.einsum("shd,td->hst", q_rot, k_rot, preferred_element_type=jnp.float32) * score_scale
    )
    causal = lax.broadcasted_iota(jnp.int32, (seq_length, seq_length), 0) >= lax.broadcasted_iota(
        jnp.int32, (seq_length, seq_length), 1
    )
    exponent = jnp.where(causal[None, :, :], jnp.exp(scores), 0.0)
    softmax_probs = exponent / jnp.sum(exponent, axis=2, keepdims=True)
    prob_weights = softmax_probs.astype(jnp.bfloat16)
    context = jnp.einsum(
        "hst,td->shd", prob_weights, value_block, preferred_element_type=jnp.float32
    ).astype(jnp.bfloat16)
    grad_ctx = grad_context.reshape(seq_length, heads_here, head_size)
    grad_probs = jnp.einsum(
        "shd,td->hst", grad_ctx, value_block, preferred_element_type=jnp.float32
    )
    row_delta = jnp.sum(grad_ctx.astype(jnp.float32) * context.astype(jnp.float32), axis=2).T[
        :, :, None
    ]
    grad_scores = (softmax_probs * (grad_probs - row_delta) * score_scale).astype(jnp.bfloat16)
    grad_qrot = jnp.einsum("hst,td->shd", grad_scores, k_rot, preferred_element_type=jnp.float32)
    grad_krot = jnp.einsum("hst,shd->td", grad_scores, q_rot, preferred_element_type=jnp.float32)
    grad_value = jnp.einsum(
        "hst,shd->td", prob_weights, grad_ctx, preferred_element_type=jnp.float32
    )
    grad_query = (
        unrotate(grad_qrot, cos_heads, sin_heads)
        .astype(jnp.bfloat16)
        .reshape(seq_length, heads_here * head_size)
    )
    grad_terms = jnp.zeros((seq_length, keyval_total), jnp.float32)
    grad_terms = lax.dynamic_update_slice_in_dim(
        grad_terms, unrotate(grad_krot, cosine_table, sine_table), group_slot * head_size, 1
    )
    grad_terms = lax.dynamic_update_slice_in_dim(
        grad_terms, grad_value, (kv_heads + group_slot) * head_size, 1
    )
    term_blocks = grad_terms.reshape(seq_length, tensor_count, group_cols).transpose(1, 0, 2)
    (keyval_terms,) = exchange("tensor", [term_blocks], [True], 2)
    grad_keyval = jnp.sum(keyval_terms, axis=0).astype(jnp.bfloat16)
    engine_blocks = engine_full.reshape(tensor_count, local_cols, split_cols + group_cols)
    ring_blocks = ring_full.reshape(tensor_count, local_cols, query_cols - split_cols)
    engine_grads = jnp.concatenate([grad_query[:, :split_cols], grad_keyval], axis=1)
    normed_terms = (
        jnp.einsum("rc,pkc->prk", engine_grads, engine_blocks, preferred_element_type=jnp.float32)
        + jnp.einsum(
            "rc,pkc->prk",
            grad_query[:, split_cols:],
            ring_blocks,
            preferred_element_type=jnp.float32,
        )
    ).astype(jnp.bfloat16)
    product_part = jnp.sum(
        normed_terms.astype(jnp.float32) * gain_blocks * unit_blocks, axis=(0, 2)
    ).reshape(1, seq_length)
    dp_count = lax.axis_size("dp")
    pair_count = 2
    ring_count = dp_count // pair_count
    keyval_partials = (
        jnp.einsum("prk,rc->pkc", normed_blocks, grad_keyval, preferred_element_type=jnp.float32)
        .reshape(pair_count, ring_count, -1, group_cols)
        .transpose(1, 0, 2, 3)
        .reshape(model_width // 2, 2 * group_cols)
    )
    ring_groups = [
        [pair * ring_count + slot for slot in range(ring_count)] for pair in range(pair_count)
    ]
    ring_sums = lax.psum_scatter(
        keyval_partials, "dp", scatter_dimension=0, tiled=True, axis_index_groups=ring_groups
    )
    normed_sums, product_parts = exchange(
        "tensor", [normed_terms, product_part], [True, False], 3
    )
    grad_normed = jnp.sum(normed_sums.astype(jnp.float32), axis=0)
    product_sum = jnp.sum(product_parts, axis=0).reshape(seq_length, 1)
    scaled_grad = grad_normed * gain_local
    grad_input = (inv_rms * (scaled_grad - unit_rows * (product_sum / model_width))).astype(
        jnp.bfloat16
    )
    gain_part = jnp.sum(grad_normed * unit_rows, axis=0).reshape(1, local_cols)
    (gain_parts,) = exchange("dp", [gain_part], [False], 4)
    grad_gain = jnp.sum(gain_parts, axis=(0, 1))
    lane_rows = ring_sums.size // (pair_count * 128)
    keyval_sums = pair_sum(ring_sums.reshape(pair_count, lane_rows, 128), ring_count, 7)
    keyval_weight_grad = keyval_sums.reshape(-1, group_cols)
    return (grad_input, grad_gain, keyval_weight_grad.astype(jnp.bfloat16))


def solution(mesh):
    in_specs = (P("dp", "tensor"), P("dp", "tensor"), P(), P("dp", "tensor"), P("dp", "tensor"))
    out_specs = (P("dp", "tensor"), P("tensor"), P("dp", "tensor"))
    return jax.shard_map(
        on_device, mesh=mesh, in_specs=in_specs, out_specs=out_specs, check_vma=False
    )
```

```python
import functools
import math

import jax
import jax.numpy as jnp
from jax import lax
from jax.experimental import pallas as pl
from jax.experimental.pallas import tpu as pltpu
from jax.sharding import PartitionSpec as P

MESH = pl.DeviceIdType.MESH


def exchange_kernel(axes, sizes, per_peer, *refs):
    count = len(per_peer)
    src_refs = refs[:count]
    out_refs = refs[count : 2 * count]
    send_sems, recv_sems = refs[2 * count :]
    barrier = pltpu.get_barrier_semaphore()
    waits = 0
    for axis in dict.fromkeys(axes):
        n = sizes[axes.index(axis)]
        me = lax.axis_index(axis)
        for step in range(1, n):
            peer = lax.rem(me + step, n)
            pl.semaphore_signal(barrier, inc=1, device_id={axis: peer}, device_id_type=MESH)
        waits += n - 1
    pl.semaphore_wait(barrier, waits)
    copies = []
    for index in range(count):
        axis, n = axes[index], sizes[index]
        me = lax.axis_index(axis)
        for step in range(1, n):
            peer = lax.rem(me + step, n)
            source = src_refs[index].at[peer] if per_peer[index] else src_refs[index]
            copy = pltpu.make_async_remote_copy(
                src_ref=source,
                dst_ref=out_refs[index].at[me],
                send_sem=send_sems.at[index, step],
                recv_sem=recv_sems.at[index, step],
                device_id={axis: peer},
                device_id_type=MESH,
            )
            copy.start()
            copies.append(copy)
    for index in range(count):
        me = lax.axis_index(axes[index])
        own = src_refs[index][me] if per_peer[index] else src_refs[index][...]
        out_refs[index][me] = own
    for copy in copies:
        copy.wait_send()
    for copy in copies:
        copy.wait_recv()


def exchange_multi(items, collective_id):
    axes = tuple(axis for axis, _, _ in items)
    sizes = tuple(lax.axis_size(axis) for axis in axes)
    blocks = [block for _, block, _ in items]
    per_peer = tuple(spread for _, _, spread in items)
    out_shapes = []
    sent = 0
    for n, block, spread in zip(sizes, blocks, per_peer):
        shape = block.shape[1:] if spread else block.shape
        out_shapes.append(jax.ShapeDtypeStruct((n,) + tuple(shape), block.dtype))
        sent += block.size * block.dtype.itemsize * (1 if spread else n)
    count = len(blocks)
    return pl.pallas_call(
        functools.partial(exchange_kernel, axes, sizes, per_peer),
        out_shape=tuple(out_shapes),
        in_specs=[pl.BlockSpec(memory_space=pltpu.VMEM)] * count,
        out_specs=tuple(pl.BlockSpec(memory_space=pltpu.VMEM) for _ in range(count)),
        scratch_shapes=[
            pltpu.SemaphoreType.DMA((count, max(sizes))),
            pltpu.SemaphoreType.DMA((count, max(sizes))),
        ],
        compiler_params=pltpu.CompilerParams(collective_id=collective_id, has_side_effects=True),
        cost_estimate=pl.CostEstimate(flops=0, bytes_accessed=2 * sent, transcendentals=0),
    )(*blocks)


def exchange(axis, blocks, per_peer, collective_id):
    return exchange_multi([(axis, b, s) for b, s in zip(blocks, per_peer)], collective_id)


def ring_gather_kernel(
    pair_count, ring_count, side_count, block_ref, side_ref, out_ref, side_out, send_sems, recv_sems, side_send, side_recv
):
    pair_slot = lax.axis_index("dp") // ring_count
    ring_slot = lax.axis_index("dp") % ring_count
    partner = (1 - pair_slot) * ring_count + ring_slot
    right = pair_slot * ring_count + lax.rem(ring_slot + 1, ring_count)
    left = pair_slot * ring_count + lax.rem(ring_slot + ring_count - 1, ring_count)
    me = pair_slot * ring_count + ring_slot
    side_me = lax.axis_index("tensor")
    barrier = pltpu.get_barrier_semaphore()
    for peer in (partner, right, left):
        pl.semaphore_signal(barrier, inc=1, device_id={"dp": peer}, device_id_type=MESH)
    for step in range(1, side_count):
        peer = lax.rem(side_me + step, side_count)
        pl.semaphore_signal(barrier, inc=1, device_id={"tensor": peer}, device_id_type=MESH)
    pl.semaphore_wait(barrier, 3 + side_count - 1)
    side_copies = []
    for step in range(1, side_count):
        peer = lax.rem(side_me + step, side_count)
        copy = pltpu.make_async_remote_copy(
            src_ref=side_ref,
            dst_ref=side_out.at[side_me],
            send_sem=side_send.at[step],
            recv_sem=side_recv.at[step],
            device_id={"tensor": peer},
            device_id_type=MESH,
        )
        copy.start()
        side_copies.append(copy)
    swap = pltpu.make_async_remote_copy(
        src_ref=block_ref,
        dst_ref=out_ref.at[me],
        send_sem=send_sems.at[2, 0, 0],
        recv_sem=recv_sems.at[2, 0, 0],
        device_id={"dp": partner},
        device_id_type=MESH,
    )
    swap.start()
    own = pltpu.make_async_copy(block_ref, out_ref.at[me], send_sems.at[2, 1, 0])
    own.start()
    side_out[side_me] = side_ref[...]
    own.wait()
    swap.wait_send()
    swap.wait_recv()
    right_steps = ring_count // 2
    left_steps = ring_count - 1 - right_steps
    sent = []

    def send(direction, step, target, origin):
        copies = []
        for member in range(pair_count):
            slot = member * ring_count + origin
            copy = pltpu.make_async_remote_copy(
                src_ref=out_ref.at[slot],
                dst_ref=out_ref.at[slot],
                send_sem=send_sems.at[direction, step, member],
                recv_sem=recv_sems.at[direction, step, member],
                device_id={"dp": target},
                device_id_type=MESH,
            )
            copy.start()
            copies.append(copy)
        sent.extend(copies)
        return copies

    right_copies = send(0, 0, right, ring_slot)
    left_copies = send(1, 0, left, ring_slot) if left_steps > 0 else []
    for step in range(1, right_steps):
        for copy in right_copies:
            copy.wait_recv()
        origin = lax.rem(ring_slot + ring_count - step, ring_count)
        right_copies = send(0, step, right, origin)
        if step < left_steps:
            for copy in left_copies:
                copy.wait_recv()
            origin = lax.rem(ring_slot + step, ring_count)
            left_copies = send(1, step, left, origin)
    for copy in right_copies + left_copies:
        copy.wait_recv()
    for copy in sent + side_copies:
        copy.wait_send()
    for copy in side_copies:
        copy.wait_recv()


def ring_gather(block, side, collective_id):
    count = lax.axis_size("dp")
    side_count = lax.axis_size("tensor")
    pair_count = 2
    ring_count = count // pair_count
    sent = count * block.size * block.dtype.itemsize + side_count * side.size * side.dtype.itemsize
    return pl.pallas_call(
        functools.partial(ring_gather_kernel, pair_count, ring_count, side_count),
        out_shape=(
            jax.ShapeDtypeStruct((count,) + block.shape, block.dtype),
            jax.ShapeDtypeStruct((side_count,) + side.shape, side.dtype),
        ),
        in_specs=[pl.BlockSpec(memory_space=pltpu.VMEM)] * 2,
        out_specs=(pl.BlockSpec(memory_space=pltpu.VMEM), pl.BlockSpec(memory_space=pltpu.VMEM)),
        scratch_shapes=[
            pltpu.SemaphoreType.DMA((3, ring_count, pair_count)),
            pltpu.SemaphoreType.DMA((3, ring_count, pair_count)),
            pltpu.SemaphoreType.DMA((side_count,)),
            pltpu.SemaphoreType.DMA((side_count,)),
        ],
        compiler_params=pltpu.CompilerParams(
            collective_id=collective_id, has_side_effects=True, vmem_limit_bytes=48 * 1024 * 1024
        ),
        cost_estimate=pl.CostEstimate(flops=0, bytes_accessed=2 * sent, transcendentals=0),
    )(block, side)

def pair_sum_kernel(ring_count, block_ref, out_ref, landing, sems):
    pair_slot = lax.axis_index("dp") // ring_count
    ring_slot = lax.axis_index("dp") % ring_count
    partner = (1 - pair_slot) * ring_count + ring_slot
    barrier = pltpu.get_barrier_semaphore()
    pl.semaphore_signal(barrier, inc=1, device_id={"dp": partner}, device_id_type=MESH)
    pl.semaphore_wait(barrier, 1)
    copy = pltpu.make_async_remote_copy(
        src_ref=block_ref.at[1 - pair_slot],
        dst_ref=landing,
        send_sem=sems.at[0],
        recv_sem=sems.at[1],
        device_id={"dp": partner},
        device_id_type=MESH,
    )
    copy.start()
    copy.wait_send()
    copy.wait_recv()
    out_ref[...] = block_ref[pair_slot] + landing[...]


def pair_sum(blocks, ring_count, collective_id):
    return pl.pallas_call(
        functools.partial(pair_sum_kernel, ring_count),
        out_shape=jax.ShapeDtypeStruct(blocks.shape[1:], blocks.dtype),
        in_specs=[pl.BlockSpec(memory_space=pltpu.VMEM)],
        out_specs=pl.BlockSpec(memory_space=pltpu.VMEM),
        scratch_shapes=[pltpu.VMEM(blocks.shape[1:], blocks.dtype), pltpu.SemaphoreType.DMA((2,))],
        compiler_params=pltpu.CompilerParams(collective_id=collective_id, has_side_effects=True),
        cost_estimate=pl.CostEstimate(
            flops=0, bytes_accessed=3 * blocks.size * blocks.dtype.itemsize, transcendentals=0
        ),
    )(blocks)


HD = 128
KV_HEADS = 4
HEADS_DEV = 4


def rope_tables(length, head_size):
    positions = lax.broadcasted_iota(jnp.int32, (length, head_size // 2), 0).astype(jnp.float32)
    index_half = lax.broadcasted_iota(jnp.int32, (length, head_size // 2), 1).astype(jnp.float32)
    frequency = jnp.exp(-(2.0 * index_half / head_size) * math.log(500000.0))
    angles = positions * frequency
    return (jnp.cos(angles), jnp.sin(angles))


def rotate(vectors, cosine_table, sine_table):
    half_size = vectors.shape[-1] // 2
    first_half = vectors[..., :half_size]
    second_half = vectors[..., half_size:]
    return jnp.concatenate(
        [
            first_half * cosine_table - second_half * sine_table,
            first_half * sine_table + second_half * cosine_table,
        ],
        axis=-1,
    )


def unrotate(vectors, cosine_table, sine_table):
    half_size = vectors.shape[-1] // 2
    first_half = vectors[..., :half_size]
    second_half = vectors[..., half_size:]
    return jnp.concatenate(
        [
            first_half * cosine_table + second_half * sine_table,
            second_half * cosine_table - first_half * sine_table,
        ],
        axis=-1,
    )


def on_device(inputs, grad_context, gain, w_query, w_keyval):
    seq_length = inputs.shape[0]
    local_cols = inputs.shape[1]
    model_width = gain.shape[0]
    head_size = HD
    heads_here = HEADS_DEV
    group_cols = w_keyval.shape[1]
    query_cols = w_query.shape[1]
    tensor_count = lax.axis_size("tensor")
    keyval_total = group_cols * tensor_count
    kv_heads = KV_HEADS
    devices_per_group = tensor_count // kv_heads
    score_scale = head_size ** (-0.5)
    tensor_slot = lax.axis_index("tensor")
    gain_local = lax.dynamic_slice_in_dim(gain, tensor_slot * local_cols, local_cols, 0)
    split_cols = query_cols // 2
    engine_block = jnp.concatenate([w_query[:, :split_cols], w_keyval], axis=1)
    engine_full = lax.all_gather(engine_block, "dp", axis=0, tiled=True)
    ring_blocks_out, input_blocks = ring_gather(w_query[:, split_cols:], inputs, 6)
    ring_full = ring_blocks_out.reshape(-1, query_cols - split_cols)
    input_values = input_blocks.astype(jnp.float32)
    row_sum = jnp.sum(input_values * input_values, axis=(0, 2)).reshape(seq_length, 1)
    inv_rms = lax.rsqrt(row_sum / model_width + 1e-05)
    gain_blocks = gain.reshape(tensor_count, 1, local_cols)
    unit_blocks = input_values * inv_rms[None, :, :]
    normed_blocks = (unit_blocks * gain_blocks).astype(jnp.bfloat16)
    normed_full = normed_blocks.transpose(1, 0, 2).reshape(seq_length, model_width)
    unit_rows = inputs.astype(jnp.float32) * inv_rms
    engine_proj = jnp.dot(normed_full, engine_full, preferred_element_type=jnp.float32).astype(
        jnp.bfloat16
    )
    ring_proj = jnp.dot(normed_full, ring_full, preferred_element_type=jnp.float32).astype(
        jnp.bfloat16
    )
    query_proj = jnp.concatenate([engine_proj[:, :split_cols], ring_proj], axis=1)
    keyval_part = engine_proj[:, split_cols:]
    (keyval_blocks,) = exchange("tensor", [keyval_part], [False], 1)
    keyval_full = keyval_blocks.transpose(1, 0, 2).reshape(seq_length, keyval_total)
    group_slot = tensor_slot // devices_per_group
    key_block = lax.dynamic_slice_in_dim(keyval_full, group_slot * head_size, head_size, 1)
    value_block = lax.dynamic_slice_in_dim(
        keyval_full, (kv_heads + group_slot) * head_size, head_size, 1
    )
    cosine_table, sine_table = rope_tables(seq_length, head_size)
    cos_heads = cosine_table[:, None, :]
    sin_heads = sine_table[:, None, :]
    query_heads = query_proj.astype(jnp.float32).reshape(seq_length, heads_here, head_size)
    q_rot = rotate(query_heads, cos_heads, sin_heads).astype(jnp.bfloat16)
    k_rot = rotate(key_block.astype(jnp.float32), cosine_table, sine_table).astype(jnp.bfloat16)
    scores = (
        jnp.einsum("shd,td->hst", q_rot, k_rot, preferred_element_type=jnp.float32) * score_scale
    )
    causal = lax.broadcasted_iota(jnp.int32, (seq_length, seq_length), 0) >= lax.broadcasted_iota(
        jnp.int32, (seq_length, seq_length), 1
    )
    exponent = jnp.where(causal[None, :, :], jnp.exp(scores), 0.0)
    softmax_probs = exponent / jnp.sum(exponent, axis=2, keepdims=True)
    prob_weights = softmax_probs.astype(jnp.bfloat16)
    context = jnp.einsum(
        "hst,td->shd", prob_weights, value_block, preferred_element_type=jnp.float32
    ).astype(jnp.bfloat16)
    grad_ctx = grad_context.reshape(seq_length, heads_here, head_size)
    grad_probs = jnp.einsum(
        "shd,td->hst", grad_ctx, value_block, preferred_element_type=jnp.float32
    )
    row_delta = jnp.sum(grad_ctx.astype(jnp.float32) * context.astype(jnp.float32), axis=2).T[
        :, :, None
    ]
    grad_scores = (softmax_probs * (grad_probs - row_delta) * score_scale).astype(jnp.bfloat16)
    grad_qrot = jnp.einsum("hst,td->shd", grad_scores, k_rot, preferred_element_type=jnp.float32)
    grad_krot = jnp.einsum("hst,shd->td", grad_scores, q_rot, preferred_element_type=jnp.float32)
    grad_value = jnp.einsum(
        "hst,shd->td", prob_weights, grad_ctx, preferred_element_type=jnp.float32
    )
    grad_query = (
        unrotate(grad_qrot, cos_heads, sin_heads)
        .astype(jnp.bfloat16)
        .reshape(seq_length, heads_here * head_size)
    )
    grad_terms = jnp.zeros((seq_length, keyval_total), jnp.float32)
    grad_terms = lax.dynamic_update_slice_in_dim(
        grad_terms, unrotate(grad_krot, cosine_table, sine_table), group_slot * head_size, 1
    )
    grad_terms = lax.dynamic_update_slice_in_dim(
        grad_terms, grad_value, (kv_heads + group_slot) * head_size, 1
    )
    term_blocks = grad_terms.reshape(seq_length, tensor_count, group_cols).transpose(1, 0, 2)
    (keyval_terms,) = exchange("tensor", [term_blocks], [True], 2)
    grad_keyval = jnp.sum(keyval_terms, axis=0).astype(jnp.bfloat16)
    engine_blocks = engine_full.reshape(tensor_count, local_cols, split_cols + group_cols)
    ring_blocks = ring_full.reshape(tensor_count, local_cols, query_cols - split_cols)
    engine_grads = jnp.concatenate([grad_query[:, :split_cols], grad_keyval], axis=1)
    normed_terms = (
        jnp.einsum("rc,pkc->prk", engine_grads, engine_blocks, preferred_element_type=jnp.float32)
        + jnp.einsum(
            "rc,pkc->prk",
            grad_query[:, split_cols:],
            ring_blocks,
            preferred_element_type=jnp.float32,
        )
    ).astype(jnp.bfloat16)
    product_part = jnp.sum(
        normed_terms.astype(jnp.float32) * gain_blocks * unit_blocks, axis=(0, 2)
    ).reshape(1, seq_length)
    dp_count = lax.axis_size("dp")
    pair_count = 2
    ring_count = dp_count // pair_count
    block_rows = model_width // dp_count
    normed_pairs = normed_full.reshape(
        seq_length, pair_count, ring_count, block_rows // 2, 2
    ).transpose(0, 2, 1, 3, 4)
    keyval_partials = jnp.concatenate(
        [
            jnp.einsum(
                "rbaq,rc->baqc",
                normed_pairs[..., half],
                grad_keyval,
                preferred_element_type=jnp.float32,
            )
            for half in range(2)
        ],
        axis=-1,
    ).reshape(model_width // 2, 2 * group_cols)
    ring_groups = [
        [pair * ring_count + slot for slot in range(ring_count)] for pair in range(pair_count)
    ]
    ring_sums = lax.psum_scatter(
        keyval_partials, "dp", scatter_dimension=0, tiled=True, axis_index_groups=ring_groups
    )
    normed_sums, product_parts = exchange(
        "tensor", [normed_terms, product_part], [True, False], 3
    )
    grad_normed = jnp.sum(normed_sums.astype(jnp.float32), axis=0)
    product_sum = jnp.sum(product_parts, axis=0).reshape(seq_length, 1)
    scaled_grad = grad_normed * gain_local
    grad_input = (inv_rms * (scaled_grad - unit_rows * (product_sum / model_width))).astype(
        jnp.bfloat16
    )
    gain_part = jnp.sum(grad_normed * unit_rows, axis=0).reshape(1, local_cols)
    (gain_parts,) = exchange("dp", [gain_part], [False], 4)
    grad_gain = jnp.sum(gain_parts, axis=(0, 1))
    lane_rows = ring_sums.size // (pair_count * 128)
    keyval_sums = pair_sum(ring_sums.reshape(pair_count, lane_rows, 128), ring_count, 7)
    keyval_weight_grad = keyval_sums.reshape(-1, group_cols)
    return (grad_input, grad_gain, keyval_weight_grad.astype(jnp.bfloat16))


def solution(mesh):
    in_specs = (P("dp", "tensor"), P("dp", "tensor"), P(), P("dp", "tensor"), P("dp", "tensor"))
    out_specs = (P("dp", "tensor"), P("tensor"), P("dp", "tensor"))
    return jax.shard_map(
        on_device, mesh=mesh, in_specs=in_specs, out_specs=out_specs, check_vma=False
    )
```

```python
import functools
import math

import jax
import jax.numpy as jnp
from jax import lax
from jax.experimental import pallas as pl
from jax.experimental.pallas import tpu as pltpu
from jax.sharding import PartitionSpec as P

MESH = pl.DeviceIdType.MESH


def exchange_kernel(axes, sizes, per_peer, *refs):
    count = len(per_peer)
    src_refs = refs[:count]
    out_refs = refs[count : 2 * count]
    send_sems, recv_sems = refs[2 * count :]
    barrier = pltpu.get_barrier_semaphore()
    waits = 0
    for axis in dict.fromkeys(axes):
        n = sizes[axes.index(axis)]
        me = lax.axis_index(axis)
        for step in range(1, n):
            peer = lax.rem(me + step, n)
            pl.semaphore_signal(barrier, inc=1, device_id={axis: peer}, device_id_type=MESH)
        waits += n - 1
    pl.semaphore_wait(barrier, waits)
    copies = []
    for index in range(count):
        axis, n = axes[index], sizes[index]
        me = lax.axis_index(axis)
        for step in range(1, n):
            peer = lax.rem(me + step, n)
            source = src_refs[index].at[peer] if per_peer[index] else src_refs[index]
            copy = pltpu.make_async_remote_copy(
                src_ref=source,
                dst_ref=out_refs[index].at[me],
                send_sem=send_sems.at[index, step],
                recv_sem=recv_sems.at[index, step],
                device_id={axis: peer},
                device_id_type=MESH,
            )
            copy.start()
            copies.append(copy)
    for index in range(count):
        me = lax.axis_index(axes[index])
        own = src_refs[index][me] if per_peer[index] else src_refs[index][...]
        out_refs[index][me] = own
    for copy in copies:
        copy.wait_send()
    for copy in copies:
        copy.wait_recv()


def exchange_multi(items, collective_id):
    axes = tuple(axis for axis, _, _ in items)
    sizes = tuple(lax.axis_size(axis) for axis in axes)
    blocks = [block for _, block, _ in items]
    per_peer = tuple(spread for _, _, spread in items)
    out_shapes = []
    sent = 0
    for n, block, spread in zip(sizes, blocks, per_peer):
        shape = block.shape[1:] if spread else block.shape
        out_shapes.append(jax.ShapeDtypeStruct((n,) + tuple(shape), block.dtype))
        sent += block.size * block.dtype.itemsize * (1 if spread else n)
    count = len(blocks)
    return pl.pallas_call(
        functools.partial(exchange_kernel, axes, sizes, per_peer),
        out_shape=tuple(out_shapes),
        in_specs=[pl.BlockSpec(memory_space=pltpu.VMEM)] * count,
        out_specs=tuple(pl.BlockSpec(memory_space=pltpu.VMEM) for _ in range(count)),
        scratch_shapes=[
            pltpu.SemaphoreType.DMA((count, max(sizes))),
            pltpu.SemaphoreType.DMA((count, max(sizes))),
        ],
        compiler_params=pltpu.CompilerParams(collective_id=collective_id, has_side_effects=True),
        cost_estimate=pl.CostEstimate(flops=0, bytes_accessed=2 * sent, transcendentals=0),
    )(*blocks)


def exchange(axis, blocks, per_peer, collective_id):
    return exchange_multi([(axis, b, s) for b, s in zip(blocks, per_peer)], collective_id)


def ring_gather_kernel(
    pair_count, ring_count, side_count, block_ref, side_ref, out_ref, side_out, send_sems, recv_sems, side_send, side_recv
):
    pair_slot = lax.axis_index("dp") // ring_count
    ring_slot = lax.axis_index("dp") % ring_count
    partner = (1 - pair_slot) * ring_count + ring_slot
    right = pair_slot * ring_count + lax.rem(ring_slot + 1, ring_count)
    left = pair_slot * ring_count + lax.rem(ring_slot + ring_count - 1, ring_count)
    me = pair_slot * ring_count + ring_slot
    side_me = lax.axis_index("tensor")
    barrier = pltpu.get_barrier_semaphore()
    for peer in (partner, right, left):
        pl.semaphore_signal(barrier, inc=1, device_id={"dp": peer}, device_id_type=MESH)
    for step in range(1, side_count):
        peer = lax.rem(side_me + step, side_count)
        pl.semaphore_signal(barrier, inc=1, device_id={"tensor": peer}, device_id_type=MESH)
    pl.semaphore_wait(barrier, 3 + side_count - 1)
    side_copies = []
    for step in range(1, side_count):
        peer = lax.rem(side_me + step, side_count)
        copy = pltpu.make_async_remote_copy(
            src_ref=side_ref,
            dst_ref=side_out.at[side_me],
            send_sem=side_send.at[step],
            recv_sem=side_recv.at[step],
            device_id={"tensor": peer},
            device_id_type=MESH,
        )
        copy.start()
        side_copies.append(copy)
    swap = pltpu.make_async_remote_copy(
        src_ref=block_ref,
        dst_ref=out_ref.at[me],
        send_sem=send_sems.at[2, 0, 0],
        recv_sem=recv_sems.at[2, 0, 0],
        device_id={"dp": partner},
        device_id_type=MESH,
    )
    swap.start()
    own = pltpu.make_async_copy(block_ref, out_ref.at[me], send_sems.at[2, 1, 0])
    own.start()
    side_out[side_me] = side_ref[...]
    own.wait()
    swap.wait_send()
    swap.wait_recv()
    right_steps = ring_count // 2
    left_steps = ring_count - 1 - right_steps
    sent = []

    def send(direction, step, target, origin):
        copies = []
        for member in range(pair_count):
            slot = member * ring_count + origin
            copy = pltpu.make_async_remote_copy(
                src_ref=out_ref.at[slot],
                dst_ref=out_ref.at[slot],
                send_sem=send_sems.at[direction, step, member],
                recv_sem=recv_sems.at[direction, step, member],
                device_id={"dp": target},
                device_id_type=MESH,
            )
            copy.start()
            copies.append(copy)
        sent.extend(copies)
        return copies

    right_copies = send(0, 0, right, ring_slot)
    left_copies = send(1, 0, left, ring_slot) if left_steps > 0 else []
    for step in range(1, right_steps):
        for copy in right_copies:
            copy.wait_recv()
        origin = lax.rem(ring_slot + ring_count - step, ring_count)
        right_copies = send(0, step, right, origin)
        if step < left_steps:
            for copy in left_copies:
                copy.wait_recv()
            origin = lax.rem(ring_slot + step, ring_count)
            left_copies = send(1, step, left, origin)
    for copy in right_copies + left_copies:
        copy.wait_recv()
    for copy in sent + side_copies:
        copy.wait_send()
    for copy in side_copies:
        copy.wait_recv()


def ring_gather(block, side, collective_id):
    count = lax.axis_size("dp")
    side_count = lax.axis_size("tensor")
    pair_count = 2
    ring_count = count // pair_count
    sent = count * block.size * block.dtype.itemsize + side_count * side.size * side.dtype.itemsize
    return pl.pallas_call(
        functools.partial(ring_gather_kernel, pair_count, ring_count, side_count),
        out_shape=(
            jax.ShapeDtypeStruct((count,) + block.shape, block.dtype),
            jax.ShapeDtypeStruct((side_count,) + side.shape, side.dtype),
        ),
        in_specs=[pl.BlockSpec(memory_space=pltpu.VMEM)] * 2,
        out_specs=(pl.BlockSpec(memory_space=pltpu.VMEM), pl.BlockSpec(memory_space=pltpu.VMEM)),
        scratch_shapes=[
            pltpu.SemaphoreType.DMA((3, ring_count, pair_count)),
            pltpu.SemaphoreType.DMA((3, ring_count, pair_count)),
            pltpu.SemaphoreType.DMA((side_count,)),
            pltpu.SemaphoreType.DMA((side_count,)),
        ],
        compiler_params=pltpu.CompilerParams(
            collective_id=collective_id, has_side_effects=True, vmem_limit_bytes=48 * 1024 * 1024
        ),
        cost_estimate=pl.CostEstimate(flops=0, bytes_accessed=2 * sent, transcendentals=0),
    )(block, side)

def pair_sum_kernel(ring_count, block_ref, out_ref, landing, sems):
    pair_slot = lax.axis_index("dp") // ring_count
    ring_slot = lax.axis_index("dp") % ring_count
    partner = (1 - pair_slot) * ring_count + ring_slot
    barrier = pltpu.get_barrier_semaphore()
    pl.semaphore_signal(barrier, inc=1, device_id={"dp": partner}, device_id_type=MESH)
    pl.semaphore_wait(barrier, 1)
    copy = pltpu.make_async_remote_copy(
        src_ref=block_ref.at[1 - pair_slot],
        dst_ref=landing,
        send_sem=sems.at[0],
        recv_sem=sems.at[1],
        device_id={"dp": partner},
        device_id_type=MESH,
    )
    copy.start()
    copy.wait_send()
    copy.wait_recv()
    out_ref[...] = block_ref[pair_slot] + landing[...]


def pair_sum(blocks, ring_count, collective_id):
    return pl.pallas_call(
        functools.partial(pair_sum_kernel, ring_count),
        out_shape=jax.ShapeDtypeStruct(blocks.shape[1:], blocks.dtype),
        in_specs=[pl.BlockSpec(memory_space=pltpu.VMEM)],
        out_specs=pl.BlockSpec(memory_space=pltpu.VMEM),
        scratch_shapes=[pltpu.VMEM(blocks.shape[1:], blocks.dtype), pltpu.SemaphoreType.DMA((2,))],
        compiler_params=pltpu.CompilerParams(collective_id=collective_id, has_side_effects=True),
        cost_estimate=pl.CostEstimate(
            flops=0, bytes_accessed=3 * blocks.size * blocks.dtype.itemsize, transcendentals=0
        ),
    )(blocks)


def group_kernel(routes, src_ref, out_ref, send_sems, recv_sems):
    me = lax.axis_index("tensor")
    dests, sources = routes(me)
    barrier = pltpu.get_barrier_semaphore()
    count = jnp.int32(0)
    for peer in [d for d, _, _ in dests] + sources:

        @pl.when(peer != me)
        def _():
            pl.semaphore_signal(barrier, inc=1, device_id={"tensor": peer}, device_id_type=MESH)

        count = count + (peer != me).astype(jnp.int32)
    pl.semaphore_wait(barrier, count)
    copies = []
    for index, (peer, slot, block) in enumerate(dests):
        copy = pltpu.make_async_remote_copy(
            src_ref=src_ref.at[block],
            dst_ref=out_ref.at[slot],
            send_sem=send_sems.at[index],
            recv_sem=recv_sems.at[slot],
            device_id={"tensor": peer},
            device_id_type=MESH,
        )
        copies.append(copy)

        @pl.when(peer != me)
        def _():
            copy.start()

        @pl.when(peer == me)
        def _():
            out_ref[slot] = src_ref[block]

    for (peer, _, _), copy in zip(dests, copies):

        @pl.when(peer != me)
        def _():
            copy.wait_send()

    for slot, peer in enumerate(sources):
        arrival = pltpu.make_async_remote_copy(
            src_ref=src_ref.at[0],
            dst_ref=out_ref.at[slot],
            send_sem=send_sems.at[0],
            recv_sem=recv_sems.at[slot],
            device_id={"tensor": peer},
            device_id_type=MESH,
        )

        @pl.when(peer != me)
        def _():
            arrival.wait_recv()


def group_exchange(routes, blocks, slots, collective_id):
    return pl.pallas_call(
        functools.partial(group_kernel, routes),
        out_shape=jax.ShapeDtypeStruct((slots,) + blocks.shape[1:], blocks.dtype),
        in_specs=[pl.BlockSpec(memory_space=pltpu.VMEM)],
        out_specs=pl.BlockSpec(memory_space=pltpu.VMEM),
        scratch_shapes=[pltpu.SemaphoreType.DMA((slots,)), pltpu.SemaphoreType.DMA((slots,))],
        compiler_params=pltpu.CompilerParams(collective_id=collective_id, has_side_effects=True),
        cost_estimate=pl.CostEstimate(
            flops=0, bytes_accessed=2 * slots * blocks[0].size * blocks.dtype.itemsize, transcendentals=0
        ),
    )(blocks)


def keyval_routes(me):
    head_group = lax.rem(me // 2, KV_HEADS)
    slot = 2 * (me // (2 * KV_HEADS)) + lax.rem(me, 2)
    dests = [(KV_HEADS * head_group + m, slot, 0) for m in range(KV_HEADS)]
    group = me // KV_HEADS
    sources = [2 * group, 2 * group + 1, 2 * KV_HEADS + 2 * group, 2 * KV_HEADS + 2 * group + 1]
    return dests, sources


def term_routes(me):
    group = me // KV_HEADS
    slot = lax.rem(me, KV_HEADS)
    targets = [2 * group, 2 * group + 1, 2 * KV_HEADS + 2 * group, 2 * KV_HEADS + 2 * group + 1]
    dests = [(target, slot, m) for m, target in enumerate(targets)]
    head_group = lax.rem(me // 2, KV_HEADS)
    sources = [KV_HEADS * head_group + m for m in range(KV_HEADS)]
    return dests, sources


HD = 128
KV_HEADS = 4
HEADS_DEV = 4


def rope_tables(length, head_size):
    positions = lax.broadcasted_iota(jnp.int32, (length, head_size // 2), 0).astype(jnp.float32)
    index_half = lax.broadcasted_iota(jnp.int32, (length, head_size // 2), 1).astype(jnp.float32)
    frequency = jnp.exp(-(2.0 * index_half / head_size) * math.log(500000.0))
    angles = positions * frequency
    return (jnp.cos(angles), jnp.sin(angles))


def rotate(vectors, cosine_table, sine_table):
    half_size = vectors.shape[-1] // 2
    first_half = vectors[..., :half_size]
    second_half = vectors[..., half_size:]
    return jnp.concatenate(
        [
            first_half * cosine_table - second_half * sine_table,
            first_half * sine_table + second_half * cosine_table,
        ],
        axis=-1,
    )


def unrotate(vectors, cosine_table, sine_table):
    half_size = vectors.shape[-1] // 2
    first_half = vectors[..., :half_size]
    second_half = vectors[..., half_size:]
    return jnp.concatenate(
        [
            first_half * cosine_table + second_half * sine_table,
            second_half * cosine_table - first_half * sine_table,
        ],
        axis=-1,
    )


def on_device(inputs, grad_context, gain, w_query, w_keyval):
    seq_length = inputs.shape[0]
    local_cols = inputs.shape[1]
    model_width = gain.shape[0]
    head_size = HD
    heads_here = HEADS_DEV
    group_cols = w_keyval.shape[1]
    query_cols = w_query.shape[1]
    tensor_count = lax.axis_size("tensor")
    keyval_total = group_cols * tensor_count
    kv_heads = KV_HEADS
    devices_per_group = tensor_count // kv_heads
    score_scale = head_size ** (-0.5)
    tensor_slot = lax.axis_index("tensor")
    gain_local = lax.dynamic_slice_in_dim(gain, tensor_slot * local_cols, local_cols, 0)
    split_cols = query_cols // 2
    engine_block = jnp.concatenate([w_query[:, :split_cols], w_keyval], axis=1)
    engine_full = lax.all_gather(engine_block, "dp", axis=0, tiled=True)
    ring_blocks_out, input_blocks = ring_gather(w_query[:, split_cols:], inputs, 6)
    ring_full = ring_blocks_out.reshape(-1, query_cols - split_cols)
    input_values = input_blocks.astype(jnp.float32)
    row_sum = jnp.sum(input_values * input_values, axis=(0, 2)).reshape(seq_length, 1)
    inv_rms = lax.rsqrt(row_sum / model_width + 1e-05)
    gain_blocks = gain.reshape(tensor_count, 1, local_cols)
    unit_blocks = input_values * inv_rms[None, :, :]
    normed_blocks = (unit_blocks * gain_blocks).astype(jnp.bfloat16)
    normed_full = normed_blocks.transpose(1, 0, 2).reshape(seq_length, model_width)
    unit_rows = inputs.astype(jnp.float32) * inv_rms
    engine_proj = jnp.dot(normed_full, engine_full, preferred_element_type=jnp.float32).astype(
        jnp.bfloat16
    )
    ring_proj = jnp.dot(normed_full, ring_full, preferred_element_type=jnp.float32).astype(
        jnp.bfloat16
    )
    query_proj = jnp.concatenate([engine_proj[:, :split_cols], ring_proj], axis=1)
    keyval_part = engine_proj[:, split_cols:]
    keyval_pieces = group_exchange(keyval_routes, keyval_part[None], 4, 1)
    key_block = jnp.concatenate([keyval_pieces[0], keyval_pieces[1]], axis=1)
    value_block = jnp.concatenate([keyval_pieces[2], keyval_pieces[3]], axis=1)
    cosine_table, sine_table = rope_tables(seq_length, head_size)
    cos_heads = cosine_table[:, None, :]
    sin_heads = sine_table[:, None, :]
    query_heads = query_proj.astype(jnp.float32).reshape(seq_length, heads_here, head_size)
    q_rot = rotate(query_heads, cos_heads, sin_heads).astype(jnp.bfloat16)
    k_rot = rotate(key_block.astype(jnp.float32), cosine_table, sine_table).astype(jnp.bfloat16)
    scores = (
        jnp.einsum("shd,td->hst", q_rot, k_rot, preferred_element_type=jnp.float32) * score_scale
    )
    causal = lax.broadcasted_iota(jnp.int32, (seq_length, seq_length), 0) >= lax.broadcasted_iota(
        jnp.int32, (seq_length, seq_length), 1
    )
    exponent = jnp.where(causal[None, :, :], jnp.exp(scores), 0.0)
    softmax_probs = exponent / jnp.sum(exponent, axis=2, keepdims=True)
    prob_weights = softmax_probs.astype(jnp.bfloat16)
    context = jnp.einsum(
        "hst,td->shd", prob_weights, value_block, preferred_element_type=jnp.float32
    ).astype(jnp.bfloat16)
    grad_ctx = grad_context.reshape(seq_length, heads_here, head_size)
    grad_probs = jnp.einsum(
        "shd,td->hst", grad_ctx, value_block, preferred_element_type=jnp.float32
    )
    row_delta = jnp.sum(grad_ctx.astype(jnp.float32) * context.astype(jnp.float32), axis=2).T[
        :, :, None
    ]
    grad_scores = (softmax_probs * (grad_probs - row_delta) * score_scale).astype(jnp.bfloat16)
    grad_qrot = jnp.einsum("hst,td->shd", grad_scores, k_rot, preferred_element_type=jnp.float32)
    grad_krot = jnp.einsum("hst,shd->td", grad_scores, q_rot, preferred_element_type=jnp.float32)
    grad_value = jnp.einsum(
        "hst,shd->td", prob_weights, grad_ctx, preferred_element_type=jnp.float32
    )
    grad_query = (
        unrotate(grad_qrot, cos_heads, sin_heads)
        .astype(jnp.bfloat16)
        .reshape(seq_length, heads_here * head_size)
    )
    grad_key = unrotate(grad_krot, cosine_table, sine_table)
    term_blocks = jnp.stack(
        [grad_key[:, :group_cols], grad_key[:, group_cols:], grad_value[:, :group_cols], grad_value[:, group_cols:]]
    )
    keyval_terms = group_exchange(term_routes, term_blocks, 4, 2)
    grad_keyval = jnp.sum(keyval_terms, axis=0).astype(jnp.bfloat16)
    engine_blocks = engine_full.reshape(tensor_count, local_cols, split_cols + group_cols)
    ring_blocks = ring_full.reshape(tensor_count, local_cols, query_cols - split_cols)
    engine_grads = jnp.concatenate([grad_query[:, :split_cols], grad_keyval], axis=1)
    normed_terms = (
        jnp.einsum("rc,pkc->prk", engine_grads, engine_blocks, preferred_element_type=jnp.float32)
        + jnp.einsum(
            "rc,pkc->prk",
            grad_query[:, split_cols:],
            ring_blocks,
            preferred_element_type=jnp.float32,
        )
    ).astype(jnp.bfloat16)
    product_part = jnp.sum(
        normed_terms.astype(jnp.float32) * gain_blocks * unit_blocks, axis=(0, 2)
    ).reshape(1, seq_length)
    dp_count = lax.axis_size("dp")
    pair_count = 2
    ring_count = dp_count // pair_count
    block_rows = model_width // dp_count
    normed_pairs = normed_full.reshape(
        seq_length, pair_count, ring_count, block_rows // 2, 2
    ).transpose(0, 2, 1, 3, 4)
    keyval_partials = jnp.concatenate(
        [
            jnp.einsum(
                "rbaq,rc->baqc",
                normed_pairs[..., half],
                grad_keyval,
                preferred_element_type=jnp.float32,
            )
            for half in range(2)
        ],
        axis=-1,
    ).reshape(model_width // 2, 2 * group_cols)
    ring_groups = [
        [pair * ring_count + slot for slot in range(ring_count)] for pair in range(pair_count)
    ]
    ring_sums = lax.psum_scatter(
        keyval_partials, "dp", scatter_dimension=0, tiled=True, axis_index_groups=ring_groups
    )
    normed_sums, product_parts = exchange(
        "tensor", [normed_terms, product_part], [True, False], 3
    )
    grad_normed = jnp.sum(normed_sums.astype(jnp.float32), axis=0)
    product_sum = jnp.sum(product_parts, axis=0).reshape(seq_length, 1)
    scaled_grad = grad_normed * gain_local
    grad_input = (inv_rms * (scaled_grad - unit_rows * (product_sum / model_width))).astype(
        jnp.bfloat16
    )
    gain_part = jnp.sum(grad_normed * unit_rows, axis=0).reshape(1, local_cols)
    (gain_parts,) = exchange("dp", [gain_part], [False], 4)
    grad_gain = jnp.sum(gain_parts, axis=(0, 1))
    lane_rows = ring_sums.size // (pair_count * 128)
    keyval_sums = pair_sum(ring_sums.reshape(pair_count, lane_rows, 128), ring_count, 7)
    keyval_weight_grad = keyval_sums.reshape(-1, group_cols)
    return (grad_input, grad_gain, keyval_weight_grad.astype(jnp.bfloat16))


def solution(mesh):
    in_specs = (P("dp", "tensor"), P("dp", "tensor"), P(), P("dp", "tensor"), P("dp", "tensor"))
    out_specs = (P("dp", "tensor"), P("tensor"), P("dp", "tensor"))
    return jax.shard_map(
        on_device, mesh=mesh, in_specs=in_specs, out_specs=out_specs, check_vma=False
    )
```

```python
import functools
import math

import jax
import jax.numpy as jnp
from jax import lax
from jax.experimental import pallas as pl
from jax.experimental.pallas import tpu as pltpu
from jax.sharding import PartitionSpec as P

MESH = pl.DeviceIdType.MESH


def exchange_kernel(axes, sizes, per_peer, *refs):
    count = len(per_peer)
    src_refs = refs[:count]
    out_refs = refs[count : 2 * count]
    send_sems, recv_sems = refs[2 * count :]
    barrier = pltpu.get_barrier_semaphore()
    waits = 0
    for axis in dict.fromkeys(axes):
        n = sizes[axes.index(axis)]
        me = lax.axis_index(axis)
        for step in range(1, n):
            peer = lax.rem(me + step, n)
            pl.semaphore_signal(barrier, inc=1, device_id={axis: peer}, device_id_type=MESH)
        waits += n - 1
    pl.semaphore_wait(barrier, waits)
    copies = []
    for index in range(count):
        axis, n = axes[index], sizes[index]
        me = lax.axis_index(axis)
        for step in range(1, n):
            peer = lax.rem(me + step, n)
            source = src_refs[index].at[peer] if per_peer[index] else src_refs[index]
            copy = pltpu.make_async_remote_copy(
                src_ref=source,
                dst_ref=out_refs[index].at[me],
                send_sem=send_sems.at[index, step],
                recv_sem=recv_sems.at[index, step],
                device_id={axis: peer},
                device_id_type=MESH,
            )
            copy.start()
            copies.append(copy)
    for index in range(count):
        me = lax.axis_index(axes[index])
        own = src_refs[index][me] if per_peer[index] else src_refs[index][...]
        out_refs[index][me] = own
    for copy in copies:
        copy.wait_send()
    for copy in copies:
        copy.wait_recv()


def exchange_multi(items, collective_id):
    axes = tuple(axis for axis, _, _ in items)
    sizes = tuple(lax.axis_size(axis) for axis in axes)
    blocks = [block for _, block, _ in items]
    per_peer = tuple(spread for _, _, spread in items)
    out_shapes = []
    sent = 0
    for n, block, spread in zip(sizes, blocks, per_peer):
        shape = block.shape[1:] if spread else block.shape
        out_shapes.append(jax.ShapeDtypeStruct((n,) + tuple(shape), block.dtype))
        sent += block.size * block.dtype.itemsize * (1 if spread else n)
    count = len(blocks)
    return pl.pallas_call(
        functools.partial(exchange_kernel, axes, sizes, per_peer),
        out_shape=tuple(out_shapes),
        in_specs=[pl.BlockSpec(memory_space=pltpu.VMEM)] * count,
        out_specs=tuple(pl.BlockSpec(memory_space=pltpu.VMEM) for _ in range(count)),
        scratch_shapes=[
            pltpu.SemaphoreType.DMA((count, max(sizes))),
            pltpu.SemaphoreType.DMA((count, max(sizes))),
        ],
        compiler_params=pltpu.CompilerParams(collective_id=collective_id, has_side_effects=True),
        cost_estimate=pl.CostEstimate(flops=0, bytes_accessed=2 * sent, transcendentals=0),
    )(*blocks)


def exchange(axis, blocks, per_peer, collective_id):
    return exchange_multi([(axis, b, s) for b, s in zip(blocks, per_peer)], collective_id)


def ring_gather_kernel(
    pair_count, ring_count, side_count, block_ref, side_ref, out_ref, side_out, send_sems, recv_sems, side_send, side_recv
):
    pair_slot = lax.axis_index("dp") // ring_count
    ring_slot = lax.axis_index("dp") % ring_count
    partner = (1 - pair_slot) * ring_count + ring_slot
    right = pair_slot * ring_count + lax.rem(ring_slot + 1, ring_count)
    left = pair_slot * ring_count + lax.rem(ring_slot + ring_count - 1, ring_count)
    me = pair_slot * ring_count + ring_slot
    side_me = lax.axis_index("tensor")
    barrier = pltpu.get_barrier_semaphore()
    for peer in (partner, right, left):
        pl.semaphore_signal(barrier, inc=1, device_id={"dp": peer}, device_id_type=MESH)
    for step in range(1, side_count):
        peer = lax.rem(side_me + step, side_count)
        pl.semaphore_signal(barrier, inc=1, device_id={"tensor": peer}, device_id_type=MESH)
    pl.semaphore_wait(barrier, 3 + side_count - 1)
    side_copies = []
    for step in range(1, side_count):
        peer = lax.rem(side_me + step, side_count)
        copy = pltpu.make_async_remote_copy(
            src_ref=side_ref,
            dst_ref=side_out.at[side_me],
            send_sem=side_send.at[step],
            recv_sem=side_recv.at[step],
            device_id={"tensor": peer},
            device_id_type=MESH,
        )
        copy.start()
        side_copies.append(copy)
    swap = pltpu.make_async_remote_copy(
        src_ref=block_ref,
        dst_ref=out_ref.at[me],
        send_sem=send_sems.at[2, 0, 0],
        recv_sem=recv_sems.at[2, 0, 0],
        device_id={"dp": partner},
        device_id_type=MESH,
    )
    swap.start()
    own = pltpu.make_async_copy(block_ref, out_ref.at[me], send_sems.at[2, 1, 0])
    own.start()
    side_out[side_me] = side_ref[...]
    own.wait()
    swap.wait_send()
    swap.wait_recv()
    right_steps = ring_count // 2
    left_steps = ring_count - 1 - right_steps
    sent = []

    def send(direction, step, target, origin):
        copies = []
        for member in range(pair_count):
            slot = member * ring_count + origin
            copy = pltpu.make_async_remote_copy(
                src_ref=out_ref.at[slot],
                dst_ref=out_ref.at[slot],
                send_sem=send_sems.at[direction, step, member],
                recv_sem=recv_sems.at[direction, step, member],
                device_id={"dp": target},
                device_id_type=MESH,
            )
            copy.start()
            copies.append(copy)
        sent.extend(copies)
        return copies

    right_copies = send(0, 0, right, ring_slot)
    left_copies = send(1, 0, left, ring_slot) if left_steps > 0 else []
    for step in range(1, right_steps):
        for copy in right_copies:
            copy.wait_recv()
        origin = lax.rem(ring_slot + ring_count - step, ring_count)
        right_copies = send(0, step, right, origin)
        if step < left_steps:
            for copy in left_copies:
                copy.wait_recv()
            origin = lax.rem(ring_slot + step, ring_count)
            left_copies = send(1, step, left, origin)
    for copy in right_copies + left_copies:
        copy.wait_recv()
    for copy in sent + side_copies:
        copy.wait_send()
    for copy in side_copies:
        copy.wait_recv()


def ring_gather(block, side, collective_id):
    count = lax.axis_size("dp")
    side_count = lax.axis_size("tensor")
    pair_count = 2
    ring_count = count // pair_count
    sent = count * block.size * block.dtype.itemsize + side_count * side.size * side.dtype.itemsize
    return pl.pallas_call(
        functools.partial(ring_gather_kernel, pair_count, ring_count, side_count),
        out_shape=(
            jax.ShapeDtypeStruct((count,) + block.shape, block.dtype),
            jax.ShapeDtypeStruct((side_count,) + side.shape, side.dtype),
        ),
        in_specs=[pl.BlockSpec(memory_space=pltpu.VMEM)] * 2,
        out_specs=(pl.BlockSpec(memory_space=pltpu.VMEM), pl.BlockSpec(memory_space=pltpu.VMEM)),
        scratch_shapes=[
            pltpu.SemaphoreType.DMA((3, ring_count, pair_count)),
            pltpu.SemaphoreType.DMA((3, ring_count, pair_count)),
            pltpu.SemaphoreType.DMA((side_count,)),
            pltpu.SemaphoreType.DMA((side_count,)),
        ],
        compiler_params=pltpu.CompilerParams(
            collective_id=collective_id, has_side_effects=True, vmem_limit_bytes=48 * 1024 * 1024
        ),
        cost_estimate=pl.CostEstimate(flops=0, bytes_accessed=2 * sent, transcendentals=0),
    )(block, side)

def pair_sum_kernel(ring_count, block_ref, out_ref, landing, sems):
    pair_slot = lax.axis_index("dp") // ring_count
    ring_slot = lax.axis_index("dp") % ring_count
    partner = (1 - pair_slot) * ring_count + ring_slot
    barrier = pltpu.get_barrier_semaphore()
    pl.semaphore_signal(barrier, inc=1, device_id={"dp": partner}, device_id_type=MESH)
    pl.semaphore_wait(barrier, 1)
    copy = pltpu.make_async_remote_copy(
        src_ref=block_ref.at[1 - pair_slot],
        dst_ref=landing,
        send_sem=sems.at[0],
        recv_sem=sems.at[1],
        device_id={"dp": partner},
        device_id_type=MESH,
    )
    copy.start()
    copy.wait_send()
    copy.wait_recv()
    out_ref[...] = block_ref[pair_slot] + landing[...]


def pair_sum(blocks, ring_count, collective_id):
    return pl.pallas_call(
        functools.partial(pair_sum_kernel, ring_count),
        out_shape=jax.ShapeDtypeStruct(blocks.shape[1:], blocks.dtype),
        in_specs=[pl.BlockSpec(memory_space=pltpu.VMEM)],
        out_specs=pl.BlockSpec(memory_space=pltpu.VMEM),
        scratch_shapes=[pltpu.VMEM(blocks.shape[1:], blocks.dtype), pltpu.SemaphoreType.DMA((2,))],
        compiler_params=pltpu.CompilerParams(collective_id=collective_id, has_side_effects=True),
        cost_estimate=pl.CostEstimate(
            flops=0, bytes_accessed=3 * blocks.size * blocks.dtype.itemsize, transcendentals=0
        ),
    )(blocks)


def group_kernel(routes, src_ref, out_ref, send_sems, recv_sems):
    me = lax.axis_index("tensor")
    dests, sources = routes(me)
    barrier = pltpu.get_barrier_semaphore()
    count = jnp.int32(0)
    for peer in [d for d, _, _ in dests] + sources:

        @pl.when(peer != me)
        def _():
            pl.semaphore_signal(barrier, inc=1, device_id={"tensor": peer}, device_id_type=MESH)

        count = count + (peer != me).astype(jnp.int32)
    pl.semaphore_wait(barrier, count)
    copies = []
    for index, (peer, slot, block) in enumerate(dests):
        copy = pltpu.make_async_remote_copy(
            src_ref=src_ref.at[block],
            dst_ref=out_ref.at[slot],
            send_sem=send_sems.at[index],
            recv_sem=recv_sems.at[slot],
            device_id={"tensor": peer},
            device_id_type=MESH,
        )
        copies.append(copy)

        @pl.when(peer != me)
        def _():
            copy.start()

        @pl.when(peer == me)
        def _():
            out_ref[slot] = src_ref[block]

    for (peer, _, _), copy in zip(dests, copies):

        @pl.when(peer != me)
        def _():
            copy.wait_send()

    for slot, peer in enumerate(sources):
        arrival = pltpu.make_async_remote_copy(
            src_ref=src_ref.at[0],
            dst_ref=out_ref.at[slot],
            send_sem=send_sems.at[0],
            recv_sem=recv_sems.at[slot],
            device_id={"tensor": peer},
            device_id_type=MESH,
        )

        @pl.when(peer != me)
        def _():
            arrival.wait_recv()


def group_exchange(routes, blocks, slots, collective_id):
    return pl.pallas_call(
        functools.partial(group_kernel, routes),
        out_shape=jax.ShapeDtypeStruct((slots,) + blocks.shape[1:], blocks.dtype),
        in_specs=[pl.BlockSpec(memory_space=pltpu.VMEM)],
        out_specs=pl.BlockSpec(memory_space=pltpu.VMEM),
        scratch_shapes=[pltpu.SemaphoreType.DMA((slots,)), pltpu.SemaphoreType.DMA((slots,))],
        compiler_params=pltpu.CompilerParams(collective_id=collective_id, has_side_effects=True),
        cost_estimate=pl.CostEstimate(
            flops=0, bytes_accessed=2 * slots * blocks[0].size * blocks.dtype.itemsize, transcendentals=0
        ),
    )(blocks)


def keyval_routes(me):
    head_group = lax.rem(me // 2, KV_HEADS)
    slot = 2 * (me // (2 * KV_HEADS)) + lax.rem(me, 2)
    dests = [(KV_HEADS * head_group + m, slot, 0) for m in range(KV_HEADS)]
    group = me // KV_HEADS
    sources = [2 * group, 2 * group + 1, 2 * KV_HEADS + 2 * group, 2 * KV_HEADS + 2 * group + 1]
    return dests, sources


def term_routes(me):
    group = me // KV_HEADS
    slot = lax.rem(me, KV_HEADS)
    targets = [2 * group, 2 * group + 1, 2 * KV_HEADS + 2 * group, 2 * KV_HEADS + 2 * group + 1]
    dests = [(target, slot, m) for m, target in enumerate(targets)]
    head_group = lax.rem(me // 2, KV_HEADS)
    sources = [KV_HEADS * head_group + m for m in range(KV_HEADS)]
    return dests, sources


HD = 128
KV_HEADS = 4
HEADS_DEV = 4


def rope_tables(length, head_size):
    positions = lax.broadcasted_iota(jnp.int32, (length, head_size // 2), 0).astype(jnp.float32)
    index_half = lax.broadcasted_iota(jnp.int32, (length, head_size // 2), 1).astype(jnp.float32)
    frequency = jnp.exp(-(2.0 * index_half / head_size) * math.log(500000.0))
    angles = positions * frequency
    return (jnp.cos(angles), jnp.sin(angles))


def rotate(vectors, cosine_table, sine_table):
    half_size = vectors.shape[-1] // 2
    first_half = vectors[..., :half_size]
    second_half = vectors[..., half_size:]
    return jnp.concatenate(
        [
            first_half * cosine_table - second_half * sine_table,
            first_half * sine_table + second_half * cosine_table,
        ],
        axis=-1,
    )


def unrotate(vectors, cosine_table, sine_table):
    half_size = vectors.shape[-1] // 2
    first_half = vectors[..., :half_size]
    second_half = vectors[..., half_size:]
    return jnp.concatenate(
        [
            first_half * cosine_table + second_half * sine_table,
            second_half * cosine_table - first_half * sine_table,
        ],
        axis=-1,
    )


def on_device(inputs, grad_context, gain, w_query, w_keyval):
    seq_length = inputs.shape[0]
    local_cols = inputs.shape[1]
    model_width = gain.shape[0]
    head_size = HD
    heads_here = HEADS_DEV
    group_cols = w_keyval.shape[1]
    query_cols = w_query.shape[1]
    tensor_count = lax.axis_size("tensor")
    keyval_total = group_cols * tensor_count
    kv_heads = KV_HEADS
    devices_per_group = tensor_count // kv_heads
    score_scale = head_size ** (-0.5)
    tensor_slot = lax.axis_index("tensor")
    gain_local = lax.dynamic_slice_in_dim(gain, tensor_slot * local_cols, local_cols, 0)
    split_cols = query_cols // 2
    engine_block = jnp.concatenate([w_query[:, :split_cols], w_keyval], axis=1)
    engine_full = lax.all_gather(engine_block, "dp", axis=0, tiled=True)
    ring_blocks_out, input_blocks = ring_gather(w_query[:, split_cols:], inputs, 6)
    ring_full = ring_blocks_out.reshape(-1, query_cols - split_cols)
    input_values = input_blocks.astype(jnp.float32)
    row_sum = jnp.sum(input_values * input_values, axis=(0, 2)).reshape(seq_length, 1)
    inv_rms = lax.rsqrt(row_sum / model_width + 1e-05)
    gain_blocks = gain.reshape(tensor_count, 1, local_cols)
    unit_blocks = input_values * inv_rms[None, :, :]
    normed_blocks = (unit_blocks * gain_blocks).astype(jnp.bfloat16)
    normed_full = normed_blocks.transpose(1, 0, 2).reshape(seq_length, model_width)
    unit_rows = inputs.astype(jnp.float32) * inv_rms
    engine_proj = jnp.dot(normed_full, engine_full, preferred_element_type=jnp.float32).astype(
        jnp.bfloat16
    )
    ring_proj = jnp.dot(normed_full, ring_full, preferred_element_type=jnp.float32).astype(
        jnp.bfloat16
    )
    query_proj = jnp.concatenate([engine_proj[:, :split_cols], ring_proj], axis=1)
    keyval_part = engine_proj[:, split_cols:]
    keyval_pieces = group_exchange(keyval_routes, keyval_part[None], 4, 1)
    key_block = jnp.concatenate([keyval_pieces[0], keyval_pieces[1]], axis=1)
    value_block = jnp.concatenate([keyval_pieces[2], keyval_pieces[3]], axis=1)
    cosine_table, sine_table = rope_tables(seq_length, head_size)
    cos_heads = cosine_table[:, None, :]
    sin_heads = sine_table[:, None, :]
    query_heads = query_proj.astype(jnp.float32).reshape(seq_length, heads_here, head_size)
    q_rot = rotate(query_heads, cos_heads, sin_heads).astype(jnp.bfloat16)
    k_rot = rotate(key_block.astype(jnp.float32), cosine_table, sine_table).astype(jnp.bfloat16)
    scores = (
        jnp.einsum("shd,td->hst", q_rot, k_rot, preferred_element_type=jnp.float32) * score_scale
    )
    causal = lax.broadcasted_iota(jnp.int32, (seq_length, seq_length), 0) >= lax.broadcasted_iota(
        jnp.int32, (seq_length, seq_length), 1
    )
    exponent = jnp.where(causal[None, :, :], jnp.exp(scores), 0.0)
    softmax_probs = exponent / jnp.sum(exponent, axis=2, keepdims=True)
    prob_weights = softmax_probs.astype(jnp.bfloat16)
    context = jnp.einsum(
        "hst,td->shd", prob_weights, value_block, preferred_element_type=jnp.float32
    ).astype(jnp.bfloat16)
    grad_ctx = grad_context.reshape(seq_length, heads_here, head_size)
    grad_probs = jnp.einsum(
        "shd,td->hst", grad_ctx, value_block, preferred_element_type=jnp.float32
    )
    row_delta = jnp.sum(grad_ctx.astype(jnp.float32) * context.astype(jnp.float32), axis=2).T[
        :, :, None
    ]
    grad_scores = (softmax_probs * (grad_probs - row_delta) * score_scale).astype(jnp.bfloat16)
    grad_qrot = jnp.einsum("hst,td->shd", grad_scores, k_rot, preferred_element_type=jnp.float32)
    grad_krot = jnp.einsum("hst,shd->td", grad_scores, q_rot, preferred_element_type=jnp.float32)
    grad_value = jnp.einsum(
        "hst,shd->td", prob_weights, grad_ctx, preferred_element_type=jnp.float32
    )
    grad_query = (
        unrotate(grad_qrot, cos_heads, sin_heads)
        .astype(jnp.bfloat16)
        .reshape(seq_length, heads_here * head_size)
    )
    grad_key = unrotate(grad_krot, cosine_table, sine_table)
    term_blocks = jnp.stack(
        [grad_key[:, :group_cols], grad_key[:, group_cols:], grad_value[:, :group_cols], grad_value[:, group_cols:]]
    )
    keyval_terms = group_exchange(term_routes, term_blocks, 4, 2)
    grad_keyval = jnp.sum(keyval_terms, axis=0).astype(jnp.bfloat16)
    engine_blocks = engine_full.reshape(tensor_count, local_cols, split_cols + group_cols)
    ring_blocks = ring_full.reshape(tensor_count, local_cols, query_cols - split_cols)
    engine_grads = jnp.concatenate([grad_query[:, :split_cols], grad_keyval], axis=1)
    normed_terms = (
        jnp.einsum("rc,pkc->prk", engine_grads, engine_blocks, preferred_element_type=jnp.float32)
        + jnp.einsum(
            "rc,pkc->prk",
            grad_query[:, split_cols:],
            ring_blocks,
            preferred_element_type=jnp.float32,
        )
    ).astype(jnp.bfloat16)
    product_part = jnp.sum(
        normed_terms.astype(jnp.float32) * gain_blocks * unit_blocks, axis=(0, 2)
    ).reshape(1, seq_length)
    dp_count = lax.axis_size("dp")
    pair_count = 2
    ring_count = dp_count // pair_count
    block_rows = model_width // dp_count
    normed_pairs = normed_full.reshape(seq_length, pair_count, ring_count, block_rows // 2, 2)
    zero_cols = jnp.zeros_like(grad_keyval)
    paired_grads = jnp.stack(
        [
            jnp.concatenate([grad_keyval, zero_cols], axis=1),
            jnp.concatenate([zero_cols, grad_keyval], axis=1),
        ],
        axis=1,
    )
    keyval_partials = jnp.stack(
        [
            jnp.einsum(
                "rbqt,rtc->bqc",
                normed_pairs[:, pair],
                paired_grads,
                preferred_element_type=jnp.float32,
            )
            for pair in range(pair_count)
        ],
        axis=1,
    ).reshape(model_width // 2, 2 * group_cols)
    ring_groups = [
        [pair * ring_count + slot for slot in range(ring_count)] for pair in range(pair_count)
    ]
    ring_sums = lax.psum_scatter(
        keyval_partials, "dp", scatter_dimension=0, tiled=True, axis_index_groups=ring_groups
    )
    normed_sums, product_parts = exchange(
        "tensor", [normed_terms, product_part], [True, False], 3
    )
    grad_normed = jnp.sum(normed_sums.astype(jnp.float32), axis=0)
    product_sum = jnp.sum(product_parts, axis=0).reshape(seq_length, 1)
    scaled_grad = grad_normed * gain_local
    grad_input = (inv_rms * (scaled_grad - unit_rows * (product_sum / model_width))).astype(
        jnp.bfloat16
    )
    gain_part = jnp.sum(grad_normed * unit_rows, axis=0).reshape(1, local_cols)
    (gain_parts,) = exchange("dp", [gain_part], [False], 4)
    grad_gain = jnp.sum(gain_parts, axis=(0, 1))
    lane_rows = ring_sums.size // (pair_count * 128)
    keyval_sums = pair_sum(ring_sums.reshape(pair_count, lane_rows, 128), ring_count, 7)
    keyval_weight_grad = keyval_sums.reshape(-1, group_cols)
    return (grad_input, grad_gain, keyval_weight_grad.astype(jnp.bfloat16))


def solution(mesh):
    in_specs = (P("dp", "tensor"), P("dp", "tensor"), P(), P("dp", "tensor"), P("dp", "tensor"))
    out_specs = (P("dp", "tensor"), P("tensor"), P("dp", "tensor"))
    return jax.shard_map(
        on_device, mesh=mesh, in_specs=in_specs, out_specs=out_specs, check_vma=False
    )
```

```python
import functools
import math

import jax
import jax.numpy as jnp
from jax import lax
from jax.experimental import pallas as pl
from jax.experimental.pallas import tpu as pltpu
from jax.sharding import PartitionSpec as P

MESH = pl.DeviceIdType.MESH


def exchange_kernel(axes, sizes, per_peer, *refs):
    count = len(per_peer)
    src_refs = refs[:count]
    out_refs = refs[count : 2 * count]
    send_sems, recv_sems = refs[2 * count :]
    barrier = pltpu.get_barrier_semaphore()
    waits = 0
    for axis in dict.fromkeys(axes):
        n = sizes[axes.index(axis)]
        me = lax.axis_index(axis)
        for step in range(1, n):
            peer = lax.rem(me + step, n)
            pl.semaphore_signal(barrier, inc=1, device_id={axis: peer}, device_id_type=MESH)
        waits += n - 1
    pl.semaphore_wait(barrier, waits)
    copies = []
    for index in range(count):
        axis, n = axes[index], sizes[index]
        me = lax.axis_index(axis)
        for step in range(1, n):
            peer = lax.rem(me + step, n)
            source = src_refs[index].at[peer] if per_peer[index] else src_refs[index]
            copy = pltpu.make_async_remote_copy(
                src_ref=source,
                dst_ref=out_refs[index].at[me],
                send_sem=send_sems.at[index, step],
                recv_sem=recv_sems.at[index, step],
                device_id={axis: peer},
                device_id_type=MESH,
            )
            copy.start()
            copies.append(copy)
    for index in range(count):
        me = lax.axis_index(axes[index])
        own = src_refs[index][me] if per_peer[index] else src_refs[index][...]
        out_refs[index][me] = own
    for copy in copies:
        copy.wait_send()
    for copy in copies:
        copy.wait_recv()


def exchange_multi(items, collective_id):
    axes = tuple(axis for axis, _, _ in items)
    sizes = tuple(lax.axis_size(axis) for axis in axes)
    blocks = [block for _, block, _ in items]
    per_peer = tuple(spread for _, _, spread in items)
    out_shapes = []
    sent = 0
    for n, block, spread in zip(sizes, blocks, per_peer):
        shape = block.shape[1:] if spread else block.shape
        out_shapes.append(jax.ShapeDtypeStruct((n,) + tuple(shape), block.dtype))
        sent += block.size * block.dtype.itemsize * (1 if spread else n)
    count = len(blocks)
    return pl.pallas_call(
        functools.partial(exchange_kernel, axes, sizes, per_peer),
        out_shape=tuple(out_shapes),
        in_specs=[pl.BlockSpec(memory_space=pltpu.VMEM)] * count,
        out_specs=tuple(pl.BlockSpec(memory_space=pltpu.VMEM) for _ in range(count)),
        scratch_shapes=[
            pltpu.SemaphoreType.DMA((count, max(sizes))),
            pltpu.SemaphoreType.DMA((count, max(sizes))),
        ],
        compiler_params=pltpu.CompilerParams(collective_id=collective_id, has_side_effects=True),
        cost_estimate=pl.CostEstimate(flops=0, bytes_accessed=2 * sent, transcendentals=0),
    )(*blocks)


def exchange(axis, blocks, per_peer, collective_id):
    return exchange_multi([(axis, b, s) for b, s in zip(blocks, per_peer)], collective_id)


def ring_gather_kernel(
    pair_count, ring_count, side_count, block_ref, side_ref, out_ref, side_out, send_sems, recv_sems, side_send, side_recv
):
    pair_slot = lax.axis_index("dp") // ring_count
    ring_slot = lax.axis_index("dp") % ring_count
    partner = (1 - pair_slot) * ring_count + ring_slot
    right = pair_slot * ring_count + lax.rem(ring_slot + 1, ring_count)
    left = pair_slot * ring_count + lax.rem(ring_slot + ring_count - 1, ring_count)
    me = pair_slot * ring_count + ring_slot
    side_me = lax.axis_index("tensor")
    barrier = pltpu.get_barrier_semaphore()
    for peer in (partner, right, left):
        pl.semaphore_signal(barrier, inc=1, device_id={"dp": peer}, device_id_type=MESH)
    for step in range(1, side_count):
        peer = lax.rem(side_me + step, side_count)
        pl.semaphore_signal(barrier, inc=1, device_id={"tensor": peer}, device_id_type=MESH)
    pl.semaphore_wait(barrier, 3 + side_count - 1)
    side_copies = []
    for step in range(1, side_count):
        peer = lax.rem(side_me + step, side_count)
        copy = pltpu.make_async_remote_copy(
            src_ref=side_ref,
            dst_ref=side_out.at[side_me],
            send_sem=side_send.at[step],
            recv_sem=side_recv.at[step],
            device_id={"tensor": peer},
            device_id_type=MESH,
        )
        copy.start()
        side_copies.append(copy)
    swap = pltpu.make_async_remote_copy(
        src_ref=block_ref,
        dst_ref=out_ref.at[me],
        send_sem=send_sems.at[2, 0, 0],
        recv_sem=recv_sems.at[2, 0, 0],
        device_id={"dp": partner},
        device_id_type=MESH,
    )
    swap.start()
    own = pltpu.make_async_copy(block_ref, out_ref.at[me], send_sems.at[2, 1, 0])
    own.start()
    side_out[side_me] = side_ref[...]
    own.wait()
    swap.wait_send()
    swap.wait_recv()
    right_steps = ring_count // 2
    left_steps = ring_count - 1 - right_steps
    sent = []

    def send(direction, step, target, origin):
        copies = []
        for member in range(pair_count):
            slot = member * ring_count + origin
            copy = pltpu.make_async_remote_copy(
                src_ref=out_ref.at[slot],
                dst_ref=out_ref.at[slot],
                send_sem=send_sems.at[direction, step, member],
                recv_sem=recv_sems.at[direction, step, member],
                device_id={"dp": target},
                device_id_type=MESH,
            )
            copy.start()
            copies.append(copy)
        sent.extend(copies)
        return copies

    right_copies = send(0, 0, right, ring_slot)
    left_copies = send(1, 0, left, ring_slot) if left_steps > 0 else []
    for step in range(1, right_steps):
        for copy in right_copies:
            copy.wait_recv()
        origin = lax.rem(ring_slot + ring_count - step, ring_count)
        right_copies = send(0, step, right, origin)
        if step < left_steps:
            for copy in left_copies:
                copy.wait_recv()
            origin = lax.rem(ring_slot + step, ring_count)
            left_copies = send(1, step, left, origin)
    for copy in right_copies + left_copies:
        copy.wait_recv()
    for copy in sent + side_copies:
        copy.wait_send()
    for copy in side_copies:
        copy.wait_recv()


def ring_gather(block, side, collective_id):
    count = lax.axis_size("dp")
    side_count = lax.axis_size("tensor")
    pair_count = 2
    ring_count = count // pair_count
    sent = count * block.size * block.dtype.itemsize + side_count * side.size * side.dtype.itemsize
    return pl.pallas_call(
        functools.partial(ring_gather_kernel, pair_count, ring_count, side_count),
        out_shape=(
            jax.ShapeDtypeStruct((count,) + block.shape, block.dtype),
            jax.ShapeDtypeStruct((side_count,) + side.shape, side.dtype),
        ),
        in_specs=[pl.BlockSpec(memory_space=pltpu.VMEM)] * 2,
        out_specs=(pl.BlockSpec(memory_space=pltpu.VMEM), pl.BlockSpec(memory_space=pltpu.VMEM)),
        scratch_shapes=[
            pltpu.SemaphoreType.DMA((3, ring_count, pair_count)),
            pltpu.SemaphoreType.DMA((3, ring_count, pair_count)),
            pltpu.SemaphoreType.DMA((side_count,)),
            pltpu.SemaphoreType.DMA((side_count,)),
        ],
        compiler_params=pltpu.CompilerParams(
            collective_id=collective_id, has_side_effects=True, vmem_limit_bytes=48 * 1024 * 1024
        ),
        cost_estimate=pl.CostEstimate(flops=0, bytes_accessed=2 * sent, transcendentals=0),
    )(block, side)

def pair_sum_kernel(ring_count, block_ref, out_ref, landing, sems):
    pair_slot = lax.axis_index("dp") // ring_count
    ring_slot = lax.axis_index("dp") % ring_count
    partner = (1 - pair_slot) * ring_count + ring_slot
    barrier = pltpu.get_barrier_semaphore()
    pl.semaphore_signal(barrier, inc=1, device_id={"dp": partner}, device_id_type=MESH)
    pl.semaphore_wait(barrier, 1)
    copy = pltpu.make_async_remote_copy(
        src_ref=block_ref.at[1 - pair_slot],
        dst_ref=landing,
        send_sem=sems.at[0],
        recv_sem=sems.at[1],
        device_id={"dp": partner},
        device_id_type=MESH,
    )
    copy.start()
    copy.wait_send()
    copy.wait_recv()
    out_ref[...] = block_ref[pair_slot] + landing[...]


def pair_sum(blocks, ring_count, collective_id):
    return pl.pallas_call(
        functools.partial(pair_sum_kernel, ring_count),
        out_shape=jax.ShapeDtypeStruct(blocks.shape[1:], blocks.dtype),
        in_specs=[pl.BlockSpec(memory_space=pltpu.VMEM)],
        out_specs=pl.BlockSpec(memory_space=pltpu.VMEM),
        scratch_shapes=[pltpu.VMEM(blocks.shape[1:], blocks.dtype), pltpu.SemaphoreType.DMA((2,))],
        compiler_params=pltpu.CompilerParams(collective_id=collective_id, has_side_effects=True),
        cost_estimate=pl.CostEstimate(
            flops=0, bytes_accessed=3 * blocks.size * blocks.dtype.itemsize, transcendentals=0
        ),
    )(blocks)


def group_kernel(routes, src_ref, out_ref, send_sems, recv_sems):
    me = lax.axis_index("tensor")
    dests, sources = routes(me)
    barrier = pltpu.get_barrier_semaphore()
    count = jnp.int32(0)
    for peer in [d for d, _, _ in dests] + sources:

        @pl.when(peer != me)
        def _():
            pl.semaphore_signal(barrier, inc=1, device_id={"tensor": peer}, device_id_type=MESH)

        count = count + (peer != me).astype(jnp.int32)
    pl.semaphore_wait(barrier, count)
    copies = []
    for index, (peer, slot, block) in enumerate(dests):
        copy = pltpu.make_async_remote_copy(
            src_ref=src_ref.at[block],
            dst_ref=out_ref.at[slot],
            send_sem=send_sems.at[index],
            recv_sem=recv_sems.at[slot],
            device_id={"tensor": peer},
            device_id_type=MESH,
        )
        copies.append(copy)

        @pl.when(peer != me)
        def _():
            copy.start()

        @pl.when(peer == me)
        def _():
            out_ref[slot] = src_ref[block]

    for (peer, _, _), copy in zip(dests, copies):

        @pl.when(peer != me)
        def _():
            copy.wait_send()

    for slot, peer in enumerate(sources):
        arrival = pltpu.make_async_remote_copy(
            src_ref=src_ref.at[0],
            dst_ref=out_ref.at[slot],
            send_sem=send_sems.at[0],
            recv_sem=recv_sems.at[slot],
            device_id={"tensor": peer},
            device_id_type=MESH,
        )

        @pl.when(peer != me)
        def _():
            arrival.wait_recv()


def group_exchange(routes, blocks, slots, collective_id):
    return pl.pallas_call(
        functools.partial(group_kernel, routes),
        out_shape=jax.ShapeDtypeStruct((slots,) + blocks.shape[1:], blocks.dtype),
        in_specs=[pl.BlockSpec(memory_space=pltpu.VMEM)],
        out_specs=pl.BlockSpec(memory_space=pltpu.VMEM),
        scratch_shapes=[pltpu.SemaphoreType.DMA((slots,)), pltpu.SemaphoreType.DMA((slots,))],
        compiler_params=pltpu.CompilerParams(collective_id=collective_id, has_side_effects=True),
        cost_estimate=pl.CostEstimate(
            flops=0, bytes_accessed=2 * slots * blocks[0].size * blocks.dtype.itemsize, transcendentals=0
        ),
    )(blocks)


def keyval_routes(me):
    head_group = lax.rem(me // 2, KV_HEADS)
    slot = 2 * (me // (2 * KV_HEADS)) + lax.rem(me, 2)
    dests = [(KV_HEADS * head_group + m, slot, 0) for m in range(KV_HEADS)]
    group = me // KV_HEADS
    sources = [2 * group, 2 * group + 1, 2 * KV_HEADS + 2 * group, 2 * KV_HEADS + 2 * group + 1]
    return dests, sources


def term_routes(me):
    group = me // KV_HEADS
    slot = lax.rem(me, KV_HEADS)
    targets = [2 * group, 2 * group + 1, 2 * KV_HEADS + 2 * group, 2 * KV_HEADS + 2 * group + 1]
    dests = [(target, slot, m) for m, target in enumerate(targets)]
    head_group = lax.rem(me // 2, KV_HEADS)
    sources = [KV_HEADS * head_group + m for m in range(KV_HEADS)]
    return dests, sources


HD = 128
KV_HEADS = 4
HEADS_DEV = 4


def rope_tables(length, head_size):
    positions = lax.broadcasted_iota(jnp.int32, (length, head_size // 2), 0).astype(jnp.float32)
    index_half = lax.broadcasted_iota(jnp.int32, (length, head_size // 2), 1).astype(jnp.float32)
    frequency = jnp.exp(-(2.0 * index_half / head_size) * math.log(500000.0))
    angles = positions * frequency
    return (jnp.cos(angles), jnp.sin(angles))


def rotate(vectors, cosine_table, sine_table):
    half_size = vectors.shape[-1] // 2
    first_half = vectors[..., :half_size]
    second_half = vectors[..., half_size:]
    return jnp.concatenate(
        [
            first_half * cosine_table - second_half * sine_table,
            first_half * sine_table + second_half * cosine_table,
        ],
        axis=-1,
    )


def unrotate(vectors, cosine_table, sine_table):
    half_size = vectors.shape[-1] // 2
    first_half = vectors[..., :half_size]
    second_half = vectors[..., half_size:]
    return jnp.concatenate(
        [
            first_half * cosine_table + second_half * sine_table,
            second_half * cosine_table - first_half * sine_table,
        ],
        axis=-1,
    )


def on_device(inputs, grad_context, gain, w_query, w_keyval):
    seq_length = inputs.shape[0]
    local_cols = inputs.shape[1]
    model_width = gain.shape[0]
    head_size = HD
    heads_here = HEADS_DEV
    group_cols = w_keyval.shape[1]
    query_cols = w_query.shape[1]
    tensor_count = lax.axis_size("tensor")
    keyval_total = group_cols * tensor_count
    kv_heads = KV_HEADS
    devices_per_group = tensor_count // kv_heads
    score_scale = head_size ** (-0.5)
    tensor_slot = lax.axis_index("tensor")
    gain_local = lax.dynamic_slice_in_dim(gain, tensor_slot * local_cols, local_cols, 0)
    split_cols = query_cols // 2
    engine_block = jnp.concatenate([w_query[:, :split_cols], w_keyval], axis=1)
    engine_full = lax.all_gather(engine_block, "dp", axis=0, tiled=True)
    ring_blocks_out, input_blocks = ring_gather(w_query[:, split_cols:], inputs, 6)
    ring_full = ring_blocks_out.reshape(-1, query_cols - split_cols)
    input_values = input_blocks.astype(jnp.float32)
    row_sum = jnp.sum(input_values * input_values, axis=(0, 2)).reshape(seq_length, 1)
    inv_rms = lax.rsqrt(row_sum / model_width + 1e-05)
    gain_blocks = gain.reshape(tensor_count, 1, local_cols)
    unit_blocks = input_values * inv_rms[None, :, :]
    normed_blocks = (unit_blocks * gain_blocks).astype(jnp.bfloat16)
    normed_full = normed_blocks.transpose(1, 0, 2).reshape(seq_length, model_width)
    unit_rows = inputs.astype(jnp.float32) * inv_rms
    engine_proj = jnp.dot(normed_full, engine_full, preferred_element_type=jnp.float32).astype(
        jnp.bfloat16
    )
    ring_proj = jnp.dot(normed_full, ring_full, preferred_element_type=jnp.float32).astype(
        jnp.bfloat16
    )
    query_proj = jnp.concatenate([engine_proj[:, :split_cols], ring_proj], axis=1)
    keyval_part = engine_proj[:, split_cols:]
    keyval_pieces = group_exchange(keyval_routes, keyval_part[None], 4, 1)
    key_block = jnp.concatenate([keyval_pieces[0], keyval_pieces[1]], axis=1)
    value_block = jnp.concatenate([keyval_pieces[2], keyval_pieces[3]], axis=1)
    cosine_table, sine_table = rope_tables(seq_length, head_size)
    cos_heads = cosine_table[:, None, :]
    sin_heads = sine_table[:, None, :]
    query_heads = query_proj.astype(jnp.float32).reshape(seq_length, heads_here, head_size)
    q_rot = rotate(query_heads, cos_heads, sin_heads).astype(jnp.bfloat16)
    k_rot = rotate(key_block.astype(jnp.float32), cosine_table, sine_table).astype(jnp.bfloat16)
    scores = (
        jnp.einsum("shd,td->hst", q_rot, k_rot, preferred_element_type=jnp.float32) * score_scale
    )
    causal = lax.broadcasted_iota(jnp.int32, (seq_length, seq_length), 0) >= lax.broadcasted_iota(
        jnp.int32, (seq_length, seq_length), 1
    )
    exponent = jnp.where(causal[None, :, :], jnp.exp(scores), 0.0)
    softmax_probs = exponent / jnp.sum(exponent, axis=2, keepdims=True)
    prob_weights = softmax_probs.astype(jnp.bfloat16)
    context = jnp.einsum(
        "hst,td->shd", prob_weights, value_block, preferred_element_type=jnp.float32
    ).astype(jnp.bfloat16)
    grad_ctx = grad_context.reshape(seq_length, heads_here, head_size)
    grad_probs = jnp.einsum(
        "shd,td->hst", grad_ctx, value_block, preferred_element_type=jnp.float32
    )
    row_delta = jnp.sum(grad_ctx.astype(jnp.float32) * context.astype(jnp.float32), axis=2).T[
        :, :, None
    ]
    grad_scores = (softmax_probs * (grad_probs - row_delta) * score_scale).astype(jnp.bfloat16)
    grad_qrot = jnp.einsum("hst,td->shd", grad_scores, k_rot, preferred_element_type=jnp.float32)
    grad_krot = jnp.einsum("hst,shd->td", grad_scores, q_rot, preferred_element_type=jnp.float32)
    grad_value = jnp.einsum(
        "hst,shd->td", prob_weights, grad_ctx, preferred_element_type=jnp.float32
    )
    grad_query = (
        unrotate(grad_qrot, cos_heads, sin_heads)
        .astype(jnp.bfloat16)
        .reshape(seq_length, heads_here * head_size)
    )
    grad_key = unrotate(grad_krot, cosine_table, sine_table)
    term_blocks = jnp.stack(
        [grad_key[:, :group_cols], grad_key[:, group_cols:], grad_value[:, :group_cols], grad_value[:, group_cols:]]
    )
    keyval_terms = group_exchange(term_routes, term_blocks, 4, 2)
    grad_keyval = jnp.sum(keyval_terms, axis=0).astype(jnp.bfloat16)
    engine_blocks = engine_full.reshape(tensor_count, local_cols, split_cols + group_cols)
    ring_blocks = ring_full.reshape(tensor_count, local_cols, query_cols - split_cols)
    engine_grads = jnp.concatenate([grad_query[:, :split_cols], grad_keyval], axis=1)
    normed_terms = (
        jnp.einsum("rc,pkc->prk", engine_grads, engine_blocks, preferred_element_type=jnp.float32)
        + jnp.einsum(
            "rc,pkc->prk",
            grad_query[:, split_cols:],
            ring_blocks,
            preferred_element_type=jnp.float32,
        )
    ).astype(jnp.bfloat16)
    product_part = jnp.sum(
        normed_terms.astype(jnp.float32) * gain_blocks * unit_blocks, axis=(0, 2)
    ).reshape(1, seq_length)
    dp_count = lax.axis_size("dp")
    pair_count = 2
    ring_count = dp_count // pair_count
    block_rows = model_width // dp_count
    normed_pairs = normed_full.reshape(
        seq_length, pair_count, ring_count, block_rows // 2, 2
    ).transpose(0, 2, 1, 3, 4)
    keyval_partials = jnp.concatenate(
        [
            jnp.einsum(
                "rbaq,rc->baqc",
                normed_pairs[..., half],
                grad_keyval,
                preferred_element_type=jnp.float32,
            )
            for half in range(2)
        ],
        axis=-1,
    ).reshape(model_width // 2, 2 * group_cols).astype(jnp.bfloat16)
    ring_groups = [
        [pair * ring_count + slot for slot in range(ring_count)] for pair in range(pair_count)
    ]
    ring_sums = lax.psum_scatter(
        keyval_partials, "dp", scatter_dimension=0, tiled=True, axis_index_groups=ring_groups
    )
    normed_sums, product_parts = exchange(
        "tensor", [normed_terms, product_part], [True, False], 3
    )
    grad_normed = jnp.sum(normed_sums.astype(jnp.float32), axis=0)
    product_sum = jnp.sum(product_parts, axis=0).reshape(seq_length, 1)
    scaled_grad = grad_normed * gain_local
    grad_input = (inv_rms * (scaled_grad - unit_rows * (product_sum / model_width))).astype(
        jnp.bfloat16
    )
    gain_part = jnp.sum(grad_normed * unit_rows, axis=0).reshape(1, local_cols)
    (gain_parts,) = exchange("dp", [gain_part], [False], 4)
    grad_gain = jnp.sum(gain_parts, axis=(0, 1))
    lane_rows = ring_sums.size // (pair_count * 128)
    keyval_sums = pair_sum(
        ring_sums.astype(jnp.float32).reshape(pair_count, lane_rows, 128), ring_count, 7
    )
    keyval_weight_grad = keyval_sums.reshape(-1, group_cols)
    return (grad_input, grad_gain, keyval_weight_grad.astype(jnp.bfloat16))


def solution(mesh):
    in_specs = (P("dp", "tensor"), P("dp", "tensor"), P(), P("dp", "tensor"), P("dp", "tensor"))
    out_specs = (P("dp", "tensor"), P("tensor"), P("dp", "tensor"))
    return jax.shard_map(
        on_device, mesh=mesh, in_specs=in_specs, out_specs=out_specs, check_vma=False
    )
```

```python
import functools
import math

import jax
import jax.numpy as jnp
from jax import lax
from jax.experimental import pallas as pl
from jax.experimental.pallas import tpu as pltpu
from jax.sharding import PartitionSpec as P

MESH = pl.DeviceIdType.MESH


def exchange_kernel(axes, sizes, per_peer, *refs):
    count = len(per_peer)
    src_refs = refs[:count]
    out_refs = refs[count : 2 * count]
    send_sems, recv_sems = refs[2 * count :]
    barrier = pltpu.get_barrier_semaphore()
    waits = 0
    for axis in dict.fromkeys(axes):
        n = sizes[axes.index(axis)]
        me = lax.axis_index(axis)
        for step in range(1, n):
            peer = lax.rem(me + step, n)
            pl.semaphore_signal(barrier, inc=1, device_id={axis: peer}, device_id_type=MESH)
        waits += n - 1
    pl.semaphore_wait(barrier, waits)
    copies = []
    for index in range(count):
        axis, n = axes[index], sizes[index]
        me = lax.axis_index(axis)
        for step in range(1, n):
            peer = lax.rem(me + step, n)
            source = src_refs[index].at[peer] if per_peer[index] else src_refs[index]
            copy = pltpu.make_async_remote_copy(
                src_ref=source,
                dst_ref=out_refs[index].at[me],
                send_sem=send_sems.at[index, step],
                recv_sem=recv_sems.at[index, step],
                device_id={axis: peer},
                device_id_type=MESH,
            )
            copy.start()
            copies.append(copy)
    for index in range(count):
        me = lax.axis_index(axes[index])
        own = src_refs[index][me] if per_peer[index] else src_refs[index][...]
        out_refs[index][me] = own
    for copy in copies:
        copy.wait_send()
    for copy in copies:
        copy.wait_recv()


def exchange_multi(items, collective_id):
    axes = tuple(axis for axis, _, _ in items)
    sizes = tuple(lax.axis_size(axis) for axis in axes)
    blocks = [block for _, block, _ in items]
    per_peer = tuple(spread for _, _, spread in items)
    out_shapes = []
    sent = 0
    for n, block, spread in zip(sizes, blocks, per_peer):
        shape = block.shape[1:] if spread else block.shape
        out_shapes.append(jax.ShapeDtypeStruct((n,) + tuple(shape), block.dtype))
        sent += block.size * block.dtype.itemsize * (1 if spread else n)
    count = len(blocks)
    return pl.pallas_call(
        functools.partial(exchange_kernel, axes, sizes, per_peer),
        out_shape=tuple(out_shapes),
        in_specs=[pl.BlockSpec(memory_space=pltpu.VMEM)] * count,
        out_specs=tuple(pl.BlockSpec(memory_space=pltpu.VMEM) for _ in range(count)),
        scratch_shapes=[
            pltpu.SemaphoreType.DMA((count, max(sizes))),
            pltpu.SemaphoreType.DMA((count, max(sizes))),
        ],
        compiler_params=pltpu.CompilerParams(collective_id=collective_id, has_side_effects=True),
        cost_estimate=pl.CostEstimate(flops=0, bytes_accessed=2 * sent, transcendentals=0),
    )(*blocks)


def exchange(axis, blocks, per_peer, collective_id):
    return exchange_multi([(axis, b, s) for b, s in zip(blocks, per_peer)], collective_id)


def ring_gather_kernel(
    pair_count, ring_count, side_count, block_ref, side_ref, out_ref, side_out, send_sems, recv_sems, side_send, side_recv
):
    pair_slot = lax.axis_index("dp") // ring_count
    ring_slot = lax.axis_index("dp") % ring_count
    partner = (1 - pair_slot) * ring_count + ring_slot
    right = pair_slot * ring_count + lax.rem(ring_slot + 1, ring_count)
    left = pair_slot * ring_count + lax.rem(ring_slot + ring_count - 1, ring_count)
    me = pair_slot * ring_count + ring_slot
    side_me = lax.axis_index("tensor")
    barrier = pltpu.get_barrier_semaphore()
    for peer in (partner, right, left):
        pl.semaphore_signal(barrier, inc=1, device_id={"dp": peer}, device_id_type=MESH)
    for step in range(1, side_count):
        peer = lax.rem(side_me + step, side_count)
        pl.semaphore_signal(barrier, inc=1, device_id={"tensor": peer}, device_id_type=MESH)
    pl.semaphore_wait(barrier, 3 + side_count - 1)
    side_copies = []
    for step in range(1, side_count):
        peer = lax.rem(side_me + step, side_count)
        copy = pltpu.make_async_remote_copy(
            src_ref=side_ref,
            dst_ref=side_out.at[side_me],
            send_sem=side_send.at[step],
            recv_sem=side_recv.at[step],
            device_id={"tensor": peer},
            device_id_type=MESH,
        )
        copy.start()
        side_copies.append(copy)
    swap = pltpu.make_async_remote_copy(
        src_ref=block_ref,
        dst_ref=out_ref.at[me],
        send_sem=send_sems.at[2, 0, 0],
        recv_sem=recv_sems.at[2, 0, 0],
        device_id={"dp": partner},
        device_id_type=MESH,
    )
    swap.start()
    own = pltpu.make_async_copy(block_ref, out_ref.at[me], send_sems.at[2, 1, 0])
    own.start()
    side_out[side_me] = side_ref[...]
    own.wait()
    swap.wait_send()
    swap.wait_recv()
    right_steps = ring_count // 2
    left_steps = ring_count - 1 - right_steps
    sent = []

    def send(direction, step, target, origin):
        copies = []
        for member in range(pair_count):
            slot = member * ring_count + origin
            copy = pltpu.make_async_remote_copy(
                src_ref=out_ref.at[slot],
                dst_ref=out_ref.at[slot],
                send_sem=send_sems.at[direction, step, member],
                recv_sem=recv_sems.at[direction, step, member],
                device_id={"dp": target},
                device_id_type=MESH,
            )
            copy.start()
            copies.append(copy)
        sent.extend(copies)
        return copies

    right_copies = send(0, 0, right, ring_slot)
    left_copies = send(1, 0, left, ring_slot) if left_steps > 0 else []
    for step in range(1, right_steps):
        for copy in right_copies:
            copy.wait_recv()
        origin = lax.rem(ring_slot + ring_count - step, ring_count)
        right_copies = send(0, step, right, origin)
        if step < left_steps:
            for copy in left_copies:
                copy.wait_recv()
            origin = lax.rem(ring_slot + step, ring_count)
            left_copies = send(1, step, left, origin)
    for copy in right_copies + left_copies:
        copy.wait_recv()
    for copy in sent + side_copies:
        copy.wait_send()
    for copy in side_copies:
        copy.wait_recv()


def ring_gather(block, side, collective_id):
    count = lax.axis_size("dp")
    side_count = lax.axis_size("tensor")
    pair_count = 2
    ring_count = count // pair_count
    sent = count * block.size * block.dtype.itemsize + side_count * side.size * side.dtype.itemsize
    return pl.pallas_call(
        functools.partial(ring_gather_kernel, pair_count, ring_count, side_count),
        out_shape=(
            jax.ShapeDtypeStruct((count,) + block.shape, block.dtype),
            jax.ShapeDtypeStruct((side_count,) + side.shape, side.dtype),
        ),
        in_specs=[pl.BlockSpec(memory_space=pltpu.VMEM)] * 2,
        out_specs=(pl.BlockSpec(memory_space=pltpu.VMEM), pl.BlockSpec(memory_space=pltpu.VMEM)),
        scratch_shapes=[
            pltpu.SemaphoreType.DMA((3, ring_count, pair_count)),
            pltpu.SemaphoreType.DMA((3, ring_count, pair_count)),
            pltpu.SemaphoreType.DMA((side_count,)),
            pltpu.SemaphoreType.DMA((side_count,)),
        ],
        compiler_params=pltpu.CompilerParams(
            collective_id=collective_id, has_side_effects=True, vmem_limit_bytes=48 * 1024 * 1024
        ),
        cost_estimate=pl.CostEstimate(flops=0, bytes_accessed=2 * sent, transcendentals=0),
    )(block, side)

def pair_sum_kernel(ring_count, block_ref, out_ref, landing, sems):
    pair_slot = lax.axis_index("dp") // ring_count
    ring_slot = lax.axis_index("dp") % ring_count
    partner = (1 - pair_slot) * ring_count + ring_slot
    barrier = pltpu.get_barrier_semaphore()
    pl.semaphore_signal(barrier, inc=1, device_id={"dp": partner}, device_id_type=MESH)
    pl.semaphore_wait(barrier, 1)
    copy = pltpu.make_async_remote_copy(
        src_ref=block_ref.at[1 - pair_slot],
        dst_ref=landing,
        send_sem=sems.at[0],
        recv_sem=sems.at[1],
        device_id={"dp": partner},
        device_id_type=MESH,
    )
    copy.start()
    copy.wait_send()
    copy.wait_recv()
    out_ref[...] = block_ref[pair_slot] + landing[...]


def pair_sum(blocks, ring_count, collective_id):
    return pl.pallas_call(
        functools.partial(pair_sum_kernel, ring_count),
        out_shape=jax.ShapeDtypeStruct(blocks.shape[1:], blocks.dtype),
        in_specs=[pl.BlockSpec(memory_space=pltpu.VMEM)],
        out_specs=pl.BlockSpec(memory_space=pltpu.VMEM),
        scratch_shapes=[pltpu.VMEM(blocks.shape[1:], blocks.dtype), pltpu.SemaphoreType.DMA((2,))],
        compiler_params=pltpu.CompilerParams(collective_id=collective_id, has_side_effects=True),
        cost_estimate=pl.CostEstimate(
            flops=0, bytes_accessed=3 * blocks.size * blocks.dtype.itemsize, transcendentals=0
        ),
    )(blocks)


def group_kernel(routes, src_ref, out_ref, send_sems, recv_sems):
    me = lax.axis_index("tensor")
    dests, sources = routes(me)
    barrier = pltpu.get_barrier_semaphore()
    count = jnp.int32(0)
    for peer in [d for d, _, _ in dests] + sources:

        @pl.when(peer != me)
        def _():
            pl.semaphore_signal(barrier, inc=1, device_id={"tensor": peer}, device_id_type=MESH)

        count = count + (peer != me).astype(jnp.int32)
    pl.semaphore_wait(barrier, count)
    copies = []
    for index, (peer, slot, block) in enumerate(dests):
        copy = pltpu.make_async_remote_copy(
            src_ref=src_ref.at[block],
            dst_ref=out_ref.at[slot],
            send_sem=send_sems.at[index],
            recv_sem=recv_sems.at[slot],
            device_id={"tensor": peer},
            device_id_type=MESH,
        )
        copies.append(copy)

        @pl.when(peer != me)
        def _():
            copy.start()

        @pl.when(peer == me)
        def _():
            out_ref[slot] = src_ref[block]

    for (peer, _, _), copy in zip(dests, copies):

        @pl.when(peer != me)
        def _():
            copy.wait_send()

    for slot, peer in enumerate(sources):
        arrival = pltpu.make_async_remote_copy(
            src_ref=src_ref.at[0],
            dst_ref=out_ref.at[slot],
            send_sem=send_sems.at[0],
            recv_sem=recv_sems.at[slot],
            device_id={"tensor": peer},
            device_id_type=MESH,
        )

        @pl.when(peer != me)
        def _():
            arrival.wait_recv()


def group_exchange(routes, blocks, slots, collective_id):
    return pl.pallas_call(
        functools.partial(group_kernel, routes),
        out_shape=jax.ShapeDtypeStruct((slots,) + blocks.shape[1:], blocks.dtype),
        in_specs=[pl.BlockSpec(memory_space=pltpu.VMEM)],
        out_specs=pl.BlockSpec(memory_space=pltpu.VMEM),
        scratch_shapes=[pltpu.SemaphoreType.DMA((slots,)), pltpu.SemaphoreType.DMA((slots,))],
        compiler_params=pltpu.CompilerParams(collective_id=collective_id, has_side_effects=True),
        cost_estimate=pl.CostEstimate(
            flops=0, bytes_accessed=2 * slots * blocks[0].size * blocks.dtype.itemsize, transcendentals=0
        ),
    )(blocks)


def keyval_routes(me):
    head_group = lax.rem(me // 2, KV_HEADS)
    slot = 2 * (me // (2 * KV_HEADS)) + lax.rem(me, 2)
    dests = [(KV_HEADS * head_group + m, slot, 0) for m in range(KV_HEADS)]
    group = me // KV_HEADS
    sources = [2 * group, 2 * group + 1, 2 * KV_HEADS + 2 * group, 2 * KV_HEADS + 2 * group + 1]
    return dests, sources


def term_routes(me):
    group = me // KV_HEADS
    slot = lax.rem(me, KV_HEADS)
    targets = [2 * group, 2 * group + 1, 2 * KV_HEADS + 2 * group, 2 * KV_HEADS + 2 * group + 1]
    dests = [(target, slot, m) for m, target in enumerate(targets)]
    head_group = lax.rem(me // 2, KV_HEADS)
    sources = [KV_HEADS * head_group + m for m in range(KV_HEADS)]
    return dests, sources


def gain_kernel(ring_count, part_ref, out_ref, send_sems, recv_sems):
    pair_slot = lax.axis_index("dp") // ring_count
    ring_slot = lax.axis_index("dp") % ring_count
    me = pair_slot * ring_count + ring_slot
    partner = (1 - pair_slot) * ring_count + ring_slot
    peers = [pair_slot * ring_count + lax.rem(ring_slot + step, ring_count) for step in range(1, ring_count)]
    barrier = pltpu.get_barrier_semaphore()
    for peer in [partner] + peers:
        pl.semaphore_signal(barrier, inc=1, device_id={"dp": peer}, device_id_type=MESH)
    pl.semaphore_wait(barrier, ring_count)
    swap = pltpu.make_async_remote_copy(
        src_ref=part_ref,
        dst_ref=out_ref.at[me],
        send_sem=send_sems.at[0, 0],
        recv_sem=recv_sems.at[0, 0],
        device_id={"dp": partner},
        device_id_type=MESH,
    )
    swap.start()
    copies = []
    for index, peer in enumerate(peers):
        copy = pltpu.make_async_remote_copy(
            src_ref=part_ref,
            dst_ref=out_ref.at[me],
            send_sem=send_sems.at[1, index],
            recv_sem=recv_sems.at[1, index],
            device_id={"dp": peer},
            device_id_type=MESH,
        )
        copy.start()
        copies.append(copy)
    out_ref[me] = part_ref[...]
    swap.wait_send()
    swap.wait_recv()
    for index, peer in enumerate(peers):
        copy = pltpu.make_async_remote_copy(
            src_ref=out_ref.at[partner],
            dst_ref=out_ref.at[partner],
            send_sem=send_sems.at[2, index],
            recv_sem=recv_sems.at[2, index],
            device_id={"dp": peer},
            device_id_type=MESH,
        )
        copy.start()
        copies.append(copy)
    for copy in copies:
        copy.wait_send()
    for copy in copies:
        copy.wait_recv()


def gain_allgather(part, collective_id):
    count = lax.axis_size("dp")
    ring_count = count // 2
    return pl.pallas_call(
        functools.partial(gain_kernel, ring_count),
        out_shape=jax.ShapeDtypeStruct((count,) + part.shape, part.dtype),
        in_specs=[pl.BlockSpec(memory_space=pltpu.VMEM)],
        out_specs=pl.BlockSpec(memory_space=pltpu.VMEM),
        scratch_shapes=[pltpu.SemaphoreType.DMA((3, ring_count)), pltpu.SemaphoreType.DMA((3, ring_count))],
        compiler_params=pltpu.CompilerParams(collective_id=collective_id, has_side_effects=True),
        cost_estimate=pl.CostEstimate(
            flops=0, bytes_accessed=4 * count * part.size * part.dtype.itemsize, transcendentals=0
        ),
    )(part)


HD = 128
KV_HEADS = 4
HEADS_DEV = 4


def rope_tables(length, head_size):
    positions = lax.broadcasted_iota(jnp.int32, (length, head_size // 2), 0).astype(jnp.float32)
    index_half = lax.broadcasted_iota(jnp.int32, (length, head_size // 2), 1).astype(jnp.float32)
    frequency = jnp.exp(-(2.0 * index_half / head_size) * math.log(500000.0))
    angles = positions * frequency
    return (jnp.cos(angles), jnp.sin(angles))


def rotate(vectors, cosine_table, sine_table):
    half_size = vectors.shape[-1] // 2
    first_half = vectors[..., :half_size]
    second_half = vectors[..., half_size:]
    return jnp.concatenate(
        [
            first_half * cosine_table - second_half * sine_table,
            first_half * sine_table + second_half * cosine_table,
        ],
        axis=-1,
    )


def unrotate(vectors, cosine_table, sine_table):
    half_size = vectors.shape[-1] // 2
    first_half = vectors[..., :half_size]
    second_half = vectors[..., half_size:]
    return jnp.concatenate(
        [
            first_half * cosine_table + second_half * sine_table,
            second_half * cosine_table - first_half * sine_table,
        ],
        axis=-1,
    )


def on_device(inputs, grad_context, gain, w_query, w_keyval):
    seq_length = inputs.shape[0]
    local_cols = inputs.shape[1]
    model_width = gain.shape[0]
    head_size = HD
    heads_here = HEADS_DEV
    group_cols = w_keyval.shape[1]
    query_cols = w_query.shape[1]
    tensor_count = lax.axis_size("tensor")
    keyval_total = group_cols * tensor_count
    kv_heads = KV_HEADS
    devices_per_group = tensor_count // kv_heads
    score_scale = head_size ** (-0.5)
    tensor_slot = lax.axis_index("tensor")
    gain_local = lax.dynamic_slice_in_dim(gain, tensor_slot * local_cols, local_cols, 0)
    split_cols = query_cols // 2
    engine_block = jnp.concatenate([w_query[:, :split_cols], w_keyval], axis=1)
    engine_full = lax.all_gather(engine_block, "dp", axis=0, tiled=True)
    ring_blocks_out, input_blocks = ring_gather(w_query[:, split_cols:], inputs, 6)
    ring_full = ring_blocks_out.reshape(-1, query_cols - split_cols)
    input_values = input_blocks.astype(jnp.float32)
    row_sum = jnp.sum(input_values * input_values, axis=(0, 2)).reshape(seq_length, 1)
    inv_rms = lax.rsqrt(row_sum / model_width + 1e-05)
    gain_blocks = gain.reshape(tensor_count, 1, local_cols)
    unit_blocks = input_values * inv_rms[None, :, :]
    normed_blocks = (unit_blocks * gain_blocks).astype(jnp.bfloat16)
    normed_full = normed_blocks.transpose(1, 0, 2).reshape(seq_length, model_width)
    unit_rows = inputs.astype(jnp.float32) * inv_rms
    engine_proj = jnp.dot(normed_full, engine_full, preferred_element_type=jnp.float32).astype(
        jnp.bfloat16
    )
    ring_proj = jnp.dot(normed_full, ring_full, preferred_element_type=jnp.float32).astype(
        jnp.bfloat16
    )
    query_proj = jnp.concatenate([engine_proj[:, :split_cols], ring_proj], axis=1)
    keyval_part = engine_proj[:, split_cols:]
    keyval_pieces = group_exchange(keyval_routes, keyval_part[None], 4, 1)
    key_block = jnp.concatenate([keyval_pieces[0], keyval_pieces[1]], axis=1)
    value_block = jnp.concatenate([keyval_pieces[2], keyval_pieces[3]], axis=1)
    cosine_table, sine_table = rope_tables(seq_length, head_size)
    cos_heads = cosine_table[:, None, :]
    sin_heads = sine_table[:, None, :]
    query_heads = query_proj.astype(jnp.float32).reshape(seq_length, heads_here, head_size)
    q_rot = rotate(query_heads, cos_heads, sin_heads).astype(jnp.bfloat16)
    k_rot = rotate(key_block.astype(jnp.float32), cosine_table, sine_table).astype(jnp.bfloat16)
    scores = (
        jnp.einsum("shd,td->hst", q_rot, k_rot, preferred_element_type=jnp.float32) * score_scale
    )
    causal = lax.broadcasted_iota(jnp.int32, (seq_length, seq_length), 0) >= lax.broadcasted_iota(
        jnp.int32, (seq_length, seq_length), 1
    )
    exponent = jnp.where(causal[None, :, :], jnp.exp(scores), 0.0)
    softmax_probs = exponent / jnp.sum(exponent, axis=2, keepdims=True)
    prob_weights = softmax_probs.astype(jnp.bfloat16)
    context = jnp.einsum(
        "hst,td->shd", prob_weights, value_block, preferred_element_type=jnp.float32
    ).astype(jnp.bfloat16)
    grad_ctx = grad_context.reshape(seq_length, heads_here, head_size)
    grad_probs = jnp.einsum(
        "shd,td->hst", grad_ctx, value_block, preferred_element_type=jnp.float32
    )
    row_delta = jnp.sum(grad_ctx.astype(jnp.float32) * context.astype(jnp.float32), axis=2).T[
        :, :, None
    ]
    grad_scores = (softmax_probs * (grad_probs - row_delta) * score_scale).astype(jnp.bfloat16)
    grad_qrot = jnp.einsum("hst,td->shd", grad_scores, k_rot, preferred_element_type=jnp.float32)
    grad_krot = jnp.einsum("hst,shd->td", grad_scores, q_rot, preferred_element_type=jnp.float32)
    grad_value = jnp.einsum(
        "hst,shd->td", prob_weights, grad_ctx, preferred_element_type=jnp.float32
    )
    grad_query = (
        unrotate(grad_qrot, cos_heads, sin_heads)
        .astype(jnp.bfloat16)
        .reshape(seq_length, heads_here * head_size)
    )
    grad_key = unrotate(grad_krot, cosine_table, sine_table)
    term_blocks = jnp.stack(
        [grad_key[:, :group_cols], grad_key[:, group_cols:], grad_value[:, :group_cols], grad_value[:, group_cols:]]
    )
    keyval_terms = group_exchange(term_routes, term_blocks, 4, 2)
    grad_keyval = jnp.sum(keyval_terms, axis=0).astype(jnp.bfloat16)
    engine_blocks = engine_full.reshape(tensor_count, local_cols, split_cols + group_cols)
    ring_blocks = ring_full.reshape(tensor_count, local_cols, query_cols - split_cols)
    engine_grads = jnp.concatenate([grad_query[:, :split_cols], grad_keyval], axis=1)
    normed_terms = (
        jnp.einsum("rc,pkc->prk", engine_grads, engine_blocks, preferred_element_type=jnp.float32)
        + jnp.einsum(
            "rc,pkc->prk",
            grad_query[:, split_cols:],
            ring_blocks,
            preferred_element_type=jnp.float32,
        )
    ).astype(jnp.bfloat16)
    product_part = jnp.sum(
        normed_terms.astype(jnp.float32) * gain_blocks * unit_blocks, axis=(0, 2)
    ).reshape(1, seq_length)
    dp_count = lax.axis_size("dp")
    pair_count = 2
    ring_count = dp_count // pair_count
    block_rows = model_width // dp_count
    normed_pairs = normed_full.reshape(
        seq_length, pair_count, ring_count, block_rows // 2, 2
    ).transpose(0, 2, 1, 3, 4)
    keyval_partials = jnp.concatenate(
        [
            jnp.einsum(
                "rbaq,rc->baqc",
                normed_pairs[..., half],
                grad_keyval,
                preferred_element_type=jnp.float32,
            )
            for half in range(2)
        ],
        axis=-1,
    ).reshape(model_width // 2, 2 * group_cols)
    ring_groups = [
        [pair * ring_count + slot for slot in range(ring_count)] for pair in range(pair_count)
    ]
    ring_sums = lax.psum_scatter(
        keyval_partials, "dp", scatter_dimension=0, tiled=True, axis_index_groups=ring_groups
    )
    normed_sums, product_parts = exchange(
        "tensor", [normed_terms, product_part], [True, False], 3
    )
    grad_normed = jnp.sum(normed_sums.astype(jnp.float32), axis=0)
    product_sum = jnp.sum(product_parts, axis=0).reshape(seq_length, 1)
    scaled_grad = grad_normed * gain_local
    grad_input = (inv_rms * (scaled_grad - unit_rows * (product_sum / model_width))).astype(
        jnp.bfloat16
    )
    gain_part = jnp.sum(grad_normed * unit_rows, axis=0).reshape(1, local_cols)
    gain_parts = gain_allgather(gain_part, 4)
    grad_gain = jnp.sum(gain_parts, axis=(0, 1))
    lane_rows = ring_sums.size // (pair_count * 128)
    keyval_sums = pair_sum(ring_sums.reshape(pair_count, lane_rows, 128), ring_count, 7)
    keyval_weight_grad = keyval_sums.reshape(-1, group_cols)
    return (grad_input, grad_gain, keyval_weight_grad.astype(jnp.bfloat16))


def solution(mesh):
    in_specs = (P("dp", "tensor"), P("dp", "tensor"), P(), P("dp", "tensor"), P("dp", "tensor"))
    out_specs = (P("dp", "tensor"), P("tensor"), P("dp", "tensor"))
    return jax.shard_map(
        on_device, mesh=mesh, in_specs=in_specs, out_specs=out_specs, check_vma=False
    )
```

```python
import functools
import math

import jax
import jax.numpy as jnp
from jax import lax
from jax.experimental import pallas as pl
from jax.experimental.pallas import tpu as pltpu
from jax.sharding import PartitionSpec as P

MESH = pl.DeviceIdType.MESH


def exchange_kernel(axes, sizes, per_peer, *refs):
    count = len(per_peer)
    src_refs = refs[:count]
    out_refs = refs[count : 2 * count]
    send_sems, recv_sems = refs[2 * count :]
    barrier = pltpu.get_barrier_semaphore()
    waits = 0
    for axis in dict.fromkeys(axes):
        n = sizes[axes.index(axis)]
        me = lax.axis_index(axis)
        for step in range(1, n):
            peer = lax.rem(me + step, n)
            pl.semaphore_signal(barrier, inc=1, device_id={axis: peer}, device_id_type=MESH)
        waits += n - 1
    pl.semaphore_wait(barrier, waits)
    copies = []
    for index in range(count):
        axis, n = axes[index], sizes[index]
        me = lax.axis_index(axis)
        for step in range(1, n):
            peer = lax.rem(me + step, n)
            source = src_refs[index].at[peer] if per_peer[index] else src_refs[index]
            copy = pltpu.make_async_remote_copy(
                src_ref=source,
                dst_ref=out_refs[index].at[me],
                send_sem=send_sems.at[index, step],
                recv_sem=recv_sems.at[index, step],
                device_id={axis: peer},
                device_id_type=MESH,
            )
            copy.start()
            copies.append(copy)
    for index in range(count):
        me = lax.axis_index(axes[index])
        own = src_refs[index][me] if per_peer[index] else src_refs[index][...]
        out_refs[index][me] = own
    for copy in copies:
        copy.wait_send()
    for copy in copies:
        copy.wait_recv()


def exchange_multi(items, collective_id):
    axes = tuple(axis for axis, _, _ in items)
    sizes = tuple(lax.axis_size(axis) for axis in axes)
    blocks = [block for _, block, _ in items]
    per_peer = tuple(spread for _, _, spread in items)
    out_shapes = []
    sent = 0
    for n, block, spread in zip(sizes, blocks, per_peer):
        shape = block.shape[1:] if spread else block.shape
        out_shapes.append(jax.ShapeDtypeStruct((n,) + tuple(shape), block.dtype))
        sent += block.size * block.dtype.itemsize * (1 if spread else n)
    count = len(blocks)
    return pl.pallas_call(
        functools.partial(exchange_kernel, axes, sizes, per_peer),
        out_shape=tuple(out_shapes),
        in_specs=[pl.BlockSpec(memory_space=pltpu.VMEM)] * count,
        out_specs=tuple(pl.BlockSpec(memory_space=pltpu.VMEM) for _ in range(count)),
        scratch_shapes=[
            pltpu.SemaphoreType.DMA((count, max(sizes))),
            pltpu.SemaphoreType.DMA((count, max(sizes))),
        ],
        compiler_params=pltpu.CompilerParams(collective_id=collective_id, has_side_effects=True),
        cost_estimate=pl.CostEstimate(flops=0, bytes_accessed=2 * sent, transcendentals=0),
    )(*blocks)


def exchange(axis, blocks, per_peer, collective_id):
    return exchange_multi([(axis, b, s) for b, s in zip(blocks, per_peer)], collective_id)


def ring_gather_kernel(
    pair_count, ring_count, side_count, block_ref, side_ref, out_ref, side_out, send_sems, recv_sems, side_send, side_recv
):
    pair_slot = lax.axis_index("dp") // ring_count
    ring_slot = lax.axis_index("dp") % ring_count
    partner = (1 - pair_slot) * ring_count + ring_slot
    right = pair_slot * ring_count + lax.rem(ring_slot + 1, ring_count)
    left = pair_slot * ring_count + lax.rem(ring_slot + ring_count - 1, ring_count)
    me = pair_slot * ring_count + ring_slot
    side_me = lax.axis_index("tensor")
    barrier = pltpu.get_barrier_semaphore()
    for peer in (partner, right, left):
        pl.semaphore_signal(barrier, inc=1, device_id={"dp": peer}, device_id_type=MESH)
    for step in range(1, side_count):
        peer = lax.rem(side_me + step, side_count)
        pl.semaphore_signal(barrier, inc=1, device_id={"tensor": peer}, device_id_type=MESH)
    pl.semaphore_wait(barrier, 3 + side_count - 1)
    swap = pltpu.make_async_remote_copy(
        src_ref=block_ref,
        dst_ref=out_ref.at[me],
        send_sem=send_sems.at[2, 0, 0],
        recv_sem=recv_sems.at[2, 0, 0],
        device_id={"dp": partner},
        device_id_type=MESH,
    )
    swap.start()
    own = pltpu.make_async_copy(block_ref, out_ref.at[me], send_sems.at[2, 1, 0])
    own.start()
    side_out[side_me] = side_ref[...]
    own.wait()
    swap.wait_send()
    swap.wait_recv()
    right_steps = ring_count // 2
    left_steps = ring_count - 1 - right_steps
    sent = []

    def send(direction, step, target, origin):
        copies = []
        for member in range(pair_count):
            slot = member * ring_count + origin
            copy = pltpu.make_async_remote_copy(
                src_ref=out_ref.at[slot],
                dst_ref=out_ref.at[slot],
                send_sem=send_sems.at[direction, step, member],
                recv_sem=recv_sems.at[direction, step, member],
                device_id={"dp": target},
                device_id_type=MESH,
            )
            copy.start()
            copies.append(copy)
        sent.extend(copies)
        return copies

    right_copies = send(0, 0, right, ring_slot)
    left_copies = send(1, 0, left, ring_slot) if left_steps > 0 else []
    side_copies = []
    for step in range(1, side_count):
        peer = lax.rem(side_me + step, side_count)
        copy = pltpu.make_async_remote_copy(
            src_ref=side_ref,
            dst_ref=side_out.at[side_me],
            send_sem=side_send.at[step],
            recv_sem=side_recv.at[step],
            device_id={"tensor": peer},
            device_id_type=MESH,
        )
        copy.start()
        side_copies.append(copy)
    for step in range(1, right_steps):
        for copy in right_copies:
            copy.wait_recv()
        origin = lax.rem(ring_slot + ring_count - step, ring_count)
        right_copies = send(0, step, right, origin)
        if step < left_steps:
            for copy in left_copies:
                copy.wait_recv()
            origin = lax.rem(ring_slot + step, ring_count)
            left_copies = send(1, step, left, origin)
    for copy in right_copies + left_copies:
        copy.wait_recv()
    for copy in sent + side_copies:
        copy.wait_send()
    for copy in side_copies:
        copy.wait_recv()


def ring_gather(block, side, collective_id):
    count = lax.axis_size("dp")
    side_count = lax.axis_size("tensor")
    pair_count = 2
    ring_count = count // pair_count
    sent = count * block.size * block.dtype.itemsize + side_count * side.size * side.dtype.itemsize
    return pl.pallas_call(
        functools.partial(ring_gather_kernel, pair_count, ring_count, side_count),
        out_shape=(
            jax.ShapeDtypeStruct((count,) + block.shape, block.dtype),
            jax.ShapeDtypeStruct((side_count,) + side.shape, side.dtype),
        ),
        in_specs=[pl.BlockSpec(memory_space=pltpu.VMEM)] * 2,
        out_specs=(pl.BlockSpec(memory_space=pltpu.VMEM), pl.BlockSpec(memory_space=pltpu.VMEM)),
        scratch_shapes=[
            pltpu.SemaphoreType.DMA((3, ring_count, pair_count)),
            pltpu.SemaphoreType.DMA((3, ring_count, pair_count)),
            pltpu.SemaphoreType.DMA((side_count,)),
            pltpu.SemaphoreType.DMA((side_count,)),
        ],
        compiler_params=pltpu.CompilerParams(
            collective_id=collective_id, has_side_effects=True, vmem_limit_bytes=48 * 1024 * 1024
        ),
        cost_estimate=pl.CostEstimate(flops=0, bytes_accessed=2 * sent, transcendentals=0),
    )(block, side)

def pair_sum_kernel(ring_count, block_ref, out_ref, landing, sems):
    pair_slot = lax.axis_index("dp") // ring_count
    ring_slot = lax.axis_index("dp") % ring_count
    partner = (1 - pair_slot) * ring_count + ring_slot
    barrier = pltpu.get_barrier_semaphore()
    pl.semaphore_signal(barrier, inc=1, device_id={"dp": partner}, device_id_type=MESH)
    pl.semaphore_wait(barrier, 1)
    copy = pltpu.make_async_remote_copy(
        src_ref=block_ref.at[1 - pair_slot],
        dst_ref=landing,
        send_sem=sems.at[0],
        recv_sem=sems.at[1],
        device_id={"dp": partner},
        device_id_type=MESH,
    )
    copy.start()
    copy.wait_send()
    copy.wait_recv()
    out_ref[...] = block_ref[pair_slot] + landing[...]


def pair_sum(blocks, ring_count, collective_id):
    return pl.pallas_call(
        functools.partial(pair_sum_kernel, ring_count),
        out_shape=jax.ShapeDtypeStruct(blocks.shape[1:], blocks.dtype),
        in_specs=[pl.BlockSpec(memory_space=pltpu.VMEM)],
        out_specs=pl.BlockSpec(memory_space=pltpu.VMEM),
        scratch_shapes=[pltpu.VMEM(blocks.shape[1:], blocks.dtype), pltpu.SemaphoreType.DMA((2,))],
        compiler_params=pltpu.CompilerParams(collective_id=collective_id, has_side_effects=True),
        cost_estimate=pl.CostEstimate(
            flops=0, bytes_accessed=3 * blocks.size * blocks.dtype.itemsize, transcendentals=0
        ),
    )(blocks)


def group_kernel(routes, src_ref, out_ref, send_sems, recv_sems):
    me = lax.axis_index("tensor")
    dests, sources = routes(me)
    barrier = pltpu.get_barrier_semaphore()
    count = jnp.int32(0)
    for peer in [d for d, _, _ in dests] + sources:

        @pl.when(peer != me)
        def _():
            pl.semaphore_signal(barrier, inc=1, device_id={"tensor": peer}, device_id_type=MESH)

        count = count + (peer != me).astype(jnp.int32)
    pl.semaphore_wait(barrier, count)
    copies = []
    for index, (peer, slot, block) in enumerate(dests):
        copy = pltpu.make_async_remote_copy(
            src_ref=src_ref.at[block],
            dst_ref=out_ref.at[slot],
            send_sem=send_sems.at[index],
            recv_sem=recv_sems.at[slot],
            device_id={"tensor": peer},
            device_id_type=MESH,
        )
        copies.append(copy)

        @pl.when(peer != me)
        def _():
            copy.start()

        @pl.when(peer == me)
        def _():
            out_ref[slot] = src_ref[block]

    for (peer, _, _), copy in zip(dests, copies):

        @pl.when(peer != me)
        def _():
            copy.wait_send()

    for slot, peer in enumerate(sources):
        arrival = pltpu.make_async_remote_copy(
            src_ref=src_ref.at[0],
            dst_ref=out_ref.at[slot],
            send_sem=send_sems.at[0],
            recv_sem=recv_sems.at[slot],
            device_id={"tensor": peer},
            device_id_type=MESH,
        )

        @pl.when(peer != me)
        def _():
            arrival.wait_recv()


def group_exchange(routes, blocks, slots, collective_id):
    return pl.pallas_call(
        functools.partial(group_kernel, routes),
        out_shape=jax.ShapeDtypeStruct((slots,) + blocks.shape[1:], blocks.dtype),
        in_specs=[pl.BlockSpec(memory_space=pltpu.VMEM)],
        out_specs=pl.BlockSpec(memory_space=pltpu.VMEM),
        scratch_shapes=[pltpu.SemaphoreType.DMA((slots,)), pltpu.SemaphoreType.DMA((slots,))],
        compiler_params=pltpu.CompilerParams(collective_id=collective_id, has_side_effects=True),
        cost_estimate=pl.CostEstimate(
            flops=0, bytes_accessed=2 * slots * blocks[0].size * blocks.dtype.itemsize, transcendentals=0
        ),
    )(blocks)


def keyval_routes(me):
    head_group = lax.rem(me // 2, KV_HEADS)
    slot = 2 * (me // (2 * KV_HEADS)) + lax.rem(me, 2)
    dests = [(KV_HEADS * head_group + m, slot, 0) for m in range(KV_HEADS)]
    group = me // KV_HEADS
    sources = [2 * group, 2 * group + 1, 2 * KV_HEADS + 2 * group, 2 * KV_HEADS + 2 * group + 1]
    return dests, sources


def term_routes(me):
    group = me // KV_HEADS
    slot = lax.rem(me, KV_HEADS)
    targets = [2 * group, 2 * group + 1, 2 * KV_HEADS + 2 * group, 2 * KV_HEADS + 2 * group + 1]
    dests = [(target, slot, m) for m, target in enumerate(targets)]
    head_group = lax.rem(me // 2, KV_HEADS)
    sources = [KV_HEADS * head_group + m for m in range(KV_HEADS)]
    return dests, sources


HD = 128
KV_HEADS = 4
HEADS_DEV = 4


def rope_tables(length, head_size):
    positions = lax.broadcasted_iota(jnp.int32, (length, head_size // 2), 0).astype(jnp.float32)
    index_half = lax.broadcasted_iota(jnp.int32, (length, head_size // 2), 1).astype(jnp.float32)
    frequency = jnp.exp(-(2.0 * index_half / head_size) * math.log(500000.0))
    angles = positions * frequency
    return (jnp.cos(angles), jnp.sin(angles))


def rotate(vectors, cosine_table, sine_table):
    half_size = vectors.shape[-1] // 2
    first_half = vectors[..., :half_size]
    second_half = vectors[..., half_size:]
    return jnp.concatenate(
        [
            first_half * cosine_table - second_half * sine_table,
            first_half * sine_table + second_half * cosine_table,
        ],
        axis=-1,
    )


def unrotate(vectors, cosine_table, sine_table):
    half_size = vectors.shape[-1] // 2
    first_half = vectors[..., :half_size]
    second_half = vectors[..., half_size:]
    return jnp.concatenate(
        [
            first_half * cosine_table + second_half * sine_table,
            second_half * cosine_table - first_half * sine_table,
        ],
        axis=-1,
    )


def on_device(inputs, grad_context, gain, w_query, w_keyval):
    seq_length = inputs.shape[0]
    local_cols = inputs.shape[1]
    model_width = gain.shape[0]
    head_size = HD
    heads_here = HEADS_DEV
    group_cols = w_keyval.shape[1]
    query_cols = w_query.shape[1]
    tensor_count = lax.axis_size("tensor")
    keyval_total = group_cols * tensor_count
    kv_heads = KV_HEADS
    devices_per_group = tensor_count // kv_heads
    score_scale = head_size ** (-0.5)
    tensor_slot = lax.axis_index("tensor")
    gain_local = lax.dynamic_slice_in_dim(gain, tensor_slot * local_cols, local_cols, 0)
    split_cols = query_cols // 2
    engine_block = jnp.concatenate([w_query[:, :split_cols], w_keyval], axis=1)
    engine_full = lax.all_gather(engine_block, "dp", axis=0, tiled=True)
    ring_blocks_out, input_blocks = ring_gather(w_query[:, split_cols:], inputs, 6)
    ring_full = ring_blocks_out.reshape(-1, query_cols - split_cols)
    input_values = input_blocks.astype(jnp.float32)
    row_sum = jnp.sum(input_values * input_values, axis=(0, 2)).reshape(seq_length, 1)
    inv_rms = lax.rsqrt(row_sum / model_width + 1e-05)
    gain_blocks = gain.reshape(tensor_count, 1, local_cols)
    unit_blocks = input_values * inv_rms[None, :, :]
    normed_blocks = (unit_blocks * gain_blocks).astype(jnp.bfloat16)
    normed_full = normed_blocks.transpose(1, 0, 2).reshape(seq_length, model_width)
    unit_rows = inputs.astype(jnp.float32) * inv_rms
    engine_proj = jnp.dot(normed_full, engine_full, preferred_element_type=jnp.float32).astype(
        jnp.bfloat16
    )
    ring_proj = jnp.dot(normed_full, ring_full, preferred_element_type=jnp.float32).astype(
        jnp.bfloat16
    )
    query_proj = jnp.concatenate([engine_proj[:, :split_cols], ring_proj], axis=1)
    keyval_part = engine_proj[:, split_cols:]
    keyval_pieces = group_exchange(keyval_routes, keyval_part[None], 4, 1)
    key_block = jnp.concatenate([keyval_pieces[0], keyval_pieces[1]], axis=1)
    value_block = jnp.concatenate([keyval_pieces[2], keyval_pieces[3]], axis=1)
    cosine_table, sine_table = rope_tables(seq_length, head_size)
    cos_heads = cosine_table[:, None, :]
    sin_heads = sine_table[:, None, :]
    query_heads = query_proj.astype(jnp.float32).reshape(seq_length, heads_here, head_size)
    q_rot = rotate(query_heads, cos_heads, sin_heads).astype(jnp.bfloat16)
    k_rot = rotate(key_block.astype(jnp.float32), cosine_table, sine_table).astype(jnp.bfloat16)
    scores = (
        jnp.einsum("shd,td->hst", q_rot, k_rot, preferred_element_type=jnp.float32) * score_scale
    )
    causal = lax.broadcasted_iota(jnp.int32, (seq_length, seq_length), 0) >= lax.broadcasted_iota(
        jnp.int32, (seq_length, seq_length), 1
    )
    exponent = jnp.where(causal[None, :, :], jnp.exp(scores), 0.0)
    softmax_probs = exponent / jnp.sum(exponent, axis=2, keepdims=True)
    prob_weights = softmax_probs.astype(jnp.bfloat16)
    context = jnp.einsum(
        "hst,td->shd", prob_weights, value_block, preferred_element_type=jnp.float32
    ).astype(jnp.bfloat16)
    grad_ctx = grad_context.reshape(seq_length, heads_here, head_size)
    grad_probs = jnp.einsum(
        "shd,td->hst", grad_ctx, value_block, preferred_element_type=jnp.float32
    )
    row_delta = jnp.sum(grad_ctx.astype(jnp.float32) * context.astype(jnp.float32), axis=2).T[
        :, :, None
    ]
    grad_scores = (softmax_probs * (grad_probs - row_delta) * score_scale).astype(jnp.bfloat16)
    grad_qrot = jnp.einsum("hst,td->shd", grad_scores, k_rot, preferred_element_type=jnp.float32)
    grad_krot = jnp.einsum("hst,shd->td", grad_scores, q_rot, preferred_element_type=jnp.float32)
    grad_value = jnp.einsum(
        "hst,shd->td", prob_weights, grad_ctx, preferred_element_type=jnp.float32
    )
    grad_query = (
        unrotate(grad_qrot, cos_heads, sin_heads)
        .astype(jnp.bfloat16)
        .reshape(seq_length, heads_here * head_size)
    )
    grad_key = unrotate(grad_krot, cosine_table, sine_table)
    term_blocks = jnp.stack(
        [grad_key[:, :group_cols], grad_key[:, group_cols:], grad_value[:, :group_cols], grad_value[:, group_cols:]]
    )
    keyval_terms = group_exchange(term_routes, term_blocks, 4, 2)
    grad_keyval = jnp.sum(keyval_terms, axis=0).astype(jnp.bfloat16)
    engine_blocks = engine_full.reshape(tensor_count, local_cols, split_cols + group_cols)
    ring_blocks = ring_full.reshape(tensor_count, local_cols, query_cols - split_cols)
    engine_grads = jnp.concatenate([grad_query[:, :split_cols], grad_keyval], axis=1)
    normed_terms = (
        jnp.einsum("rc,pkc->prk", engine_grads, engine_blocks, preferred_element_type=jnp.float32)
        + jnp.einsum(
            "rc,pkc->prk",
            grad_query[:, split_cols:],
            ring_blocks,
            preferred_element_type=jnp.float32,
        )
    ).astype(jnp.bfloat16)
    product_part = jnp.sum(
        normed_terms.astype(jnp.float32) * gain_blocks * unit_blocks, axis=(0, 2)
    ).reshape(1, seq_length)
    dp_count = lax.axis_size("dp")
    pair_count = 2
    ring_count = dp_count // pair_count
    block_rows = model_width // dp_count
    normed_pairs = normed_full.reshape(
        seq_length, pair_count, ring_count, block_rows // 2, 2
    ).transpose(0, 2, 1, 3, 4)
    keyval_partials = jnp.concatenate(
        [
            jnp.einsum(
                "rbaq,rc->baqc",
                normed_pairs[..., half],
                grad_keyval,
                preferred_element_type=jnp.float32,
            )
            for half in range(2)
        ],
        axis=-1,
    ).reshape(model_width // 2, 2 * group_cols)
    ring_groups = [
        [pair * ring_count + slot for slot in range(ring_count)] for pair in range(pair_count)
    ]
    ring_sums = lax.psum_scatter(
        keyval_partials, "dp", scatter_dimension=0, tiled=True, axis_index_groups=ring_groups
    )
    normed_sums, product_parts = exchange(
        "tensor", [normed_terms, product_part], [True, False], 3
    )
    grad_normed = jnp.sum(normed_sums.astype(jnp.float32), axis=0)
    product_sum = jnp.sum(product_parts, axis=0).reshape(seq_length, 1)
    scaled_grad = grad_normed * gain_local
    grad_input = (inv_rms * (scaled_grad - unit_rows * (product_sum / model_width))).astype(
        jnp.bfloat16
    )
    gain_part = jnp.sum(grad_normed * unit_rows, axis=0).reshape(1, local_cols)
    (gain_parts,) = exchange("dp", [gain_part], [False], 4)
    grad_gain = jnp.sum(gain_parts, axis=(0, 1))
    lane_rows = ring_sums.size // (pair_count * 128)
    keyval_sums = pair_sum(ring_sums.reshape(pair_count, lane_rows, 128), ring_count, 7)
    keyval_weight_grad = keyval_sums.reshape(-1, group_cols)
    return (grad_input, grad_gain, keyval_weight_grad.astype(jnp.bfloat16))


def solution(mesh):
    in_specs = (P("dp", "tensor"), P("dp", "tensor"), P(), P("dp", "tensor"), P("dp", "tensor"))
    out_specs = (P("dp", "tensor"), P("tensor"), P("dp", "tensor"))
    return jax.shard_map(
        on_device, mesh=mesh, in_specs=in_specs, out_specs=out_specs, check_vma=False
    )
```

```python
import functools
import math

import jax
import jax.numpy as jnp
from jax import lax
from jax.experimental import pallas as pl
from jax.experimental.pallas import tpu as pltpu
from jax.sharding import PartitionSpec as P

MESH = pl.DeviceIdType.MESH


def exchange_kernel(axes, sizes, per_peer, *refs):
    count = len(per_peer)
    src_refs = refs[:count]
    out_refs = refs[count : 2 * count]
    send_sems, recv_sems = refs[2 * count :]
    barrier = pltpu.get_barrier_semaphore()
    waits = 0
    for axis in dict.fromkeys(axes):
        n = sizes[axes.index(axis)]
        me = lax.axis_index(axis)
        for step in range(1, n):
            peer = lax.rem(me + step, n)
            pl.semaphore_signal(barrier, inc=1, device_id={axis: peer}, device_id_type=MESH)
        waits += n - 1
    pl.semaphore_wait(barrier, waits)
    copies = []
    for index in range(count):
        axis, n = axes[index], sizes[index]
        me = lax.axis_index(axis)
        for step in range(1, n):
            peer = lax.rem(me + step, n)
            source = src_refs[index].at[peer] if per_peer[index] else src_refs[index]
            copy = pltpu.make_async_remote_copy(
                src_ref=source,
                dst_ref=out_refs[index].at[me],
                send_sem=send_sems.at[index, step],
                recv_sem=recv_sems.at[index, step],
                device_id={axis: peer},
                device_id_type=MESH,
            )
            copy.start()
            copies.append(copy)
    for index in range(count):
        me = lax.axis_index(axes[index])
        own = src_refs[index][me] if per_peer[index] else src_refs[index][...]
        out_refs[index][me] = own
    for copy in copies:
        copy.wait_send()
    for copy in copies:
        copy.wait_recv()


def exchange_multi(items, collective_id):
    axes = tuple(axis for axis, _, _ in items)
    sizes = tuple(lax.axis_size(axis) for axis in axes)
    blocks = [block for _, block, _ in items]
    per_peer = tuple(spread for _, _, spread in items)
    out_shapes = []
    sent = 0
    for n, block, spread in zip(sizes, blocks, per_peer):
        shape = block.shape[1:] if spread else block.shape
        out_shapes.append(jax.ShapeDtypeStruct((n,) + tuple(shape), block.dtype))
        sent += block.size * block.dtype.itemsize * (1 if spread else n)
    count = len(blocks)
    return pl.pallas_call(
        functools.partial(exchange_kernel, axes, sizes, per_peer),
        out_shape=tuple(out_shapes),
        in_specs=[pl.BlockSpec(memory_space=pltpu.VMEM)] * count,
        out_specs=tuple(pl.BlockSpec(memory_space=pltpu.VMEM) for _ in range(count)),
        scratch_shapes=[
            pltpu.SemaphoreType.DMA((count, max(sizes))),
            pltpu.SemaphoreType.DMA((count, max(sizes))),
        ],
        compiler_params=pltpu.CompilerParams(collective_id=collective_id, has_side_effects=True),
        cost_estimate=pl.CostEstimate(flops=0, bytes_accessed=2 * sent, transcendentals=0),
    )(*blocks)


def exchange(axis, blocks, per_peer, collective_id):
    return exchange_multi([(axis, b, s) for b, s in zip(blocks, per_peer)], collective_id)


def ring_gather_kernel(
    pair_count, ring_count, side_count, block_ref, side_ref, out_ref, side_out, send_sems, recv_sems, side_send, side_recv
):
    pair_slot = lax.axis_index("dp") // ring_count
    ring_slot = lax.axis_index("dp") % ring_count
    partner = (1 - pair_slot) * ring_count + ring_slot
    right = pair_slot * ring_count + lax.rem(ring_slot + 1, ring_count)
    left = pair_slot * ring_count + lax.rem(ring_slot + ring_count - 1, ring_count)
    me = pair_slot * ring_count + ring_slot
    side_me = lax.axis_index("tensor")
    barrier = pltpu.get_barrier_semaphore()
    for peer in (partner, right, left):
        pl.semaphore_signal(barrier, inc=1, device_id={"dp": peer}, device_id_type=MESH)
    for step in range(1, side_count):
        peer = lax.rem(side_me + step, side_count)
        pl.semaphore_signal(barrier, inc=1, device_id={"tensor": peer}, device_id_type=MESH)
    pl.semaphore_wait(barrier, 3 + side_count - 1)
    swap = pltpu.make_async_remote_copy(
        src_ref=block_ref,
        dst_ref=out_ref.at[me],
        send_sem=send_sems.at[2, 0, 0],
        recv_sem=recv_sems.at[2, 0, 0],
        device_id={"dp": partner},
        device_id_type=MESH,
    )
    swap.start()
    own = pltpu.make_async_copy(block_ref, out_ref.at[me], send_sems.at[2, 1, 0])
    own.start()
    side_out[side_me] = side_ref[...]
    own.wait()
    swap.wait_send()
    swap.wait_recv()
    right_steps = ring_count // 2
    left_steps = ring_count - 1 - right_steps
    sent = []

    def send(direction, step, target, origin):
        copies = []
        for member in range(pair_count):
            slot = member * ring_count + origin
            copy = pltpu.make_async_remote_copy(
                src_ref=out_ref.at[slot],
                dst_ref=out_ref.at[slot],
                send_sem=send_sems.at[direction, step, member],
                recv_sem=recv_sems.at[direction, step, member],
                device_id={"dp": target},
                device_id_type=MESH,
            )
            copy.start()
            copies.append(copy)
        sent.extend(copies)
        return copies

    right_copies = send(0, 0, right, ring_slot)
    left_copies = send(1, 0, left, ring_slot) if left_steps > 0 else []
    side_copies = []
    for step in range(1, side_count):
        peer = lax.rem(side_me + step, side_count)
        copy = pltpu.make_async_remote_copy(
            src_ref=side_ref,
            dst_ref=side_out.at[side_me],
            send_sem=side_send.at[step],
            recv_sem=side_recv.at[step],
            device_id={"tensor": peer},
            device_id_type=MESH,
        )
        copy.start()
        side_copies.append(copy)
    for step in range(1, right_steps):
        for copy in right_copies:
            copy.wait_recv()
        origin = lax.rem(ring_slot + ring_count - step, ring_count)
        right_copies = send(0, step, right, origin)
        if step < left_steps:
            for copy in left_copies:
                copy.wait_recv()
            origin = lax.rem(ring_slot + step, ring_count)
            left_copies = send(1, step, left, origin)
    for copy in right_copies + left_copies:
        copy.wait_recv()
    for copy in sent + side_copies:
        copy.wait_send()
    for copy in side_copies:
        copy.wait_recv()


def ring_gather(block, side, collective_id):
    count = lax.axis_size("dp")
    side_count = lax.axis_size("tensor")
    pair_count = 2
    ring_count = count // pair_count
    sent = count * block.size * block.dtype.itemsize + side_count * side.size * side.dtype.itemsize
    return pl.pallas_call(
        functools.partial(ring_gather_kernel, pair_count, ring_count, side_count),
        out_shape=(
            jax.ShapeDtypeStruct((count,) + block.shape, block.dtype),
            jax.ShapeDtypeStruct((side_count,) + side.shape, side.dtype),
        ),
        in_specs=[pl.BlockSpec(memory_space=pltpu.VMEM)] * 2,
        out_specs=(pl.BlockSpec(memory_space=pltpu.VMEM), pl.BlockSpec(memory_space=pltpu.VMEM)),
        scratch_shapes=[
            pltpu.SemaphoreType.DMA((3, ring_count, pair_count)),
            pltpu.SemaphoreType.DMA((3, ring_count, pair_count)),
            pltpu.SemaphoreType.DMA((side_count,)),
            pltpu.SemaphoreType.DMA((side_count,)),
        ],
        compiler_params=pltpu.CompilerParams(
            collective_id=collective_id, has_side_effects=True, vmem_limit_bytes=48 * 1024 * 1024
        ),
        cost_estimate=pl.CostEstimate(flops=0, bytes_accessed=2 * sent, transcendentals=0),
    )(block, side)

def pair_sum_kernel(ring_count, block_ref, out_ref, landing, sems):
    pair_slot = lax.axis_index("dp") // ring_count
    ring_slot = lax.axis_index("dp") % ring_count
    partner = (1 - pair_slot) * ring_count + ring_slot
    barrier = pltpu.get_barrier_semaphore()
    pl.semaphore_signal(barrier, inc=1, device_id={"dp": partner}, device_id_type=MESH)
    pl.semaphore_wait(barrier, 1)
    copy = pltpu.make_async_remote_copy(
        src_ref=block_ref.at[1 - pair_slot],
        dst_ref=landing,
        send_sem=sems.at[0],
        recv_sem=sems.at[1],
        device_id={"dp": partner},
        device_id_type=MESH,
    )
    copy.start()
    copy.wait_send()
    copy.wait_recv()
    out_ref[...] = block_ref[pair_slot] + landing[...]


def pair_sum(blocks, ring_count, collective_id):
    return pl.pallas_call(
        functools.partial(pair_sum_kernel, ring_count),
        out_shape=jax.ShapeDtypeStruct(blocks.shape[1:], blocks.dtype),
        in_specs=[pl.BlockSpec(memory_space=pltpu.VMEM)],
        out_specs=pl.BlockSpec(memory_space=pltpu.VMEM),
        scratch_shapes=[pltpu.VMEM(blocks.shape[1:], blocks.dtype), pltpu.SemaphoreType.DMA((2,))],
        compiler_params=pltpu.CompilerParams(collective_id=collective_id, has_side_effects=True),
        cost_estimate=pl.CostEstimate(
            flops=0, bytes_accessed=3 * blocks.size * blocks.dtype.itemsize, transcendentals=0
        ),
    )(blocks)


def group_kernel(routes, src_ref, out_ref, send_sems, recv_sems):
    me = lax.axis_index("tensor")
    dests, sources = routes(me)
    barrier = pltpu.get_barrier_semaphore()
    count = jnp.int32(0)
    for peer in [d for d, _, _ in dests] + sources:

        @pl.when(peer != me)
        def _():
            pl.semaphore_signal(barrier, inc=1, device_id={"tensor": peer}, device_id_type=MESH)

        count = count + (peer != me).astype(jnp.int32)
    pl.semaphore_wait(barrier, count)
    copies = []
    for index, (peer, slot, block) in enumerate(dests):
        copy = pltpu.make_async_remote_copy(
            src_ref=src_ref.at[block],
            dst_ref=out_ref.at[slot],
            send_sem=send_sems.at[index],
            recv_sem=recv_sems.at[slot],
            device_id={"tensor": peer},
            device_id_type=MESH,
        )
        copies.append(copy)

        @pl.when(peer != me)
        def _():
            copy.start()

        @pl.when(peer == me)
        def _():
            out_ref[slot] = src_ref[block]

    for (peer, _, _), copy in zip(dests, copies):

        @pl.when(peer != me)
        def _():
            copy.wait_send()

    for slot, peer in enumerate(sources):
        arrival = pltpu.make_async_remote_copy(
            src_ref=src_ref.at[0],
            dst_ref=out_ref.at[slot],
            send_sem=send_sems.at[0],
            recv_sem=recv_sems.at[slot],
            device_id={"tensor": peer},
            device_id_type=MESH,
        )

        @pl.when(peer != me)
        def _():
            arrival.wait_recv()


def group_exchange(routes, blocks, slots, collective_id):
    return pl.pallas_call(
        functools.partial(group_kernel, routes),
        out_shape=jax.ShapeDtypeStruct((slots,) + blocks.shape[1:], blocks.dtype),
        in_specs=[pl.BlockSpec(memory_space=pltpu.VMEM)],
        out_specs=pl.BlockSpec(memory_space=pltpu.VMEM),
        scratch_shapes=[pltpu.SemaphoreType.DMA((slots,)), pltpu.SemaphoreType.DMA((slots,))],
        compiler_params=pltpu.CompilerParams(collective_id=collective_id, has_side_effects=True),
        cost_estimate=pl.CostEstimate(
            flops=0, bytes_accessed=2 * slots * blocks[0].size * blocks.dtype.itemsize, transcendentals=0
        ),
    )(blocks)


def keyval_routes(me):
    head_group = lax.rem(me // 2, KV_HEADS)
    slot = 2 * (me // (2 * KV_HEADS)) + lax.rem(me, 2)
    dests = [(KV_HEADS * head_group + m, slot, 0) for m in range(KV_HEADS)]
    group = me // KV_HEADS
    sources = [2 * group, 2 * group + 1, 2 * KV_HEADS + 2 * group, 2 * KV_HEADS + 2 * group + 1]
    return dests, sources


def term_routes(me):
    group = me // KV_HEADS
    slot = lax.rem(me, KV_HEADS)
    targets = [2 * group, 2 * group + 1, 2 * KV_HEADS + 2 * group, 2 * KV_HEADS + 2 * group + 1]
    dests = [(target, slot, m) for m, target in enumerate(targets)]
    head_group = lax.rem(me // 2, KV_HEADS)
    sources = [KV_HEADS * head_group + m for m in range(KV_HEADS)]
    return dests, sources


HD = 128
KV_HEADS = 4
HEADS_DEV = 4


def rope_tables(length, head_size):
    positions = lax.broadcasted_iota(jnp.int32, (length, head_size // 2), 0).astype(jnp.float32)
    index_half = lax.broadcasted_iota(jnp.int32, (length, head_size // 2), 1).astype(jnp.float32)
    frequency = jnp.exp(-(2.0 * index_half / head_size) * math.log(500000.0))
    angles = positions * frequency
    return (jnp.cos(angles), jnp.sin(angles))


def rotate(vectors, cosine_table, sine_table):
    half_size = vectors.shape[-1] // 2
    first_half = vectors[..., :half_size]
    second_half = vectors[..., half_size:]
    return jnp.concatenate(
        [
            first_half * cosine_table - second_half * sine_table,
            first_half * sine_table + second_half * cosine_table,
        ],
        axis=-1,
    )


def unrotate(vectors, cosine_table, sine_table):
    half_size = vectors.shape[-1] // 2
    first_half = vectors[..., :half_size]
    second_half = vectors[..., half_size:]
    return jnp.concatenate(
        [
            first_half * cosine_table + second_half * sine_table,
            second_half * cosine_table - first_half * sine_table,
        ],
        axis=-1,
    )


def on_device(inputs, grad_context, gain, w_query, w_keyval):
    seq_length = inputs.shape[0]
    local_cols = inputs.shape[1]
    model_width = gain.shape[0]
    head_size = HD
    heads_here = HEADS_DEV
    group_cols = w_keyval.shape[1]
    query_cols = w_query.shape[1]
    tensor_count = lax.axis_size("tensor")
    keyval_total = group_cols * tensor_count
    kv_heads = KV_HEADS
    devices_per_group = tensor_count // kv_heads
    score_scale = head_size ** (-0.5)
    tensor_slot = lax.axis_index("tensor")
    gain_local = lax.dynamic_slice_in_dim(gain, tensor_slot * local_cols, local_cols, 0)
    split_cols = query_cols * 3 // 8
    engine_block = jnp.concatenate([w_query[:, :split_cols], w_keyval], axis=1)
    engine_full = lax.all_gather(engine_block, "dp", axis=0, tiled=True)
    ring_blocks_out, input_blocks = ring_gather(w_query[:, split_cols:], inputs, 6)
    ring_full = ring_blocks_out.reshape(-1, query_cols - split_cols)
    input_values = input_blocks.astype(jnp.float32)
    row_sum = jnp.sum(input_values * input_values, axis=(0, 2)).reshape(seq_length, 1)
    inv_rms = lax.rsqrt(row_sum / model_width + 1e-05)
    gain_blocks = gain.reshape(tensor_count, 1, local_cols)
    unit_blocks = input_values * inv_rms[None, :, :]
    normed_blocks = (unit_blocks * gain_blocks).astype(jnp.bfloat16)
    normed_full = normed_blocks.transpose(1, 0, 2).reshape(seq_length, model_width)
    unit_rows = inputs.astype(jnp.float32) * inv_rms
    engine_proj = jnp.dot(normed_full, engine_full, preferred_element_type=jnp.float32).astype(
        jnp.bfloat16
    )
    ring_proj = jnp.dot(normed_full, ring_full, preferred_element_type=jnp.float32).astype(
        jnp.bfloat16
    )
    query_proj = jnp.concatenate([engine_proj[:, :split_cols], ring_proj], axis=1)
    keyval_part = engine_proj[:, split_cols:]
    keyval_pieces = group_exchange(keyval_routes, keyval_part[None], 4, 1)
    key_block = jnp.concatenate([keyval_pieces[0], keyval_pieces[1]], axis=1)
    value_block = jnp.concatenate([keyval_pieces[2], keyval_pieces[3]], axis=1)
    cosine_table, sine_table = rope_tables(seq_length, head_size)
    cos_heads = cosine_table[:, None, :]
    sin_heads = sine_table[:, None, :]
    query_heads = query_proj.astype(jnp.float32).reshape(seq_length, heads_here, head_size)
    q_rot = rotate(query_heads, cos_heads, sin_heads).astype(jnp.bfloat16)
    k_rot = rotate(key_block.astype(jnp.float32), cosine_table, sine_table).astype(jnp.bfloat16)
    scores = (
        jnp.einsum("shd,td->hst", q_rot, k_rot, preferred_element_type=jnp.float32) * score_scale
    )
    causal = lax.broadcasted_iota(jnp.int32, (seq_length, seq_length), 0) >= lax.broadcasted_iota(
        jnp.int32, (seq_length, seq_length), 1
    )
    exponent = jnp.where(causal[None, :, :], jnp.exp(scores), 0.0)
    softmax_probs = exponent / jnp.sum(exponent, axis=2, keepdims=True)
    prob_weights = softmax_probs.astype(jnp.bfloat16)
    context = jnp.einsum(
        "hst,td->shd", prob_weights, value_block, preferred_element_type=jnp.float32
    ).astype(jnp.bfloat16)
    grad_ctx = grad_context.reshape(seq_length, heads_here, head_size)
    grad_probs = jnp.einsum(
        "shd,td->hst", grad_ctx, value_block, preferred_element_type=jnp.float32
    )
    row_delta = jnp.sum(grad_ctx.astype(jnp.float32) * context.astype(jnp.float32), axis=2).T[
        :, :, None
    ]
    grad_scores = (softmax_probs * (grad_probs - row_delta) * score_scale).astype(jnp.bfloat16)
    grad_qrot = jnp.einsum("hst,td->shd", grad_scores, k_rot, preferred_element_type=jnp.float32)
    grad_krot = jnp.einsum("hst,shd->td", grad_scores, q_rot, preferred_element_type=jnp.float32)
    grad_value = jnp.einsum(
        "hst,shd->td", prob_weights, grad_ctx, preferred_element_type=jnp.float32
    )
    grad_query = (
        unrotate(grad_qrot, cos_heads, sin_heads)
        .astype(jnp.bfloat16)
        .reshape(seq_length, heads_here * head_size)
    )
    grad_key = unrotate(grad_krot, cosine_table, sine_table)
    term_blocks = jnp.stack(
        [grad_key[:, :group_cols], grad_key[:, group_cols:], grad_value[:, :group_cols], grad_value[:, group_cols:]]
    )
    keyval_terms = group_exchange(term_routes, term_blocks, 4, 2)
    grad_keyval = jnp.sum(keyval_terms, axis=0).astype(jnp.bfloat16)
    engine_blocks = engine_full.reshape(tensor_count, local_cols, split_cols + group_cols)
    ring_blocks = ring_full.reshape(tensor_count, local_cols, query_cols - split_cols)
    engine_grads = jnp.concatenate([grad_query[:, :split_cols], grad_keyval], axis=1)
    normed_terms = (
        jnp.einsum("rc,pkc->prk", engine_grads, engine_blocks, preferred_element_type=jnp.float32)
        + jnp.einsum(
            "rc,pkc->prk",
            grad_query[:, split_cols:],
            ring_blocks,
            preferred_element_type=jnp.float32,
        )
    ).astype(jnp.bfloat16)
    product_part = jnp.sum(
        normed_terms.astype(jnp.float32) * gain_blocks * unit_blocks, axis=(0, 2)
    ).reshape(1, seq_length)
    dp_count = lax.axis_size("dp")
    pair_count = 2
    ring_count = dp_count // pair_count
    block_rows = model_width // dp_count
    normed_pairs = normed_full.reshape(
        seq_length, pair_count, ring_count, block_rows // 2, 2
    ).transpose(0, 2, 1, 3, 4)
    keyval_partials = jnp.concatenate(
        [
            jnp.einsum(
                "rbaq,rc->baqc",
                normed_pairs[..., half],
                grad_keyval,
                preferred_element_type=jnp.float32,
            )
            for half in range(2)
        ],
        axis=-1,
    ).reshape(model_width // 2, 2 * group_cols)
    ring_groups = [
        [pair * ring_count + slot for slot in range(ring_count)] for pair in range(pair_count)
    ]
    ring_sums = lax.psum_scatter(
        keyval_partials, "dp", scatter_dimension=0, tiled=True, axis_index_groups=ring_groups
    )
    normed_sums, product_parts = exchange(
        "tensor", [normed_terms, product_part], [True, False], 3
    )
    grad_normed = jnp.sum(normed_sums.astype(jnp.float32), axis=0)
    product_sum = jnp.sum(product_parts, axis=0).reshape(seq_length, 1)
    scaled_grad = grad_normed * gain_local
    grad_input = (inv_rms * (scaled_grad - unit_rows * (product_sum / model_width))).astype(
        jnp.bfloat16
    )
    gain_part = jnp.sum(grad_normed * unit_rows, axis=0).reshape(1, local_cols)
    (gain_parts,) = exchange("dp", [gain_part], [False], 4)
    grad_gain = jnp.sum(gain_parts, axis=(0, 1))
    lane_rows = ring_sums.size // (pair_count * 128)
    keyval_sums = pair_sum(ring_sums.reshape(pair_count, lane_rows, 128), ring_count, 7)
    keyval_weight_grad = keyval_sums.reshape(-1, group_cols)
    return (grad_input, grad_gain, keyval_weight_grad.astype(jnp.bfloat16))


def solution(mesh):
    in_specs = (P("dp", "tensor"), P("dp", "tensor"), P(), P("dp", "tensor"), P("dp", "tensor"))
    out_specs = (P("dp", "tensor"), P("tensor"), P("dp", "tensor"))
    return jax.shard_map(
        on_device, mesh=mesh, in_specs=in_specs, out_specs=out_specs, check_vma=False
    )
```
